128 devices in a mesh: member: 32 (over x, z, core), mp: 4 (over y).
Axes of the slice: x: 4, y: 4, z: 4, core: 2. Of those that a mesh axis runs over, the one named last changes fastest.
Arguments:
- latents: bfloat16 [128, 1024, 1024], P('member', 'mp'), may hold values from -6 to 6
- w_first: bfloat16 [1024, 2048], P(None, 'mp'), may hold values from -0.1875 to 0.1875
- w_second: bfloat16 [2048, 1024], P('mp'), may hold values from -0.125 to 0.125
- readout_matrix: bfloat16 [1024, 768], P(None, 'mp'), may hold values from -0.1875 to 0.1875
- observed: float32 [1024, 768], P(('mp', 'member')), may hold values from -9 to 9
- obs_index: int32 [1024], P(('mp', 'member')), may hold values from 0 to 1023, as said below
- valid_mask: int32 [1024], P(('mp', 'member')), may hold values from 0 to 1
Outputs:
- grad_first: float32 [1024, 2048], P(('member', 'mp'))
- grad_second: float32 [2048, 1024], P(('member', 'mp'))
- grad_head: float32 [1024, 768], P(('member', 'mp'))
- loss: float32 [], replicated
The draws below stay inside these ranges and needn't reach their ends.
Inputs may be any that keep to these rules, and one draw needn't show every extreme that they name: obs_index[p] names a record of the same aligned block of 8 patches as p.
All inputs are finite; a program needn't handle non-finite values.
Results may differ from the reference program's by a relative error of at most 0.006.
Values may be sent and summed in bfloat16 or wider, within the bound.
No kernel may reach another device: no remote copies, remote signals or barrier semaphores. Data moves between devices by JAX's collectives and lax.ppermute only.
A program may use at most 128 MiB of HBM per device.

```python
import jax
import jax.numpy as jnp
from jax import lax

D = 1024
HID = 2048
OUT = 768
MEMBERS = 128
PATCHES = 1024
P_OWN = 8


def draw_obs_index(key, part):
    subkey = jax.random.fold_in(key, 11)
    base_rows = jnp.arange(PATCHES, dtype=jnp.int32) // P_OWN * P_OWN
    return base_rows + jax.random.randint(subkey, (PATCHES,), 0, P_OWN, dtype=jnp.int32)


def draw_valid_mask(key, part):
    subkey = jax.random.fold_in(key, 23)
    levels = jax.random.randint(subkey, (PATCHES,), 0, 4 * PATCHES, dtype=jnp.int32)
    bounds = PATCHES + 2 * jnp.arange(PATCHES, dtype=jnp.int32)
    return (levels < bounds).astype(jnp.int32)


def block_scale(stream_key, dims, pieces, smallest, largest):
    loudness = 1.0
    for position, parts in pieces:
        steps = jax.random.uniform(jax.random.fold_in(jax.random.fold_in(stream_key, 6), position), (parts,), jnp.float32, smallest / len(pieces), largest / len(pieces))
        loudness = loudness * jnp.repeat(jnp.exp(steps), dims[position] // parts).reshape((-1,) + (1,) * (len(dims) - 1 - position))
    return loudness


def noise(rng, dims, deviation, limit, cuts=(), kind=jnp.bfloat16):
    array = jax.random.normal(rng, dims, jnp.float32) * deviation
    if len(cuts) > 0:
        array = block_scale(rng, dims, cuts, -0.22, 0.18) * array
    return jnp.clip(array, min=-limit, max=limit).astype(kind)


def setup_inputs(seed: int = 0) -> dict:
    key_of = jax.random.split(jax.random.key(seed), 8)
    return {
        "latents": noise(key_of[0], (MEMBERS, PATCHES, D), 1.0, 6.0, ((0, 32), (1, 4))),
        "w_first": noise(key_of[1], (D, HID), D ** -0.5, 0.1875, ((1, 4),)),
        "w_second": noise(key_of[2], (HID, D), HID ** -0.5, 0.125, ((0, 4),)),
        "readout_matrix": noise(key_of[3], (D, OUT), D ** -0.5, 0.1875, ((1, 4),)),
        "observed": noise(key_of[4], (PATCHES, OUT), 1.5, 9.0, ((0, 128),), jnp.float32),
        "obs_index": draw_obs_index(jax.random.fold_in(key_of[7], 71), 0),
        "valid_mask": draw_valid_mask(jax.random.fold_in(key_of[7], 71), 0),
    }


SMOOTHING = 1.0
LOSS_SCALE = 4096.0

def gelu_fn(values):
    return jax.nn.gelu(values, approximate=True)

def gelu_back(preact, upstream):
    return jax.vjp(gelu_fn, preact)[1](upstream)[0]

def row_outer(left_rows, right_rows):
    return lax.dot_general(left_rows, right_rows, (((0,), (0,)), ((), ())), preferred_element_type=jnp.float32)

def reference(latents, w_first, w_second, readout_matrix, observed, obs_index, valid_mask):
    sample_indices = latents.shape[0]
    token_rows = latents.reshape(-1, latents.shape[2])
    preact = jnp.dot(token_rows, w_first, preferred_element_type=jnp.float32)
    hidden = gelu_fn(preact).astype(jnp.bfloat16)
    skip_activation = (token_rows.astype(jnp.float32) + jnp.dot(hidden, w_second, preferred_element_type=jnp.float32)).astype(jnp.bfloat16)
    prediction_lines = jnp.dot(skip_activation, readout_matrix, preferred_element_type=jnp.float32).astype(jnp.bfloat16)
    predicted_samples = prediction_lines.reshape(sample_indices, -1, readout_matrix.shape[1]).astype(jnp.float32)
    target = observed[obs_index.astype(jnp.int32)]
    gram_matrix = jnp.einsum('mpo,npo->pmn', predicted_samples, predicted_samples, precision=lax.Precision.HIGHEST)
    squares = lax.optimization_barrier(jnp.sum(predicted_samples * predicted_samples, axis=2)).T
    dist_sq = squares[:, :, None] + squares[:, None, :] - 2.0 * gram_matrix
    spread = jnp.sqrt(dist_sq + SMOOTHING)
    kernel = 1.0 / spread
    kernel_sum = lax.optimization_barrier(jnp.sum(kernel, axis=2))
    pulled = jnp.einsum('pmn,npo->mpo', kernel, predicted_samples, precision=lax.Precision.HIGHEST)
    offset = predicted_samples - target[None]
    error_norm = jnp.sqrt(lax.optimization_barrier(jnp.sum(offset * offset, axis=2)) + SMOOTHING)
    repulse = predicted_samples * kernel_sum.T[:, :, None] - pulled
    validity = valid_mask.astype(jnp.float32)
    grad_raw = (LOSS_SCALE * validity[None, :, None] * (offset / (sample_indices * error_norm[:, :, None]) - repulse / (sample_indices * sample_indices))).astype(jnp.bfloat16)
    scores = validity * (lax.optimization_barrier(jnp.mean(error_norm, axis=0)) - lax.optimization_barrier(jnp.sum(spread, axis=(1, 2))) / (2.0 * sample_indices * sample_indices))
    valid_total = jnp.maximum(jnp.sum(validity), 1.0)
    loss = jnp.sum(scores) / valid_total
    grad_rows = grad_raw.reshape(-1, readout_matrix.shape[1])
    resid_grad = jnp.dot(grad_rows, readout_matrix.T, preferred_element_type=jnp.float32).astype(jnp.bfloat16)
    hidden_grad = jnp.dot(resid_grad, w_second.T, preferred_element_type=jnp.float32)
    preact_grad = gelu_back(preact, hidden_grad).astype(jnp.bfloat16)
    grad_scale = 1.0 / valid_total
    return (row_outer(token_rows, preact_grad) * grad_scale, row_outer(hidden, resid_grad) * grad_scale, row_outer(skip_activation, grad_rows) * grad_scale, loss)
```

```python
import jax
import jax.numpy as jnp
from jax import lax
from jax.sharding import Mesh
from jax.sharding import PartitionSpec as P

SMOOTHING = 1.0
LOSS_SCALE = 4096.0
RING = 4
PAIR_LOW = ((0, 1), (1, 0), (2, 3), (3, 2))
PAIR_HIGH = ((0, 3), (3, 0), (1, 2), (2, 1))


def shift(x, axis, by):
    size = lax.axis_size(axis)
    return lax.ppermute(x, axis, [(i, (i + by) % size) for i in range(size)])


def from_ring(x):
    right = shift(x, "y", 1)
    left = shift(x, "y", -1)
    half = x.shape[0] // 2
    far = jnp.concatenate([shift(right[:half], "y", 1), shift(left[half:], "y", -1)])
    return {1: left, 3: right, 2: far}


def core_halves(x, core, dim):
    other = shift(x, "c", 1)
    return jnp.where(
        core == 0, jnp.concatenate([x, other], dim), jnp.concatenate([other, x], dim)
    )


def gelu_fn(values):
    return jax.nn.gelu(values, approximate=True)


def gelu_back(preact, upstream):
    return jax.vjp(gelu_fn, preact)[1](upstream)[0]


def row_outer(left_rows, right_rows):
    return lax.dot_general(
        left_rows, right_rows, (((0,), (0,)), ((), ())), preferred_element_type=jnp.float32
    )


def pick(flag, one, zero):
    return jnp.where(flag == 1, one, zero)


def add(a, b):
    return (a.astype(jnp.float32) + b.astype(jnp.float32)).astype(jnp.bfloat16)


def core_sum(parts, core):
    mine = pick(core, parts[:, 1], parts[:, 0])
    theirs = pick(core, parts[:, 0], parts[:, 1])
    return add(mine, shift(theirs, "c", 1))


def ring_sum(parts, low, high):
    half = parts.shape[0] // 2
    a, b = parts[:half], parts[half:]

    def two(v, i, j):
        return jnp.stack([v[:, i], v[:, j]], 1)

    a0, a1 = two(a, 0, 3), two(a, 1, 2)
    b0, b1 = two(b, 0, 1), two(b, 3, 2)
    a_in = lax.ppermute(pick(low, a0, a1), "y", PAIR_LOW)
    b_in = lax.ppermute(pick(high, b0, b1), "y", PAIR_HIGH)
    a = add(pick(low, a1, a0), a_in)
    b = add(pick(high, b1, b0), b_in)
    a_in = lax.ppermute(pick(high, a[:, 0], a[:, 1]), "y", PAIR_HIGH)
    b_in = lax.ppermute(pick(low, b[:, 0], b[:, 1]), "y", PAIR_LOW)
    a = add(pick(high, a[:, 1], a[:, 0]), a_in)
    b = add(pick(low, b[:, 1], b[:, 0]), b_in)
    return jnp.concatenate([a, b])


def terms(value):
    first = lax.reduce_precision(value, 8, 7)
    second = lax.reduce_precision(value - first, 8, 7)
    third = value - first - second
    return first, second, third


def per_device(latents, w_first, w_second, readout_matrix, observed, obs_index, valid_mask):
    members, patches, width = latents.shape
    out_width = observed.shape[1]
    core = lax.axis_index("c")
    here = lax.axis_index("y")
    high = here // 2
    low = (high + here) % 2
    own = obs_index.shape[0]
    rows = members * patches
    shard = w_first.shape[1]

    head_shard = readout_matrix.T
    first_half = lax.dynamic_slice_in_dim(w_first, core * (shard // 2), shard // 2, 1)
    second_half = lax.dynamic_slice_in_dim(w_second, core * (shard // 2), shard // 2, 0)
    head_half = lax.dynamic_slice_in_dim(head_shard, core * (width // 2), width // 2, 1)
    first_in = from_ring(first_half)
    second_in = from_ring(second_half)
    head_in = from_ring(head_half)

    token_rows = (
        latents.reshape(members, 16, 2, own, width).transpose(2, 1, 0, 3, 4).reshape(rows, width)
    )
    preact = jnp.zeros((rows, shard * RING), jnp.float32)
    hidden = jnp.zeros((rows, shard * RING), jnp.bfloat16)
    full_second = jnp.zeros((shard * RING, width), jnp.bfloat16)
    full_head = jnp.zeros((out_width, width), jnp.bfloat16)
    total = token_rows.astype(jnp.float32)
    for off in (0, 1, 3, 2):
        if off == 0:
            first, second, head = w_first, w_second, head_shard
        else:
            first = core_halves(first_in[off], core, 1)
            second = core_halves(second_in[off], core, 0)
            head = core_halves(head_in[off], core, 1)
        block = (here + off) % RING
        part = jnp.dot(token_rows, first, preferred_element_type=jnp.float32)
        active = gelu_fn(part).astype(jnp.bfloat16)
        total = total + jnp.dot(active, second, preferred_element_type=jnp.float32)
        preact = lax.dynamic_update_slice_in_dim(preact, part, block * shard, 1)
        hidden = lax.dynamic_update_slice_in_dim(hidden, active, block * shard, 1)
        full_second = lax.dynamic_update_slice_in_dim(full_second, second, block * shard, 0)
        full_head = lax.dynamic_update_slice_in_dim(
            full_head, head, block * (out_width // RING), 0
        )
    residual = total.astype(jnp.bfloat16)
    forecast = lax.dot_general(
        residual, full_head, (((1,), (1,)), ((), ())), preferred_element_type=jnp.float32
    ).astype(jnp.bfloat16)

    forecast = forecast.reshape(2, 16, members, own, out_width)
    mine = pick(core, forecast[1], forecast[0])
    theirs = shift(pick(core, forecast[0], forecast[1]), "c", 1)
    pair = jnp.stack([mine, theirs], 1).reshape(16, 2 * members * own, out_width)
    gathered = lax.all_to_all(pair, ("x", "z"), 0, 0, tiled=True)
    samples = gathered.reshape(16 * 2 * members, own, out_width)

    count = samples.shape[0]
    device = (
        (here * 4 + lax.axis_index("x")) * 4 + lax.axis_index("z")
    ) * 2 + core
    target = jnp.take(observed, obs_index - device * own, axis=0)
    wide = samples.astype(jnp.float32)
    gram = jnp.einsum("mpo,npo->pmn", samples, samples, preferred_element_type=jnp.float32)
    squares = jnp.sum(wide * wide, axis=2).T
    dist_sq = squares[:, :, None] + squares[:, None, :] - 2.0 * gram
    spread = jnp.sqrt(dist_sq + SMOOTHING)
    kernel = 1.0 / spread
    kernel_sum = jnp.sum(kernel, axis=2)
    pulled = jnp.einsum("pmn,npo->mpo", kernel, wide, precision=lax.Precision.HIGHEST)
    offset = wide - target[None]
    error_norm = jnp.sqrt(jnp.sum(offset * offset, axis=2) + SMOOTHING)
    repulse = wide * kernel_sum.T[:, :, None] - pulled
    validity = valid_mask.astype(jnp.float32)
    grad_raw = (
        LOSS_SCALE
        * validity[None, :, None]
        * (offset / (count * error_norm[:, :, None]) - repulse / (count * count))
    ).astype(jnp.bfloat16)
    scores = validity * (
        jnp.mean(error_norm, axis=0) - jnp.sum(spread, axis=(1, 2)) / (2.0 * count * count)
    )

    line = jnp.arange(8)[:, None]
    sums = jnp.where(line == 0, jnp.sum(scores), jnp.sum(validity)) + jnp.zeros((8, 128))
    sums = sums + shift(sums, "c", 1)
    sums = sums + shift(sums, "y", 1)
    sums = sums + shift(sums, "y", 2)
    ones = terms(sums[0, 0]) + terms(sums[1, 0])
    riders = jnp.zeros((8, 256))
    for i, value in enumerate(ones):
        riders = jnp.where(line == i, value, riders)
    riders = jnp.broadcast_to(riders.astype(jnp.bfloat16), (16, 8, 256))

    returned = lax.all_to_all(
        grad_raw.reshape(16, 2 * members * own, out_width), ("x", "z"), 0, 0, tiled=True
    ).reshape(16, 2, members * own, out_width)
    back = shift(returned[:, 1], "c", 1)
    grad_rows = jnp.where(
        core == 0,
        jnp.stack([returned[:, 0], back]),
        jnp.stack([back, returned[:, 0]]),
    ).reshape(rows, out_width)

    resid_grad = jnp.dot(grad_rows, full_head, preferred_element_type=jnp.float32).astype(
        jnp.bfloat16
    )
    grad_head = row_outer(residual, grad_rows).astype(jnp.bfloat16)
    grad_second = row_outer(hidden, resid_grad).astype(jnp.bfloat16)
    early = jnp.concatenate(
        [
            grad_second.reshape(16, 2, RING, -1, width),
            jnp.pad(
                grad_head.reshape(16, 2, RING, -1, out_width),
                ((0, 0),) * 4 + ((0, width - out_width),),
            ),
        ],
        3,
    )
    early = ring_sum(core_sum(early, core), low, high)
    hidden_grad = lax.dot_general(
        resid_grad, full_second, (((1,), (1,)), ((), ())), preferred_element_type=jnp.float32
    )
    preact_grad = gelu_back(preact, hidden_grad).astype(jnp.bfloat16)
    grad_first = row_outer(token_rows, preact_grad).astype(jnp.bfloat16)
    late = grad_first.reshape(16, 2, RING, -1, shard * RING)
    late = jnp.concatenate([late[..., :width], late[..., width:]], 3)
    late = ring_sum(core_sum(late, core), low, high)
    n_second = shard * RING // 128
    n_head = width // 128
    early = lax.dynamic_update_slice(early, riders, (0, n_second, out_width))
    arrived = lax.all_to_all(
        jnp.concatenate([early, late], 1), ("x", "z"), 0, 0, tiled=True
    )
    summed = jnp.sum(arrived.astype(jnp.float32), 0)
    ride = summed[n_second : n_second + 8, out_width]
    score_total = ride[0] + ride[1] + ride[2]
    valid_total = jnp.maximum(ride[3] + ride[4] + ride[5], 1.0)
    scaled = summed * (1.0 / valid_total)
    at = n_second + n_head
    return (
        jnp.concatenate([scaled[at : at + n_head], scaled[at + n_head :]], 1),
        scaled[:n_second],
        scaled[n_second:at, :out_width],
        score_total / valid_total,
    )


def solution(mesh):
    grid = Mesh(mesh.devices.reshape(4, 4, 2, 4), ("x", "z", "c", "y"))
    rows = P(("y", "x", "z", "c"))
    shares = P(("x", "z", "c", "y"), None)
    return jax.shard_map(
        per_device,
        mesh=grid,
        in_specs=(
            P(("x", "z", "c"), "y", None),
            P(None, "y"),
            P("y", None),
            P(None, "y"),
            rows,
            rows,
            rows,
        ),
        out_specs=(shares, shares, shares, P()),
        check_vma=False,
    )
```

```python
import functools

import jax
import jax.numpy as jnp
from jax import lax
from jax.experimental import pallas as pl
from jax.experimental.pallas import tpu as pltpu
from jax.sharding import Mesh
from jax.sharding import PartitionSpec as P

SMOOTHING = 1.0
LOSS_SCALE = 4096.0
RING = 4
PAIR_LOW = ((0, 1), (1, 0), (2, 3), (3, 2))
PAIR_HIGH = ((0, 3), (3, 0), (1, 2), (2, 1))
ROOT_2_PI = 0.7978845608028654
CUBIC = 0.044715
LANES = 256
MIB = 1 << 20
F32 = jnp.float32
BF16 = jnp.bfloat16


def shift(x, axis, by):
    size = lax.axis_size(axis)
    return lax.ppermute(x, axis, [(i, (i + by) % size) for i in range(size)])


def dot(a, b, contract=((1,), (0,))):
    return lax.dot_general(a, b, (contract, ((), ())), preferred_element_type=F32)


def params(cells):
    return pltpu.CompilerParams(
        dimension_semantics=("arbitrary",) * cells, vmem_limit_bytes=56 * MIB
    )


def forward_kernel(first_call, last_call, block_rows, sizes, *refs):
    width, half, head_rows = sizes
    place, tokens, mine, theirs = refs[:4]
    refs = refs[4:]
    if first_call:
        total_in = None
        slope, hidden, second, head, total = refs
    elif last_call:
        total_in, _, _, _, head_in, slope, hidden, second, head, residual, forecast = refs
    else:
        total_in, _, _, _, _, slope, hidden, second, head, total = refs
    block, core = place[0], place[1]
    chunks = width // LANES
    start = width
    head_start = start + chunks * half

    @pl.when(pl.program_id(0) == 0)
    def _():
        if last_call:
            head[...] = head_in[...]
        for pack, side in ((mine, core), (theirs, 1 - core)):
            second[side] = pack[start : start + chunks * half, :]
            for e in range(2):
                piece = pack[head_start + e * head_rows : head_start + (e + 1) * head_rows, :]
                lane = pl.multiple_of(side * (width // 2) + e * LANES, LANES)
                row = pl.multiple_of(block * head_rows, 64) if last_call else 0
                head[pl.ds(row, head_rows), pl.ds(lane, LANES)] = piece

    rows = tokens[...]
    base = rows.astype(F32) if first_call else total_in[...]
    sums = [base[:, q * LANES : (q + 1) * LANES] for q in range(chunks)]
    for pack, side in ((mine, core), (theirs, 1 - core)):
        x = dot(rows, pack[:width, :])
        sq = x * x
        t = jnp.tanh(ROOT_2_PI * (x + CUBIC * x * sq))
        up = 0.5 * (1.0 + t)
        active = (x * up).astype(BF16)
        lane = pl.multiple_of(side * half, half)
        slope[:, pl.ds(lane, half)] = up + (0.5 * ROOT_2_PI) * x * (1.0 - t * t) * (
            1.0 + (3.0 * CUBIC) * sq
        )
        hidden[:, pl.ds(lane, half)] = active
        for q in range(chunks):
            sums[q] = sums[q] + dot(active, pack[start + q * half : start + (q + 1) * half, :])
    full = jnp.concatenate(sums, 1)
    if last_call:
        rounded = full.astype(BF16)
        residual[...] = rounded
        forecast[...] = dot(rounded, head[...], ((1,), (1,))).astype(BF16)
    else:
        total[...] = full


def forward_part(place, tokens, mine, theirs, carried, out_width, last_call):
    rows, width = tokens.shape
    half = LANES
    hid = 2 * half * RING
    head_rows = out_width // RING
    first_call = carried is None
    block_rows = min(rows, 256)
    whole = lambda shape: pl.BlockSpec(shape, lambda i, s: (0,) * len(shape))
    by_rows = lambda cols: pl.BlockSpec((block_rows, cols), lambda i, s: (i, 0))
    in_place = pl.BlockSpec(memory_space=pl.ANY)
    in_specs = [by_rows(width), whole(mine.shape), whole(theirs.shape)]
    args = [tokens, mine, theirs]
    aliases = {}
    if not first_call:
        slope, hidden, second, head, total = carried
        args += [total, slope, hidden, second, head]
        in_specs += [by_rows(width), in_place, in_place, in_place]
        in_specs += [whole((out_width, width)) if last_call else in_place]
        aliases = {5: 0, 6: 1, 7: 2}
        if not last_call:
            aliases = {**aliases, 8: 3, 4: 4}
    column = pl.BlockSpec((block_rows, 2 * half), lambda i, s: (i, s[0]))
    out_specs = [
        column,
        column,
        pl.BlockSpec((2, width * half // LANES, LANES), lambda i, s: (s[0], 0, 0)),
        whole((out_width, width))
        if last_call
        else pl.BlockSpec((head_rows, width), lambda i, s: (s[0], 0)),
    ]
    out_shape = [
        jax.ShapeDtypeStruct((rows, hid), F32),
        jax.ShapeDtypeStruct((rows, hid), BF16),
        jax.ShapeDtypeStruct((2 * RING, width * half // LANES, LANES), BF16),
        jax.ShapeDtypeStruct((out_width, width), BF16),
    ]
    if last_call:
        out_specs += [by_rows(width), by_rows(out_width)]
        out_shape += [
            jax.ShapeDtypeStruct((rows, width), BF16),
            jax.ShapeDtypeStruct((rows, out_width), BF16),
        ]
    else:
        out_specs += [by_rows(width)]
        out_shape += [jax.ShapeDtypeStruct((rows, width), F32)]
    return pl.pallas_call(
        functools.partial(
            forward_kernel, first_call, last_call, block_rows, (width, half, head_rows)
        ),
        grid_spec=pltpu.PrefetchScalarGridSpec(
            num_scalar_prefetch=1,
            grid=(rows // block_rows,),
            in_specs=in_specs,
            out_specs=out_specs,
        ),
        out_shape=out_shape,
        input_output_aliases=aliases,
        compiler_params=params(1),
        cost_estimate=pl.CostEstimate(
            flops=8 * rows * width * half, bytes_accessed=12 * MIB, transcendentals=rows * 2 * half
        ),
        name="forward_part",
    )(place, *args)


def store_halves(core, parts, keep, send):
    n, _, rows, cols = parts.shape
    zero = parts[:, 0].reshape(n * rows, cols).astype(BF16)
    one = parts[:, 1].reshape(n * rows, cols).astype(BF16)

    @pl.when(core == 0)
    def _():
        keep[0] = zero
        send[0] = one

    @pl.when(core == 1)
    def _():
        keep[0] = one
        send[0] = zero


def early_kernel(place, hidden_t, resid_grad, residual_t, grad_rows, keep, send):
    second = dot(hidden_t[...], resid_grad[...])
    head = dot(residual_t[...], grad_rows[...])
    width, out_width = second.shape[1], head.shape[1]
    second = second.reshape(RING, 2, RING, -1, width)
    head = head.reshape(RING, 2, RING, -1, out_width)
    blank = jnp.zeros((*head.shape[:4], width - out_width), F32)
    both = jnp.concatenate([second, jnp.concatenate([head, blank], 4)], 3)
    both = both.reshape(RING, 2, -1, width)
    store_halves(place[1], both, keep, send)


def early_grads(place, hidden_t, resid_grad, residual_t, grad_rows):
    hid, rows = hidden_t.shape
    width, out_width = residual_t.shape[0], grad_rows.shape[1]
    lines = (hid + width) // RING // 2
    gray = lambda i: 2 * ((i // 2 + i) % 2) + i // 2
    out = pl.BlockSpec((1, lines, width), lambda i, s: (gray(i), 0, 0))
    return pl.pallas_call(
        early_kernel,
        grid_spec=pltpu.PrefetchScalarGridSpec(
            num_scalar_prefetch=1,
            grid=(RING,),
            in_specs=[
                pl.BlockSpec((hid // RING, rows), lambda i, s: (i, 0)),
                pl.BlockSpec((rows, width), lambda i, s: (0, 0)),
                pl.BlockSpec((width // RING, rows), lambda i, s: (i, 0)),
                pl.BlockSpec((rows, out_width), lambda i, s: (0, 0)),
            ],
            out_specs=[out, out],
        ),
        out_shape=[jax.ShapeDtypeStruct((RING, lines, width), BF16)] * 2,
        compiler_params=params(1),
        cost_estimate=pl.CostEstimate(
            flops=2 * rows * width * (hid + out_width), bytes_accessed=18 * MIB, transcendentals=0
        ),
        name="early_grads",
    )(place, hidden_t, resid_grad, residual_t, grad_rows)


def late_kernel(place, resid_grad, second, slope, tokens_t, keep, send):
    grad = resid_grad[...]
    width = grad.shape[1]
    total = None
    for q in range(width // LANES):
        term = dot(
            grad[:, q * LANES : (q + 1) * LANES],
            second[0, q * LANES : (q + 1) * LANES, :],
            ((1,), (1,)),
        )
        total = term if total is None else total + term
    preact_grad = (slope[...] * total).astype(BF16)
    first = dot(tokens_t[...], preact_grad)
    parts = first.reshape(16, 2, RING, -1, LANES)
    parts = jnp.stack([parts[:, :, i] for i in (0, 3, 1, 2)], 2)
    store_halves(place[1], parts.reshape(16, 2, -1, LANES), keep, send)


def late_grads(place, resid_grad, second, slope, tokens_t):
    rows, width = resid_grad.shape
    hid = slope.shape[1]
    per = width // LANES
    out = pl.BlockSpec((1, width // 2, LANES), lambda j, s: (j // per, 0, j % per))
    return pl.pallas_call(
        late_kernel,
        grid_spec=pltpu.PrefetchScalarGridSpec(
            num_scalar_prefetch=1,
            grid=(hid // LANES,),
            in_specs=[
                pl.BlockSpec((rows, width), lambda j, s: (0, 0)),
                pl.BlockSpec((1, *second.shape[1:]), lambda j, s: (j, 0, 0)),
                pl.BlockSpec((rows, LANES), lambda j, s: (0, j)),
                pl.BlockSpec((width, rows), lambda j, s: (0, 0)),
            ],
            out_specs=[out, out],
        ),
        out_shape=[jax.ShapeDtypeStruct((hid // width, width // 2, width), BF16)] * 2,
        compiler_params=params(1),
        cost_estimate=pl.CostEstimate(
            flops=4 * rows * width * hid, bytes_accessed=20 * MIB, transcendentals=0
        ),
        name="late_grads",
    )(place, resid_grad, second, slope, tokens_t)


def add(a, b):
    return (a.astype(F32) + b.astype(F32)).astype(BF16)


def take(x, index, axis):
    return lax.dynamic_index_in_dim(x, index, axis, keepdims=False)


def ring_bits(axis):
    here = lax.axis_index(axis)
    high = here // 2
    return (high + here) % 2, high


def ring_sum(a, b, axis):
    low, high = ring_bits(axis)
    a_in = lax.ppermute(take(a, 1 - low, 0), axis, PAIR_LOW)
    b_in = lax.ppermute(take(b, 1 - high, 1), axis, PAIR_HIGH)
    a = add(take(a, low, 0), a_in)
    b = add(take(b, high, 1), b_in)
    a_in = lax.ppermute(take(a, 1 - high, 0), axis, PAIR_HIGH)
    b_in = lax.ppermute(take(b, 1 - low, 0), axis, PAIR_LOW)
    return add(take(a, high, 0), a_in), add(take(b, low, 0), b_in)


def terms(value):
    first = lax.reduce_precision(value, 8, 7)
    second = lax.reduce_precision(value - first, 8, 7)
    third = value - first - second
    return first, second, third


def pick(flag, one, zero):
    return jnp.where(flag == 1, one, zero)


def packed(first, second, head):
    columns = lambda v: [v[:, i : i + LANES] for i in range(0, v.shape[1], LANES)]
    return jnp.concatenate([first, *columns(second), *columns(head)], 0)


def score(samples, target, valid_mask):
    count = samples.shape[0]
    wide = samples.astype(F32)
    gram = jnp.einsum("mpo,npo->pmn", samples, samples, preferred_element_type=F32)
    squares = jnp.sum(wide * wide, axis=2).T
    dist_sq = squares[:, :, None] + squares[:, None, :] - 2.0 * gram
    spread = jnp.sqrt(dist_sq + SMOOTHING)
    kernel = 1.0 / spread
    kernel_sum = jnp.sum(kernel, axis=2)
    pulled = jnp.einsum("pmn,npo->mpo", kernel, wide, precision=lax.Precision.HIGHEST)
    offset = wide - target[None]
    error_norm = jnp.sqrt(jnp.sum(offset * offset, axis=2) + SMOOTHING)
    repulse = wide * kernel_sum.T[:, :, None] - pulled
    validity = valid_mask.astype(F32)
    grad_raw = (
        LOSS_SCALE
        * validity[None, :, None]
        * (offset / (count * error_norm[:, :, None]) - repulse / (count * count))
    ).astype(BF16)
    scores = validity * (
        jnp.mean(error_norm, axis=0) - jnp.sum(spread, axis=(1, 2)) / (2.0 * count * count)
    )
    return grad_raw, jnp.sum(scores), jnp.sum(validity)


def per_device(latents, w_first, w_second, readout_matrix, observed, obs_index, valid_mask):
    members, patches, width = latents.shape
    out_width = observed.shape[1]
    core = lax.axis_index("c")
    here = lax.axis_index("y")
    own = obs_index.shape[0]
    rows = members * patches
    shard = w_first.shape[1]
    half = shard // 2

    head_shard = readout_matrix.T

    def half_of(side):
        return packed(
            lax.dynamic_slice_in_dim(w_first, side * half, half, 1),
            lax.dynamic_slice_in_dim(w_second, side * half, half, 0),
            lax.dynamic_slice_in_dim(head_shard, side * (width // 2), width // 2, 1),
        )

    mine = half_of(core)
    right = shift(mine, "y", 1)
    left = shift(mine, "y", -1)
    lines = mine.shape[0] // 2
    far = [shift(right[:lines], "y", 1), shift(left[lines:], "y", -1)]
    right_other = shift(right, "c", 1)
    left_other = shift(left, "c", 1)
    far = jnp.concatenate(far, 0)
    far_other = shift(far, "c", 1)

    tokens = (
        latents.reshape(members, 16, 2, own, width).transpose(2, 1, 0, 3, 4).reshape(rows, width)
    )
    place = lambda off: jnp.stack([(here + off) % RING, core]).astype(jnp.int32)
    run = functools.partial(forward_part, out_width=out_width)
    carried = run(place(0), tokens, mine, half_of(1 - core), carried=None, last_call=False)
    carried = run(place(3), tokens, right, right_other, carried=carried, last_call=False)
    carried = run(place(1), tokens, left, left_other, carried=carried, last_call=False)
    slope, hidden, second, head, residual, forecast = run(
        place(2), tokens, far, far_other, carried=carried, last_call=True
    )

    forecast = forecast.reshape(2, 16, members * own, out_width)
    theirs = shift(take(forecast, 1 - core, 0), "c", 1)
    pair = jnp.concatenate([take(forecast, core, 0), theirs], 1)
    pair, hidden, residual, tokens = lax.optimization_barrier((pair, hidden, residual, tokens))
    gathered = lax.all_to_all(pair, ("x", "z"), 0, 0, tiled=True)
    samples = gathered.reshape(16 * 2 * members, own, out_width)
    hidden_t, residual_t, tokens_t = hidden.T, residual.T, tokens.T

    device = ((here * 4 + lax.axis_index("x")) * 4 + lax.axis_index("z")) * 2 + core
    target = jnp.take(observed, obs_index - device * own, axis=0)
    grad_raw, score_part, count_part = score(samples, target, valid_mask)

    line = jnp.arange(8)[:, None]
    sums = jnp.where(line == 0, score_part, count_part) + jnp.zeros((8, 128))
    sums = sums + shift(sums, "c", 1)
    sums = sums + shift(sums, "x", 1)
    sums = sums + shift(sums, "x", 2)
    riders = jnp.zeros((8, width - out_width))
    for i, value in enumerate(terms(sums[0, 0]) + terms(sums[1, 0])):
        riders = jnp.where(line == i, value, riders)
    riders = jnp.broadcast_to(riders.astype(BF16), (16, *riders.shape))

    returned = lax.all_to_all(
        grad_raw.reshape(16, 2 * members * own, out_width), ("x", "z"), 0, 0, tiled=True
    ).reshape(16, 2, members * own, out_width)
    back = shift(returned[:, 1], "c", 1)
    grad_rows = jnp.where(
        core == 0, jnp.stack([returned[:, 0], back]), jnp.stack([back, returned[:, 0]])
    ).reshape(rows, out_width)

    at = place(0)
    resid_grad = dot(grad_rows, head).astype(BF16)
    keep, send = early_grads(at, hidden_t, resid_grad, residual_t, grad_rows)
    early = add(keep, shift(send, "c", 1)).reshape(2, 2, 2, -1, width)
    keep, send = late_grads(at, resid_grad, second, slope, tokens_t)
    late = add(keep, shift(send, "c", 1)).reshape(2, 16, 2, 2, -1, width)
    a, b = ring_sum(early[:, :, 0], early[:, :, 1], "x")
    early = jnp.concatenate([a, b]).reshape(16, -1, width)
    n_second = shard * RING // 128
    early = lax.dynamic_update_slice(early, riders, (0, n_second, out_width))
    early = lax.all_to_all(early, ("z", "y"), 0, 0, tiled=True)
    late = late.transpose(0, 2, 3, 1, 4, 5)
    a, b = ring_sum(late[0], late[1], "y")
    late = lax.all_to_all(jnp.concatenate([a, b], 1), ("x", "z"), 0, 0, tiled=True)
    early = jnp.sum(early.astype(F32), 0)
    late = jnp.sum(late.astype(F32), 0)
    ride = early[n_second : n_second + 8, out_width]
    score_total = ride[0] + ride[1] + ride[2]
    valid_total = jnp.maximum(ride[3] + ride[4] + ride[5], 1.0)
    scale = 1.0 / valid_total
    n_first = late.shape[0] // 2
    return (
        jnp.concatenate([late[:n_first], late[n_first:]], 1) * scale,
        early[:n_second] * scale,
        early[n_second:, :out_width] * scale,
        score_total / valid_total,
    )


def solution(mesh):
    grid = Mesh(mesh.devices.reshape(4, 4, 2, 4), ("x", "z", "c", "y"))
    rows = P(("y", "x", "z", "c"))
    shares = P(("x", "z", "c", "y"), None)
    return jax.shard_map(
        per_device,
        mesh=grid,
        in_specs=(
            P(("x", "z", "c"), "y", None),
            P(None, "y"),
            P("y", None),
            P(None, "y"),
            rows,
            rows,
            rows,
        ),
        out_specs=(shares, shares, shares, P()),
        check_vma=False,
    )
```

```python
import functools

import jax
import jax.numpy as jnp
from jax import lax
from jax.experimental import pallas as pl
from jax.experimental.pallas import tpu as pltpu
from jax.sharding import Mesh
from jax.sharding import PartitionSpec as P

SMOOTHING = 1.0
LOSS_SCALE = 4096.0
RING = 4
PAIR_LOW = ((0, 1), (1, 0), (2, 3), (3, 2))
PAIR_HIGH = ((0, 3), (3, 0), (1, 2), (2, 1))
ROOT_2_PI = 0.7978845608028654
CUBIC = 0.044715
LANES = 256
MIB = 1 << 20
F32 = jnp.float32
BF16 = jnp.bfloat16


def shift(x, axis, by):
    size = lax.axis_size(axis)
    return lax.ppermute(x, axis, [(i, (i + by) % size) for i in range(size)])


def dot(a, b, contract=((1,), (0,))):
    return lax.dot_general(a, b, (contract, ((), ())), preferred_element_type=F32)


def params(cells):
    return pltpu.CompilerParams(
        dimension_semantics=("arbitrary",) * cells, vmem_limit_bytes=56 * MIB
    )


def forward_kernel(first_call, last_call, block_rows, sizes, *refs):
    width, half, head_rows = sizes
    place, tokens, mine, theirs = refs[:4]
    refs = refs[4:]
    if first_call:
        total_in = None
        slope, hidden, second, head, total = refs
    elif last_call:
        total_in, _, _, _, head_in, slope, hidden, second, head, residual, forecast = refs
    else:
        total_in, _, _, _, _, slope, hidden, second, head, total = refs
    block, core = place[0], place[1]
    chunks = width // LANES
    start = width
    head_start = start + chunks * half

    @pl.when(pl.program_id(0) == 0)
    def _():
        if last_call:
            head[...] = head_in[...]
        for pack, side in ((mine, core), (theirs, 1 - core)):
            below = pl.multiple_of(side * half, half)
            for q in range(chunks):
                second[pl.ds(below, half), q * LANES : (q + 1) * LANES] = pack[
                    start + q * half : start + (q + 1) * half, :
                ]
            for e in range(2):
                piece = pack[head_start + e * head_rows : head_start + (e + 1) * head_rows, :]
                lane = pl.multiple_of(side * (width // 2) + e * LANES, LANES)
                row = pl.multiple_of(block * head_rows, 64) if last_call else 0
                head[pl.ds(row, head_rows), pl.ds(lane, LANES)] = piece

    rows = tokens[...]
    base = rows.astype(F32) if first_call else total_in[...]
    sums = [base[:, q * LANES : (q + 1) * LANES] for q in range(chunks)]
    for pack, side in ((mine, core), (theirs, 1 - core)):
        x = dot(rows, pack[:width, :])
        sq = x * x
        t = jnp.tanh(ROOT_2_PI * (x + CUBIC * x * sq))
        up = 0.5 * (1.0 + t)
        active = (x * up).astype(BF16)
        lane = pl.multiple_of(side * half, half)
        slope[:, pl.ds(lane, half)] = up + (0.5 * ROOT_2_PI) * x * (1.0 - t * t) * (
            1.0 + (3.0 * CUBIC) * sq
        )
        hidden[:, pl.ds(lane, half)] = active
        for q in range(chunks):
            sums[q] = sums[q] + dot(active, pack[start + q * half : start + (q + 1) * half, :])
    full = jnp.concatenate(sums, 1)
    if last_call:
        rounded = full.astype(BF16)
        residual[...] = rounded
        forecast[...] = dot(rounded, head[...], ((1,), (1,))).astype(BF16)
    else:
        total[...] = full


def forward_part(place, tokens, mine, theirs, carried, out_width, last_call):
    rows, width = tokens.shape
    half = LANES
    hid = 2 * half * RING
    head_rows = out_width // RING
    first_call = carried is None
    block_rows = min(rows, 256)
    whole = lambda shape: pl.BlockSpec(shape, lambda i, s: (0,) * len(shape))
    by_rows = lambda cols: pl.BlockSpec((block_rows, cols), lambda i, s: (i, 0))
    in_place = pl.BlockSpec(memory_space=pl.ANY)
    in_specs = [by_rows(width), whole(mine.shape), whole(theirs.shape)]
    args = [tokens, mine, theirs]
    aliases = {}
    if not first_call:
        slope, hidden, second, head, total = carried
        args += [total, slope, hidden, second, head]
        in_specs += [by_rows(width), in_place, in_place, in_place]
        in_specs += [whole((out_width, width)) if last_call else in_place]
        aliases = {5: 0, 6: 1, 7: 2}
        if not last_call:
            aliases = {**aliases, 8: 3, 4: 4}
    column = pl.BlockSpec((block_rows, 2 * half), lambda i, s: (i, s[0]))
    out_specs = [
        column,
        column,
        pl.BlockSpec((2 * half, width), lambda i, s: (s[0], 0)),
        whole((out_width, width))
        if last_call
        else pl.BlockSpec((head_rows, width), lambda i, s: (s[0], 0)),
    ]
    out_shape = [
        jax.ShapeDtypeStruct((rows, hid), F32),
        jax.ShapeDtypeStruct((rows, hid), BF16),
        jax.ShapeDtypeStruct((hid, width), BF16),
        jax.ShapeDtypeStruct((out_width, width), BF16),
    ]
    if last_call:
        out_specs += [by_rows(width), by_rows(out_width)]
        out_shape += [
            jax.ShapeDtypeStruct((rows, width), BF16),
            jax.ShapeDtypeStruct((rows, out_width), BF16),
        ]
    else:
        out_specs += [by_rows(width)]
        out_shape += [jax.ShapeDtypeStruct((rows, width), F32)]
    return pl.pallas_call(
        functools.partial(
            forward_kernel, first_call, last_call, block_rows, (width, half, head_rows)
        ),
        grid_spec=pltpu.PrefetchScalarGridSpec(
            num_scalar_prefetch=1,
            grid=(rows // block_rows,),
            in_specs=in_specs,
            out_specs=out_specs,
        ),
        out_shape=out_shape,
        input_output_aliases=aliases,
        compiler_params=params(1),
        cost_estimate=pl.CostEstimate(
            flops=8 * rows * width * half, bytes_accessed=12 * MIB, transcendentals=rows * 2 * half
        ),
        name="forward_part",
    )(place, *args)


def store_halves(core, parts, keep, send):
    n, _, rows, cols = parts.shape
    zero = parts[:, 0].reshape(n * rows, cols).astype(BF16)
    one = parts[:, 1].reshape(n * rows, cols).astype(BF16)

    @pl.when(core == 0)
    def _():
        keep[0] = zero
        send[0] = one

    @pl.when(core == 1)
    def _():
        keep[0] = one
        send[0] = zero


def early_kernel(place, hidden, resid_grad, residual, grad_rows, riders, keep, send):
    second = dot(hidden[...], resid_grad[...], ((0,), (0,)))
    head = dot(residual[...], grad_rows[...], ((0,), (0,)))
    width, out_width = second.shape[1], head.shape[1]
    second = second.reshape(RING, 2, RING, -1, width)
    head = head.reshape(RING, 2, RING, -1, out_width)
    blank = jnp.broadcast_to(riders[...], (*head.shape[:4], width - out_width))
    both = jnp.concatenate([second, jnp.concatenate([head, blank], 4)], 3)
    both = both.reshape(RING, 2, -1, width)
    store_halves(place[1], both, keep, send)


def early_grads(place, hidden, resid_grad, residual, grad_rows, riders):
    rows, hid = hidden.shape
    width, out_width = residual.shape[1], grad_rows.shape[1]
    lines = (hid + width) // RING // 2
    gray = lambda i: 2 * ((i // 2 + i) % 2) + i // 2
    out = pl.BlockSpec((1, lines, width), lambda i, s: (gray(i), 0, 0))
    return pl.pallas_call(
        early_kernel,
        grid_spec=pltpu.PrefetchScalarGridSpec(
            num_scalar_prefetch=1,
            grid=(RING,),
            in_specs=[
                pl.BlockSpec((rows, hid // RING), lambda i, s: (0, i)),
                pl.BlockSpec((rows, width), lambda i, s: (0, 0)),
                pl.BlockSpec((rows, width // RING), lambda i, s: (0, i)),
                pl.BlockSpec((rows, out_width), lambda i, s: (0, 0)),
                pl.BlockSpec(riders.shape, lambda i, s: (0, 0)),
            ],
            out_specs=[out, out],
        ),
        out_shape=[jax.ShapeDtypeStruct((RING, lines, width), BF16)] * 2,
        compiler_params=params(1),
        cost_estimate=pl.CostEstimate(
            flops=2 * rows * width * (hid + out_width), bytes_accessed=18 * MIB, transcendentals=0
        ),
        name="early_grads",
    )(place, hidden, resid_grad, residual, grad_rows, riders)


def late_kernel(place, resid_grad, second, slope, tokens, keep, send):
    hidden_grad = dot(resid_grad[...], second[...], ((1,), (1,)))
    preact_grad = (slope[...] * hidden_grad).astype(BF16)
    first = dot(tokens[...], preact_grad, ((0,), (0,)))
    cols = first.shape[1]
    parts = first.reshape(16, 2, RING, -1, cols)
    parts = jnp.stack([parts[:, :, i] for i in (0, 3, 1, 2)], 2)
    store_halves(place[1], parts.reshape(16, 2, -1, cols), keep, send)


def late_grads(place, part, resid_grad, second, slope, tokens):
    rows, width = resid_grad.shape
    tile = 2 * LANES
    steps = width // tile
    out = pl.BlockSpec((1, width // 2, tile), lambda j, s: (0, 0, j))
    return pl.pallas_call(
        late_kernel,
        grid_spec=pltpu.PrefetchScalarGridSpec(
            num_scalar_prefetch=1,
            grid=(steps,),
            in_specs=[
                pl.BlockSpec((rows, width), lambda j, s: (0, 0)),
                pl.BlockSpec((tile, width), lambda j, s: (part * steps + j, 0)),
                pl.BlockSpec((rows, tile), lambda j, s: (0, part * steps + j)),
                pl.BlockSpec((rows, width), lambda j, s: (0, 0)),
            ],
            out_specs=[out, out],
        ),
        out_shape=[jax.ShapeDtypeStruct((1, width // 2, width), BF16)] * 2,
        compiler_params=params(1),
        cost_estimate=pl.CostEstimate(
            flops=4 * rows * width * width, bytes_accessed=12 * MIB, transcendentals=0
        ),
        name="late_grads",
    )(place, resid_grad, second, slope, tokens)


def add(a, b):
    return (a.astype(F32) + b.astype(F32)).astype(BF16)


def take(x, index, axis):
    return lax.dynamic_index_in_dim(x, index, axis, keepdims=False)


def ring_bits(axis):
    here = lax.axis_index(axis)
    high = here // 2
    return (high + here) % 2, high


def ring_chain(axis, low_first):
    low, high = ring_bits(axis)
    if low_first:
        steps = ((PAIR_LOW, low, 0), (PAIR_HIGH, high, 0))
    else:
        steps = ((PAIR_HIGH, high, 1), (PAIR_LOW, low, 0))
    return [(pairs, axis, bit, dim) for pairs, bit, dim in steps]


def outgoing(x, step):
    _, _, bit, dim = step
    return take(x, 1 - bit, dim)


def swapped(x, sent, step):
    pairs, axis, bit, dim = step
    return add(take(x, bit, dim), lax.ppermute(sent, axis, pairs))


def tie(*arrays):
    return lax.optimization_barrier(arrays)


def terms(value):
    first = lax.reduce_precision(value, 8, 7)
    second = lax.reduce_precision(value - first, 8, 7)
    third = value - first - second
    return first, second, third


def pick(flag, one, zero):
    return jnp.where(flag == 1, one, zero)


def pack_kernel(side, first, second, head, out):
    width, half = first.shape
    out[:width, :] = first[...]
    at = width
    for q in range(second.shape[1] // LANES):
        out[at : at + half, :] = second[:, q * LANES : (q + 1) * LANES]
        at += half
    turned = head[...].astype(F32).T.astype(BF16)
    for e in range(turned.shape[1] // LANES):
        out[at : at + turned.shape[0], :] = turned[:, e * LANES : (e + 1) * LANES]
        at += turned.shape[0]


def packed(side, first, second, head):
    width, shard = first.shape
    half = shard // 2
    lines = width + half * width // LANES + head.shape[1] * width // 2 // LANES
    return pl.pallas_call(
        pack_kernel,
        grid_spec=pltpu.PrefetchScalarGridSpec(
            num_scalar_prefetch=1,
            grid=(1,),
            in_specs=[
                pl.BlockSpec((width, half), lambda i, s: (0, s[0])),
                pl.BlockSpec((half, width), lambda i, s: (s[0], 0)),
                pl.BlockSpec((width // 2, head.shape[1]), lambda i, s: (s[0], 0)),
            ],
            out_specs=pl.BlockSpec((lines, LANES), lambda i, s: (0, 0)),
        ),
        out_shape=jax.ShapeDtypeStruct((lines, LANES), BF16),
        compiler_params=params(1),
        name="packed",
    )(side, first, second, head)


def score(samples, target, valid_mask):
    count = samples.shape[0]
    wide = samples.astype(F32)
    gram = jnp.einsum("mpo,npo->pmn", samples, samples, preferred_element_type=F32)
    squares = jnp.sum(wide * wide, axis=2).T
    dist_sq = squares[:, :, None] + squares[:, None, :] - 2.0 * gram
    spread = jnp.sqrt(dist_sq + SMOOTHING)
    kernel = 1.0 / spread
    kernel_sum = jnp.sum(kernel, axis=2)
    pulled = jnp.einsum("pmn,npo->mpo", kernel, wide, precision=lax.Precision.HIGHEST)
    offset = wide - target[None]
    error_norm = jnp.sqrt(jnp.sum(offset * offset, axis=2) + SMOOTHING)
    repulse = wide * kernel_sum.T[:, :, None] - pulled
    validity = valid_mask.astype(F32)
    grad_raw = (
        LOSS_SCALE
        * validity[None, :, None]
        * (offset / (count * error_norm[:, :, None]) - repulse / (count * count))
    ).astype(BF16)
    scores = validity * (
        jnp.mean(error_norm, axis=0) - jnp.sum(spread, axis=(1, 2)) / (2.0 * count * count)
    )
    return grad_raw, jnp.sum(scores), jnp.sum(validity)


def per_device(latents, w_first, w_second, readout_matrix, observed, obs_index, valid_mask):
    members, patches, width = latents.shape
    out_width = observed.shape[1]
    core = lax.axis_index("c")
    here = lax.axis_index("y")
    own = obs_index.shape[0]
    rows = members * patches
    shard = w_first.shape[1]
    half = shard // 2

    side = jnp.reshape(core, (1,)).astype(jnp.int32)
    mine = packed(side, w_first, w_second, readout_matrix)
    right = shift(mine, "y", 1)
    left = shift(mine, "y", -1)
    lines = mine.shape[0] // 2
    latents, other_side, mine = tie(latents, 1 - side, mine)
    tokens = (
        latents.reshape(members, 16, 2, own, width).transpose(2, 1, 0, 3, 4).reshape(rows, width)
    )
    theirs = packed(other_side, w_first, w_second, readout_matrix)
    place = lambda off: jnp.stack([(here + off) % RING, core]).astype(jnp.int32)
    run = functools.partial(forward_part, out_width=out_width)
    carried = run(place(0), tokens, mine, theirs, carried=None, last_call=False)
    right, left, *carried = tie(right, left, *carried)
    far = [shift(right[:lines], "y", 1), shift(left[lines:], "y", -1)]
    right_other = shift(right, "c", 1)
    left_other = shift(left, "c", 1)
    carried = run(place(3), tokens, right, right_other, carried=carried, last_call=False)
    carried = run(place(1), tokens, left, left_other, carried=carried, last_call=False)
    near, past, *carried = tie(*far, *carried)
    far = jnp.concatenate([near, past], 0)
    far_other = shift(far, "c", 1)
    slope, hidden, second, head, residual, forecast = run(
        place(2), tokens, far, far_other, carried=carried, last_call=True
    )

    forecast = forecast.reshape(2, 16, members * own, out_width)
    theirs = shift(take(forecast, 1 - core, 0), "c", 1)
    pair = jnp.concatenate([take(forecast, core, 0), theirs], 1)
    device = ((here * 4 + lax.axis_index("x")) * 4 + lax.axis_index("z")) * 2 + core
    target = jnp.take(observed, obs_index - device * own, axis=0)
    pair, target = tie(pair, target)
    gathered = lax.all_to_all(pair, ("x", "z"), 0, 0, tiled=True)
    samples = gathered.reshape(16 * 2 * members, own, out_width)
    grad_raw, score_part, count_part = score(samples, target, valid_mask)

    shape = (8, width - out_width)
    line = lax.broadcasted_iota(jnp.int32, shape, 0)
    lane = lax.broadcasted_iota(jnp.int32, shape, 1)
    riders = jnp.where(line == 3, count_part, 0.0)
    for i, value in enumerate(terms(score_part)):
        riders = jnp.where(line == i, value, riders)
    riders = jnp.where(lane == 2 * lax.axis_index("x") + core, riders, 0.0)

    returned = lax.all_to_all(
        grad_raw.reshape(16, 2 * members * own, out_width), ("x", "z"), 0, 0, tiled=True
    ).reshape(16, 2, members * own, out_width)
    back = shift(returned[:, 1], "c", 1)
    grad_rows = jnp.where(
        core == 0, jnp.stack([returned[:, 0], back]), jnp.stack([back, returned[:, 0]])
    ).reshape(rows, out_width)

    at = place(0)
    resid_grad = dot(grad_rows, head).astype(BF16)
    early = early_grads(at, hidden, resid_grad, residual, grad_rows, riders)
    resid_grad, *early = tie(resid_grad, *early)
    early = add(early[0], shift(early[1], "c", 1)).reshape(2, 2, 2, -1, width)
    flows = [
        (early[:, :, 0], ring_chain("x", True)),
        (early[:, :, 1], ring_chain("x", False)),
    ]
    late = late_grads(at, 0, resid_grad, second, slope, tokens)
    sent = [outgoing(x, steps[0]) for x, steps in flows]
    resid_grad, *rest = tie(resid_grad, *sent, *late)
    sent, late = rest[:2], rest[2:]
    early = [swapped(x, s, steps[0]) for (x, steps), s in zip(flows, sent)]
    a = add(late[0], shift(late[1], "c", 1)).reshape(16, 2, 2, -1, width)
    a = a.transpose(1, 2, 0, 3, 4)
    late = late_grads(at, 1, resid_grad, second, slope, tokens)
    a_steps, b_steps = ring_chain("y", True), ring_chain("y", False)
    a_sent = outgoing(a, a_steps[0])
    a_sent, *late = tie(a_sent, *late)
    a = swapped(a, a_sent, a_steps[0])
    b = add(late[0], shift(late[1], "c", 1)).reshape(16, 2, 2, -1, width)
    b = b.transpose(1, 2, 0, 3, 4)
    early = [
        swapped(x, outgoing(x, steps[1]), steps[1]) for x, (_, steps) in zip(early, flows)
    ]
    b = swapped(b, outgoing(b, b_steps[0]), b_steps[0])
    a = swapped(a, outgoing(a, a_steps[1]), a_steps[1])
    b = swapped(b, outgoing(b, b_steps[1]), b_steps[1])
    early = jnp.concatenate(early).reshape(16, -1, width)
    early = lax.all_to_all(early, ("z", "y"), 0, 0, tiled=True)
    late = lax.all_to_all(jnp.concatenate([a, b], 1), ("x", "z"), 0, 0, tiled=True)
    early = jnp.sum(early.astype(F32), 0)
    late = jnp.sum(late.astype(F32), 0)
    n_second = shard * RING // 128
    ride = jnp.sum(early[n_second : n_second + 8, out_width:], 1)
    score_total = ride[0] + ride[1] + ride[2]
    valid_total = jnp.maximum(ride[3], 1.0)
    scale = 1.0 / valid_total
    n_first = late.shape[0] // 2
    return (
        jnp.concatenate([late[:n_first], late[n_first:]], 1) * scale,
        early[:n_second] * scale,
        early[n_second:, :out_width] * scale,
        score_total / valid_total,
    )


def solution(mesh):
    grid = Mesh(mesh.devices.reshape(4, 4, 2, 4), ("x", "z", "c", "y"))
    rows = P(("y", "x", "z", "c"))
    shares = P(("x", "z", "c", "y"), None)
    return jax.shard_map(
        per_device,
        mesh=grid,
        in_specs=(
            P(("x", "z", "c"), "y", None),
            P(None, "y"),
            P("y", None),
            P(None, "y"),
            rows,
            rows,
            rows,
        ),
        out_specs=(shares, shares, shares, P()),
        check_vma=False,
    )
```

```python
import functools

import jax
import jax.numpy as jnp
from jax import lax
from jax.experimental import pallas as pl
from jax.experimental.pallas import tpu as pltpu
from jax.sharding import Mesh
from jax.sharding import PartitionSpec as P

SMOOTHING = 1.0
LOSS_SCALE = 4096.0
RING = 4
PAIR_LOW = ((0, 1), (1, 0), (2, 3), (3, 2))
PAIR_HIGH = ((0, 3), (3, 0), (1, 2), (2, 1))
ROOT_2_PI = 0.7978845608028654
CUBIC = 0.044715
LANES = 256
MIB = 1 << 20
F32 = jnp.float32
BF16 = jnp.bfloat16


def shift(x, axis, by):
    size = lax.axis_size(axis)
    return lax.ppermute(x, axis, [(i, (i + by) % size) for i in range(size)])


def dot(a, b, contract=((1,), (0,))):
    return lax.dot_general(a, b, (contract, ((), ())), preferred_element_type=F32)


def params(cells):
    return pltpu.CompilerParams(
        dimension_semantics=("arbitrary",) * cells, vmem_limit_bytes=56 * MIB
    )


def forward_kernel(first_call, last_call, block_rows, sizes, *refs):
    width, half, head_rows = sizes
    place, tokens, mine, theirs = refs[:4]
    refs = refs[4:]
    if first_call:
        total_in = None
        slope, hidden, second, head, total = refs
    elif last_call:
        total_in, _, _, _, head_in, slope, hidden, second, head, residual, forecast = refs
    else:
        total_in, _, _, _, _, slope, hidden, second, head, total = refs
    block, core = place[0], place[1]
    chunks = width // LANES
    start = width
    head_start = start + chunks * half

    @pl.when(pl.program_id(0) == 0)
    def _():
        if last_call:
            head[...] = head_in[...]
        for pack, side in ((mine, core), (theirs, 1 - core)):
            below = pl.multiple_of(side * half, half)
            for q in range(chunks):
                second[pl.ds(below, half), q * LANES : (q + 1) * LANES] = pack[
                    start + q * half : start + (q + 1) * half, :
                ]
            for e in range(2):
                piece = pack[head_start + e * head_rows : head_start + (e + 1) * head_rows, :]
                lane = pl.multiple_of(side * (width // 2) + e * LANES, LANES)
                row = pl.multiple_of(block * head_rows, 64) if last_call else 0
                head[pl.ds(row, head_rows), pl.ds(lane, LANES)] = piece

    rows = tokens[...]
    base = rows.astype(F32) if first_call else total_in[...]
    sums = [base[:, q * LANES : (q + 1) * LANES] for q in range(chunks)]
    for pack, side in ((mine, core), (theirs, 1 - core)):
        x = dot(rows, pack[:width, :])
        sq = x * x
        t = jnp.tanh(ROOT_2_PI * (x + CUBIC * x * sq))
        up = 0.5 * (1.0 + t)
        active = (x * up).astype(BF16)
        lane = pl.multiple_of(side * half, half)
        slope[:, pl.ds(lane, half)] = up + (0.5 * ROOT_2_PI) * x * (1.0 - t * t) * (
            1.0 + (3.0 * CUBIC) * sq
        )
        hidden[:, pl.ds(lane, half)] = active
        for q in range(chunks):
            sums[q] = sums[q] + dot(active, pack[start + q * half : start + (q + 1) * half, :])
    full = jnp.concatenate(sums, 1)
    if last_call:
        rounded = full.astype(BF16)
        residual[...] = rounded
        forecast[...] = dot(rounded, head[...], ((1,), (1,))).astype(BF16)
    else:
        total[...] = full


def forward_part(place, tokens, mine, theirs, carried, out_width, last_call):
    rows, width = tokens.shape
    half = LANES
    hid = 2 * half * RING
    head_rows = out_width // RING
    first_call = carried is None
    block_rows = min(rows, 256)
    whole = lambda shape: pl.BlockSpec(shape, lambda i, s: (0,) * len(shape))
    by_rows = lambda cols: pl.BlockSpec((block_rows, cols), lambda i, s: (i, 0))
    in_place = pl.BlockSpec(memory_space=pl.ANY)
    in_specs = [by_rows(width), whole(mine.shape), whole(theirs.shape)]
    args = [tokens, mine, theirs]
    aliases = {}
    if not first_call:
        slope, hidden, second, head, total = carried
        args += [total, slope, hidden, second, head]
        in_specs += [by_rows(width), in_place, in_place, in_place]
        in_specs += [whole((out_width, width)) if last_call else in_place]
        aliases = {5: 0, 6: 1, 7: 2}
        if not last_call:
            aliases = {**aliases, 8: 3, 4: 4}
    column = pl.BlockSpec((block_rows, 2 * half), lambda i, s: (i, s[0]))
    out_specs = [
        column,
        column,
        pl.BlockSpec((2 * half, width), lambda i, s: (s[0], 0)),
        whole((out_width, width))
        if last_call
        else pl.BlockSpec((head_rows, width), lambda i, s: (s[0], 0)),
    ]
    out_shape = [
        jax.ShapeDtypeStruct((rows, hid), F32),
        jax.ShapeDtypeStruct((rows, hid), BF16),
        jax.ShapeDtypeStruct((hid, width), BF16),
        jax.ShapeDtypeStruct((out_width, width), BF16),
    ]
    if last_call:
        out_specs += [by_rows(width), by_rows(out_width)]
        out_shape += [
            jax.ShapeDtypeStruct((rows, width), BF16),
            jax.ShapeDtypeStruct((rows, out_width), BF16),
        ]
    else:
        out_specs += [by_rows(width)]
        out_shape += [jax.ShapeDtypeStruct((rows, width), F32)]
    return pl.pallas_call(
        functools.partial(
            forward_kernel, first_call, last_call, block_rows, (width, half, head_rows)
        ),
        grid_spec=pltpu.PrefetchScalarGridSpec(
            num_scalar_prefetch=1,
            grid=(rows // block_rows,),
            in_specs=in_specs,
            out_specs=out_specs,
        ),
        out_shape=out_shape,
        input_output_aliases=aliases,
        compiler_params=params(1),
        cost_estimate=pl.CostEstimate(
            flops=8 * rows * width * half, bytes_accessed=12 * MIB, transcendentals=rows * 2 * half
        ),
        name="forward_part",
    )(place, *args)


def store_halves(core, parts, keep, send):
    n, _, rows, cols = parts.shape
    zero = parts[:, 0].reshape(n * rows, cols).astype(BF16)
    one = parts[:, 1].reshape(n * rows, cols).astype(BF16)

    @pl.when(core == 0)
    def _():
        keep[0] = zero
        send[0] = one

    @pl.when(core == 1)
    def _():
        keep[0] = one
        send[0] = zero


def riders(place, scalars, shape):
    line = lax.broadcasted_iota(jnp.int32, shape, 0)
    lane = lax.broadcasted_iota(jnp.int32, shape, 1)
    score = jnp.full(shape, scalars[0], F32)
    out = jnp.where(line == 3, scalars[1], 0.0)
    for i in range(3):
        term = score.astype(BF16).astype(F32)
        out = jnp.where(line == i, term, out)
        score = score - term
    return jnp.where(lane == 2 * place[2] + place[1], out, 0.0)


def early_kernel(place, hidden, resid_grad, residual, grad_rows, scalars, keep, send):
    second = dot(hidden[...], resid_grad[...], ((0,), (0,)))
    head = dot(residual[...], grad_rows[...], ((0,), (0,)))
    width, out_width = second.shape[1], head.shape[1]
    second = second.reshape(RING, 2, RING, -1, width)
    head = head.reshape(RING, 2, RING, -1, out_width)
    blank = riders(place, scalars, (head.shape[3], width - out_width))
    blank = jnp.broadcast_to(blank, (*head.shape[:3], *blank.shape))
    both = jnp.concatenate([second, jnp.concatenate([head, blank], 4)], 3)
    both = both.reshape(RING, 2, -1, width)
    store_halves(place[1], both, keep, send)


def early_grads(place, hidden, resid_grad, residual, grad_rows, scalars):
    rows, hid = hidden.shape
    width, out_width = residual.shape[1], grad_rows.shape[1]
    lines = (hid + width) // RING // 2
    gray = lambda i: 2 * ((i // 2 + i) % 2) + i // 2
    out = pl.BlockSpec((1, lines, width), lambda i, s: (gray(i), 0, 0))
    return pl.pallas_call(
        early_kernel,
        grid_spec=pltpu.PrefetchScalarGridSpec(
            num_scalar_prefetch=1,
            grid=(RING,),
            in_specs=[
                pl.BlockSpec((rows, hid // RING), lambda i, s: (0, i)),
                pl.BlockSpec((rows, width), lambda i, s: (0, 0)),
                pl.BlockSpec((rows, width // RING), lambda i, s: (0, i)),
                pl.BlockSpec((rows, out_width), lambda i, s: (0, 0)),
                pl.BlockSpec(memory_space=pltpu.SMEM),
            ],
            out_specs=[out, out],
        ),
        out_shape=[jax.ShapeDtypeStruct((RING, lines, width), BF16)] * 2,
        compiler_params=params(1),
        cost_estimate=pl.CostEstimate(
            flops=2 * rows * width * (hid + out_width), bytes_accessed=18 * MIB, transcendentals=0
        ),
        name="early_grads",
    )(place, hidden, resid_grad, residual, grad_rows, scalars)


def late_kernel(place, resid_grad, second, slope, tokens, keep, send):
    hidden_grad = dot(resid_grad[...], second[...], ((1,), (1,)))
    preact_grad = (slope[...] * hidden_grad).astype(BF16)
    first = dot(tokens[...], preact_grad, ((0,), (0,)))
    cols = first.shape[1]
    parts = first.reshape(16, 2, RING, -1, cols)
    parts = jnp.stack([parts[:, :, i] for i in (0, 3, 1, 2)], 2)
    store_halves(place[1], parts.reshape(16, 2, -1, cols), keep, send)


def late_grads(place, part, resid_grad, second, slope, tokens):
    rows, width = resid_grad.shape
    tile = 2 * LANES
    steps = width // tile
    out = pl.BlockSpec((1, width // 2, tile), lambda j, s: (0, 0, j))
    return pl.pallas_call(
        late_kernel,
        grid_spec=pltpu.PrefetchScalarGridSpec(
            num_scalar_prefetch=1,
            grid=(steps,),
            in_specs=[
                pl.BlockSpec((rows, width), lambda j, s: (0, 0)),
                pl.BlockSpec((tile, width), lambda j, s: (part * steps + j, 0)),
                pl.BlockSpec((rows, tile), lambda j, s: (0, part * steps + j)),
                pl.BlockSpec((rows, width), lambda j, s: (0, 0)),
            ],
            out_specs=[out, out],
        ),
        out_shape=[jax.ShapeDtypeStruct((1, width // 2, width), BF16)] * 2,
        compiler_params=params(1),
        cost_estimate=pl.CostEstimate(
            flops=4 * rows * width * width, bytes_accessed=12 * MIB, transcendentals=0
        ),
        name="late_grads",
    )(place, resid_grad, second, slope, tokens)


def add(a, b):
    return (a.astype(F32) + b.astype(F32)).astype(BF16)


def take(x, index, axis):
    return lax.dynamic_index_in_dim(x, index, axis, keepdims=False)


def ring_bits(axis):
    here = lax.axis_index(axis)
    high = here // 2
    return (high + here) % 2, high


def ring_chain(axis, low_first):
    low, high = ring_bits(axis)
    if low_first:
        steps = ((PAIR_LOW, low, 0), (PAIR_HIGH, high, 0))
    else:
        steps = ((PAIR_HIGH, high, 1), (PAIR_LOW, low, 0))
    return [(pairs, axis, bit, dim) for pairs, bit, dim in steps]


def outgoing(x, step):
    _, _, bit, dim = step
    return take(x, 1 - bit, dim)


def sent_along(x, step):
    return lax.ppermute(x, step[1], step[0])


def kept_plus(x, arrived, step):
    _, _, bit, dim = step
    return add(take(x, bit, dim), arrived)


def by_ring(x):
    return x.reshape(16, 2, 2, -1, x.shape[-1]).transpose(1, 2, 0, 3, 4)


def tie(*arrays):
    return lax.optimization_barrier(arrays)


def after(x, *others):
    return lax.optimization_barrier((x, *others))[0]


def pack_kernel(side, first, second, head, out):
    width, half = first.shape
    out[:width, :] = first[...]
    at = width
    for q in range(second.shape[1] // LANES):
        out[at : at + half, :] = second[:, q * LANES : (q + 1) * LANES]
        at += half
    turned = head[...].astype(F32).T.astype(BF16)
    for e in range(turned.shape[1] // LANES):
        out[at : at + turned.shape[0], :] = turned[:, e * LANES : (e + 1) * LANES]
        at += turned.shape[0]


def packed(side, first, second, head):
    width, shard = first.shape
    half = shard // 2
    lines = width + half * width // LANES + head.shape[1] * width // 2 // LANES
    return pl.pallas_call(
        pack_kernel,
        grid_spec=pltpu.PrefetchScalarGridSpec(
            num_scalar_prefetch=1,
            grid=(1,),
            in_specs=[
                pl.BlockSpec((width, half), lambda i, s: (0, s[0])),
                pl.BlockSpec((half, width), lambda i, s: (s[0], 0)),
                pl.BlockSpec((width // 2, head.shape[1]), lambda i, s: (s[0], 0)),
            ],
            out_specs=pl.BlockSpec((lines, LANES), lambda i, s: (0, 0)),
        ),
        out_shape=jax.ShapeDtypeStruct((lines, LANES), BF16),
        compiler_params=params(1),
        name="packed",
    )(side, first, second, head)


def score(samples, target, valid_mask):
    count = samples.shape[0]
    wide = samples.astype(F32)
    gram = jnp.einsum("mpo,npo->pmn", samples, samples, preferred_element_type=F32)
    squares = jnp.sum(wide * wide, axis=2).T
    dist_sq = squares[:, :, None] + squares[:, None, :] - 2.0 * gram
    spread = jnp.sqrt(dist_sq + SMOOTHING)
    kernel = 1.0 / spread
    kernel_sum = jnp.sum(kernel, axis=2)
    pulled = jnp.einsum("pmn,npo->mpo", kernel, wide, precision=lax.Precision.HIGHEST)
    offset = wide - target[None]
    error_norm = jnp.sqrt(jnp.sum(offset * offset, axis=2) + SMOOTHING)
    repulse = wide * kernel_sum.T[:, :, None] - pulled
    validity = valid_mask.astype(F32)
    grad_raw = (
        LOSS_SCALE
        * validity[None, :, None]
        * (offset / (count * error_norm[:, :, None]) - repulse / (count * count))
    ).astype(BF16)
    scores = validity * (
        jnp.mean(error_norm, axis=0) - jnp.sum(spread, axis=(1, 2)) / (2.0 * count * count)
    )
    return grad_raw, jnp.sum(scores), jnp.sum(validity)


def per_device(latents, w_first, w_second, readout_matrix, observed, obs_index, valid_mask):
    members, patches, width = latents.shape
    out_width = observed.shape[1]
    core = lax.axis_index("c")
    here = lax.axis_index("y")
    own = obs_index.shape[0]
    rows = members * patches
    shard = w_first.shape[1]
    half = shard // 2

    side = jnp.reshape(core, (1,)).astype(jnp.int32)
    mine = packed(side, w_first, w_second, readout_matrix)
    right = shift(mine, "y", 1)
    left = shift(mine, "y", -1)
    lines = mine.shape[0] // 2
    latents, other_side, mine = tie(latents, 1 - side, mine)
    tokens = (
        latents.reshape(members, 32, own, width).transpose(1, 0, 2, 3).reshape(rows, width)
    )
    theirs = packed(other_side, w_first, w_second, readout_matrix)
    place = lambda off: jnp.stack([(here + off) % RING, core, lax.axis_index("x")]).astype(jnp.int32)
    run = functools.partial(forward_part, out_width=out_width)
    carried = run(place(0), tokens, mine, theirs, carried=None, last_call=False)
    right, left, *carried = tie(right, left, *carried)
    far = [right[:lines], left[lines:]]
    right_other = shift(after(right, *far), "c", 1)
    left_other = shift(after(left, *far), "c", 1)
    far = [shift(far[0], "y", 1), shift(far[1], "y", -1)]
    carried = run(place(3), tokens, right, right_other, carried=carried, last_call=False)
    carried = run(place(1), tokens, left, left_other, carried=carried, last_call=False)
    near, past, *carried = tie(*far, *carried)
    far = jnp.concatenate([near, past], 0)
    far_other = shift(far, "c", 1)
    slope, hidden, second, head, residual, forecast = run(
        place(2), tokens, far, far_other, carried=carried, last_call=True
    )

    group = ("x", "z", "c")
    device = ((here * 4 + lax.axis_index("x")) * 4 + lax.axis_index("z")) * 2 + core
    target = jnp.take(observed, obs_index - device * own, axis=0)
    forecast, target = tie(forecast.reshape(32, members * own, out_width), target)
    gathered = lax.all_to_all(forecast, group, 0, 0, tiled=True)
    samples = gathered.reshape(32 * members, own, out_width)
    grad_raw, score_part, count_part = score(samples, target, valid_mask)
    grad_rows = lax.all_to_all(
        grad_raw.reshape(32, members * own, out_width), group, 0, 0, tiled=True
    ).reshape(rows, out_width)

    at = place(0)
    scalars = jnp.stack([score_part, count_part])
    resid_grad = dot(grad_rows, head).astype(BF16)
    early = early_grads(at, hidden, resid_grad, residual, grad_rows, scalars)
    early_in = shift(early[1], "c", 1)
    late = late_grads(at, 0, after(resid_grad, early[1]), second, slope, tokens)
    a_in = shift(late[1], "c", 1)
    x_steps = [ring_chain("x", True), ring_chain("x", False)]
    y_steps = [ring_chain("y", True), ring_chain("y", False)]
    early = add(after(early[0], late[1]), early_in).reshape(2, 2, 2, -1, width)
    early = [early[:, :, 0], early[:, :, 1]]
    early_sent = [outgoing(x, steps[0]) for x, steps in zip(early, x_steps)]
    early_in = [sent_along(x, steps[0]) for x, steps in zip(early_sent, x_steps)]
    a = by_ring(add(after(late[0], *early_sent), a_in))
    a_sent = outgoing(a, y_steps[0][0])
    a_in = sent_along(a_sent, y_steps[0][0])
    late = late_grads(at, 1, after(resid_grad, a_sent), second, slope, tokens)
    b_in = shift(after(late[1], a_in, *early_in), "c", 1)
    a = kept_plus(a, a_in, y_steps[0][0])
    a_sent = outgoing(a, y_steps[0][1])
    a_in = sent_along(a_sent, y_steps[0][1])
    b = by_ring(add(after(late[0], a_sent), b_in))
    b_sent = outgoing(b, y_steps[1][0])
    b_in = sent_along(b_sent, y_steps[1][0])
    early = [
        kept_plus(x, after(v, b_sent), steps[0]) for x, v, steps in zip(early, early_in, x_steps)
    ]
    early_sent = [outgoing(x, steps[1]) for x, steps in zip(early, x_steps)]
    early_in = [sent_along(x, steps[1]) for x, steps in zip(early_sent, x_steps)]
    b = kept_plus(b, after(b_in, *early_sent), y_steps[1][0])
    b_sent = outgoing(b, y_steps[1][1])
    b_in = sent_along(b_sent, y_steps[1][1])
    early = [
        kept_plus(x, after(v, b_sent), steps[1]) for x, v, steps in zip(early, early_in, x_steps)
    ]
    early = jnp.concatenate(early).reshape(16, -1, width)
    a = kept_plus(a, after(a_in, early), y_steps[0][1])
    b = kept_plus(b, b_in, y_steps[1][1])
    early = lax.all_to_all(early, ("z", "y"), 0, 0, tiled=True)
    late = lax.all_to_all(jnp.concatenate([a, b], 1), ("x", "z"), 0, 0, tiled=True)
    early = jnp.sum(early.astype(F32), 0)
    late = jnp.sum(late.astype(F32), 0)
    n_second = shard * RING // 128
    ride = jnp.sum(early[n_second : n_second + 8, out_width:], 1)
    score_total = ride[0] + ride[1] + ride[2]
    valid_total = jnp.maximum(ride[3], 1.0)
    scale = 1.0 / valid_total
    n_first = late.shape[0] // 2
    return (
        jnp.concatenate([late[:n_first], late[n_first:]], 1) * scale,
        early[:n_second] * scale,
        early[n_second:, :out_width] * scale,
        score_total / valid_total,
    )


def solution(mesh):
    grid = Mesh(mesh.devices.reshape(4, 4, 2, 4), ("x", "z", "c", "y"))
    rows = P(("y", "x", "z", "c"))
    shares = P(("x", "z", "c", "y"), None)
    return jax.shard_map(
        per_device,
        mesh=grid,
        in_specs=(
            P(("x", "z", "c"), "y", None),
            P(None, "y"),
            P("y", None),
            P(None, "y"),
            rows,
            rows,
            rows,
        ),
        out_specs=(shares, shares, shares, P()),
        check_vma=False,
    )
```

```python
import functools

import jax
import jax.numpy as jnp
from jax import lax
from jax.experimental import pallas as pl
from jax.experimental.pallas import tpu as pltpu
from jax.sharding import Mesh
from jax.sharding import PartitionSpec as P

SMOOTHING = 1.0
LOSS_SCALE = 4096.0
RING = 4
PAIR_LOW = ((0, 1), (1, 0), (2, 3), (3, 2))
PAIR_HIGH = ((0, 3), (3, 0), (1, 2), (2, 1))
ROOT_2_PI = 0.7978845608028654
CUBIC = 0.044715
LANES = 256
MIB = 1 << 20
F32 = jnp.float32
BF16 = jnp.bfloat16


def shift(x, axis, by):
    size = lax.axis_size(axis)
    return lax.ppermute(x, axis, [(i, (i + by) % size) for i in range(size)])


def dot(a, b, contract=((1,), (0,))):
    return lax.dot_general(a, b, (contract, ((), ())), preferred_element_type=F32)


def params(mib):
    return pltpu.CompilerParams(dimension_semantics=("arbitrary",), vmem_limit_bytes=mib * MIB)


def forward_kernel(first_call, last_call, block_rows, sizes, *refs):
    width, half, head_rows = sizes
    place, tokens, mine, theirs = refs[:4]
    refs = refs[4:]
    if first_call:
        total_in = None
        slope, hidden, second, head, total = refs
    elif last_call:
        total_in, _, _, _, head_in, slope, hidden, second, head, residual, forecast = refs
    else:
        total_in, _, _, _, _, slope, hidden, second, head, total = refs
    block, core = place[0], place[1]
    chunks = width // LANES
    start = width
    head_start = start + chunks * half

    @pl.when(pl.program_id(0) == 0)
    def _():
        if last_call:
            head[...] = head_in[...]
        for pack, side in ((mine, core), (theirs, 1 - core)):
            below = pl.multiple_of(side * half, half)
            for q in range(chunks):
                second[pl.ds(below, half), q * LANES : (q + 1) * LANES] = pack[
                    start + q * half : start + (q + 1) * half, :
                ]
            for e in range(2):
                piece = pack[head_start + e * head_rows : head_start + (e + 1) * head_rows, :]
                lane = pl.multiple_of(side * (width // 2) + e * LANES, LANES)
                row = pl.multiple_of(block * head_rows, 64) if last_call else 0
                head[pl.ds(row, head_rows), pl.ds(lane, LANES)] = piece

    rows = tokens[...]
    base = rows.astype(F32) if first_call else total_in[...]
    sums = [base[:, q * LANES : (q + 1) * LANES] for q in range(chunks)]
    for pack, side in ((mine, core), (theirs, 1 - core)):
        x = dot(rows, pack[:width, :])
        sq = x * x
        t = jnp.tanh(ROOT_2_PI * (x + CUBIC * x * sq))
        up = 0.5 * (1.0 + t)
        active = (x * up).astype(BF16)
        lane = pl.multiple_of(side * half, half)
        slope[:, pl.ds(lane, half)] = up + (0.5 * ROOT_2_PI) * x * (1.0 - t * t) * (
            1.0 + (3.0 * CUBIC) * sq
        )
        hidden[:, pl.ds(lane, half)] = active
        for q in range(chunks):
            sums[q] = sums[q] + dot(active, pack[start + q * half : start + (q + 1) * half, :])
    full = jnp.concatenate(sums, 1)
    if last_call:
        rounded = full.astype(BF16)
        residual[...] = rounded
        forecast[...] = dot(rounded, head[...], ((1,), (1,))).astype(BF16)
    else:
        total[...] = full


def forward_part(place, tokens, mine, theirs, carried, out_width, last_call):
    rows, width = tokens.shape
    half = LANES
    hid = 2 * half * RING
    head_rows = out_width // RING
    first_call = carried is None
    block_rows = min(rows, 256)
    whole = lambda shape: pl.BlockSpec(
        shape, lambda i, s: (0,) * len(shape), pipeline_mode=pl.Buffered(1)
    )
    by_rows = lambda cols: pl.BlockSpec((block_rows, cols), lambda i, s: (i, 0))
    in_place = pl.BlockSpec(memory_space=pl.ANY)
    in_specs = [by_rows(width), whole(mine.shape), whole(theirs.shape)]
    args = [tokens, mine, theirs]
    aliases = {}
    if not first_call:
        slope, hidden, second, head, total = carried
        args += [total, slope, hidden, second, head]
        in_specs += [by_rows(width), in_place, in_place, in_place]
        in_specs += [whole((out_width, width)) if last_call else in_place]
        aliases = {5: 0, 6: 1, 7: 2}
        if not last_call:
            aliases = {**aliases, 8: 3, 4: 4}
    column = pl.BlockSpec((block_rows, 2 * half), lambda i, s: (i, s[0]))
    out_specs = [
        column,
        column,
        pl.BlockSpec((2 * half, width), lambda i, s: (s[0], 0)),
        whole((out_width, width))
        if last_call
        else pl.BlockSpec((head_rows, width), lambda i, s: (s[0], 0)),
    ]
    out_shape = [
        jax.ShapeDtypeStruct((rows, hid), F32),
        jax.ShapeDtypeStruct((rows, hid), BF16),
        jax.ShapeDtypeStruct((hid, width), BF16),
        jax.ShapeDtypeStruct((out_width, width), BF16),
    ]
    if last_call:
        out_specs += [by_rows(width), by_rows(out_width)]
        out_shape += [
            jax.ShapeDtypeStruct((rows, width), BF16),
            jax.ShapeDtypeStruct((rows, out_width), BF16),
        ]
    else:
        out_specs += [by_rows(width)]
        out_shape += [jax.ShapeDtypeStruct((rows, width), F32)]
    return pl.pallas_call(
        functools.partial(
            forward_kernel, first_call, last_call, block_rows, (width, half, head_rows)
        ),
        grid_spec=pltpu.PrefetchScalarGridSpec(
            num_scalar_prefetch=1,
            grid=(rows // block_rows,),
            in_specs=in_specs,
            out_specs=out_specs,
        ),
        out_shape=out_shape,
        input_output_aliases=aliases,
        compiler_params=params(24),
        cost_estimate=pl.CostEstimate(
            flops=8 * rows * width * half, bytes_accessed=12 * MIB, transcendentals=rows * 2 * half
        ),
        name="forward_part",
    )(place, *args)


def once(shape):
    return pl.BlockSpec(shape, lambda i, s: (0, 0), pipeline_mode=pl.Buffered(1))


def store_halves(core, parts, keep, send):
    n, _, rows, cols = parts.shape
    zero = parts[:, 0].reshape(n * rows, cols).astype(BF16)
    one = parts[:, 1].reshape(n * rows, cols).astype(BF16)

    @pl.when(core == 0)
    def _():
        keep[0] = zero
        send[0] = one

    @pl.when(core == 1)
    def _():
        keep[0] = one
        send[0] = zero


def riders(place, scalars, shape):
    line = lax.broadcasted_iota(jnp.int32, shape, 0)
    lane = lax.broadcasted_iota(jnp.int32, shape, 1)
    score = jnp.full(shape, scalars[0], F32)
    out = jnp.where(line == 3, scalars[1], 0.0)
    for i in range(3):
        term = score.astype(BF16).astype(F32)
        out = jnp.where(line == i, term, out)
        score = score - term
    return jnp.where(lane == 2 * place[2] + place[1], out, 0.0)


def early_kernel(place, hidden, resid_grad, residual, grad_rows, scalars, keep, send):
    second = dot(hidden[...], resid_grad[...], ((0,), (0,)))
    head = dot(residual[...], grad_rows[...], ((0,), (0,)))
    width, out_width = second.shape[1], head.shape[1]
    second = second.reshape(RING, 2, RING, -1, width)
    head = head.reshape(RING, 2, RING, -1, out_width)
    blank = riders(place, scalars, (head.shape[3], width - out_width))
    blank = jnp.broadcast_to(blank, (*head.shape[:3], *blank.shape))
    both = jnp.concatenate([second, jnp.concatenate([head, blank], 4)], 3)
    both = both.reshape(RING, 2, -1, width)
    store_halves(place[1], both, keep, send)


def early_grads(place, hidden, resid_grad, residual, grad_rows, scalars):
    rows, hid = hidden.shape
    width, out_width = residual.shape[1], grad_rows.shape[1]
    lines = (hid + width) // RING // 2
    gray = lambda i: 2 * ((i // 2 + i) % 2) + i // 2
    out = pl.BlockSpec((1, lines, width), lambda i, s: (gray(i), 0, 0))
    return pl.pallas_call(
        early_kernel,
        grid_spec=pltpu.PrefetchScalarGridSpec(
            num_scalar_prefetch=1,
            grid=(RING,),
            in_specs=[
                pl.BlockSpec((rows, hid // RING), lambda i, s: (0, i)),
                once((rows, width)),
                pl.BlockSpec((rows, width // RING), lambda i, s: (0, i)),
                once((rows, out_width)),
                pl.BlockSpec(memory_space=pltpu.SMEM),
            ],
            out_specs=[out, out],
        ),
        out_shape=[jax.ShapeDtypeStruct((RING, lines, width), BF16)] * 2,
        compiler_params=params(32),
        cost_estimate=pl.CostEstimate(
            flops=2 * rows * width * (hid + out_width), bytes_accessed=18 * MIB, transcendentals=0
        ),
        name="early_grads",
    )(place, hidden, resid_grad, residual, grad_rows, scalars)


def late_kernel(place, resid_grad, second, slope, tokens, keep, send):
    hidden_grad = dot(resid_grad[...], second[...], ((1,), (1,)))
    preact_grad = (slope[...] * hidden_grad).astype(BF16)
    first = dot(tokens[...], preact_grad, ((0,), (0,)))
    cols = first.shape[1]
    parts = first.reshape(16, 2, RING, -1, cols)
    parts = jnp.stack([parts[:, :, i] for i in (0, 3, 1, 2)], 2)
    store_halves(place[1], parts.reshape(16, 2, -1, cols), keep, send)


def late_grads(place, part, resid_grad, second, slope, tokens):
    rows, width = resid_grad.shape
    tile = 2 * LANES
    steps = width // tile
    out = pl.BlockSpec((1, width // 2, tile), lambda j, s: (0, 0, j))
    return pl.pallas_call(
        late_kernel,
        grid_spec=pltpu.PrefetchScalarGridSpec(
            num_scalar_prefetch=1,
            grid=(steps,),
            in_specs=[
                once((rows, width)),
                pl.BlockSpec((tile, width), lambda j, s: (part * steps + j, 0)),
                pl.BlockSpec((rows, tile), lambda j, s: (0, part * steps + j)),
                once((rows, width)),
            ],
            out_specs=[out, out],
        ),
        out_shape=[jax.ShapeDtypeStruct((1, width // 2, width), BF16)] * 2,
        compiler_params=params(28),
        cost_estimate=pl.CostEstimate(
            flops=4 * rows * width * width, bytes_accessed=12 * MIB, transcendentals=0
        ),
        name="late_grads",
    )(place, resid_grad, second, slope, tokens)


def add(a, b):
    return (a.astype(F32) + b.astype(F32)).astype(BF16)


def take(x, index, axis):
    return lax.dynamic_index_in_dim(x, index, axis, keepdims=False)


def ring_bits(axis):
    here = lax.axis_index(axis)
    high = here // 2
    return (high + here) % 2, high


def ring_chain(axis, low_first):
    low, high = ring_bits(axis)
    if low_first:
        steps = ((PAIR_LOW, low, 0), (PAIR_HIGH, high, 0))
    else:
        steps = ((PAIR_HIGH, high, 1), (PAIR_LOW, low, 0))
    return [(pairs, axis, bit, dim) for pairs, bit, dim in steps]


def outgoing(x, step):
    _, _, bit, dim = step
    return take(x, 1 - bit, dim)


def sent_along(x, step):
    return lax.ppermute(x, step[1], step[0])


def kept_plus(x, arrived, step):
    _, _, bit, dim = step
    return add(take(x, bit, dim), arrived)


def by_ring(x):
    return x.reshape(16, 2, 2, -1, x.shape[-1]).transpose(1, 2, 0, 3, 4)


def tie(*arrays):
    return lax.optimization_barrier(arrays)


def after(x, *others):
    return lax.optimization_barrier((x, *others))[0]


def pack_kernel(side, first, second, head, out):
    width, half = first.shape
    out[:width, :] = first[...]
    at = width
    for q in range(second.shape[1] // LANES):
        out[at : at + half, :] = second[:, q * LANES : (q + 1) * LANES]
        at += half
    for e in range(head.shape[1] // LANES):
        out[at : at + head.shape[0], :] = head[:, e * LANES : (e + 1) * LANES]
        at += head.shape[0]


def packed(side, first, second, head):
    width, shard = first.shape
    half = shard // 2
    lines = width + half * width // LANES + head.shape[0] * width // 2 // LANES
    return pl.pallas_call(
        pack_kernel,
        grid_spec=pltpu.PrefetchScalarGridSpec(
            num_scalar_prefetch=1,
            grid=(1,),
            in_specs=[
                pl.BlockSpec((width, half), lambda i, s: (0, s[0])),
                pl.BlockSpec((half, width), lambda i, s: (s[0], 0)),
                pl.BlockSpec((head.shape[0], width // 2), lambda i, s: (0, s[0])),
            ],
            out_specs=pl.BlockSpec((lines, LANES), lambda i, s: (0, 0)),
        ),
        out_shape=jax.ShapeDtypeStruct((lines, LANES), BF16),
        compiler_params=params(8),
        name="packed",
    )(side, first, second, head)


def score(samples, target, valid_mask):
    count = samples.shape[0]
    wide = samples.astype(F32)
    gram = jnp.einsum("mpo,npo->pmn", samples, samples, preferred_element_type=F32)
    squares = jnp.sum(wide * wide, axis=2).T
    dist_sq = squares[:, :, None] + squares[:, None, :] - 2.0 * gram
    spread = jnp.sqrt(dist_sq + SMOOTHING)
    kernel = 1.0 / spread
    kernel_sum = jnp.sum(kernel, axis=2)
    pulled = jnp.einsum("pmn,npo->mpo", kernel, wide, precision=lax.Precision.HIGHEST)
    offset = wide - target[None]
    error_norm = jnp.sqrt(jnp.sum(offset * offset, axis=2) + SMOOTHING)
    repulse = wide * kernel_sum.T[:, :, None] - pulled
    validity = valid_mask.astype(F32)
    grad_raw = (
        LOSS_SCALE
        * validity[None, :, None]
        * (offset / (count * error_norm[:, :, None]) - repulse / (count * count))
    ).astype(BF16)
    scores = validity * (
        jnp.mean(error_norm, axis=0) - jnp.sum(spread, axis=(1, 2)) / (2.0 * count * count)
    )
    return grad_raw, jnp.sum(scores), jnp.sum(validity)


def per_device(latents, w_first, w_second, readout_matrix, observed, obs_index, valid_mask):
    members, patches, width = latents.shape
    out_width = observed.shape[1]
    core = lax.axis_index("c")
    here = lax.axis_index("y")
    own = obs_index.shape[0]
    rows = members * patches
    shard = w_first.shape[1]
    half = shard // 2

    side = jnp.reshape(core, (1,)).astype(jnp.int32)
    turned = readout_matrix.T
    mine = packed(side, w_first, w_second, turned)
    right = shift(mine, "y", 1)
    left = shift(mine, "y", -1)
    lines = mine.shape[0] // 2
    latents, other_side, mine = tie(latents, 1 - side, mine)
    tokens = (
        latents.reshape(members, 32, own, width).transpose(1, 0, 2, 3).reshape(rows, width)
    )
    theirs = packed(other_side, w_first, w_second, turned)
    place = lambda off: jnp.stack([(here + off) % RING, core, lax.axis_index("x")]).astype(jnp.int32)
    run = functools.partial(forward_part, out_width=out_width)
    carried = run(place(0), tokens, mine, theirs, carried=None, last_call=False)
    right, left, *carried = tie(right, left, *carried)
    far = [right[:lines], left[lines:]]
    right_other = shift(after(right, *far), "c", 1)
    left_other = shift(after(left, *far), "c", 1)
    far = [shift(far[0], "y", 1), shift(far[1], "y", -1)]
    carried = run(place(3), tokens, right, right_other, carried=carried, last_call=False)
    carried = run(place(1), tokens, left, left_other, carried=carried, last_call=False)
    near, past, *carried = tie(*far, *carried)
    far = jnp.concatenate([near, past], 0)
    far_other = shift(far, "c", 1)
    slope, hidden, second, head, residual, forecast = run(
        place(2), tokens, far, far_other, carried=carried, last_call=True
    )

    group = ("x", "z", "c")
    device = ((here * 4 + lax.axis_index("x")) * 4 + lax.axis_index("z")) * 2 + core
    target = jnp.take(observed, obs_index - device * own, axis=0)
    forecast, target = tie(forecast.reshape(32, members * own, out_width), target)
    gathered = lax.all_to_all(forecast, group, 0, 0, tiled=True)
    samples = gathered.reshape(32 * members, own, out_width)
    grad_raw, score_part, count_part = score(samples, target, valid_mask)
    grad_rows = lax.all_to_all(
        grad_raw.reshape(32, members * own, out_width), group, 0, 0, tiled=True
    ).reshape(rows, out_width)

    at = place(0)
    scalars = jnp.stack([score_part, count_part])
    resid_grad = dot(grad_rows, head).astype(BF16)
    early = early_grads(at, hidden, resid_grad, residual, grad_rows, scalars)
    early_in = shift(early[1], "c", 1)
    late = late_grads(at, 0, after(resid_grad, early[1]), second, slope, tokens)
    a_in = shift(late[1], "c", 1)
    x_steps = [ring_chain("x", True), ring_chain("x", False)]
    y_steps = [ring_chain("y", True), ring_chain("y", False)]
    early = add(after(early[0], late[1]), early_in).reshape(2, 2, 2, -1, width)
    early = [early[:, :, 0], early[:, :, 1]]
    early_sent = [outgoing(x, steps[0]) for x, steps in zip(early, x_steps)]
    early_in = [sent_along(x, steps[0]) for x, steps in zip(early_sent, x_steps)]
    a = by_ring(add(after(late[0], *early_sent), a_in))
    a_sent = outgoing(a, y_steps[0][0])
    a_in = sent_along(a_sent, y_steps[0][0])
    late = late_grads(at, 1, after(resid_grad, a_sent), second, slope, tokens)
    b_in = shift(after(late[1], a_in, *early_in), "c", 1)
    a = kept_plus(a, a_in, y_steps[0][0])
    a_sent = outgoing(a, y_steps[0][1])
    a_in = sent_along(a_sent, y_steps[0][1])
    b = by_ring(add(after(late[0], a_sent), b_in))
    b_sent = outgoing(b, y_steps[1][0])
    b_in = sent_along(b_sent, y_steps[1][0])
    early = [
        kept_plus(x, after(v, b_sent), steps[0]) for x, v, steps in zip(early, early_in, x_steps)
    ]
    early_sent = [outgoing(x, steps[1]) for x, steps in zip(early, x_steps)]
    early_in = [sent_along(x, steps[1]) for x, steps in zip(early_sent, x_steps)]
    b = kept_plus(b, after(b_in, *early_sent), y_steps[1][0])
    b_sent = outgoing(b, y_steps[1][1])
    b_in = sent_along(b_sent, y_steps[1][1])
    early = [
        kept_plus(x, after(v, b_sent), steps[1]) for x, v, steps in zip(early, early_in, x_steps)
    ]
    early = jnp.concatenate(early).reshape(16, -1, width)
    a = kept_plus(a, after(a_in, early), y_steps[0][1])
    b = kept_plus(b, b_in, y_steps[1][1])
    early = lax.all_to_all(early, ("z", "y"), 0, 0, tiled=True)
    late = lax.all_to_all(jnp.concatenate([a, b], 1), ("x", "z"), 0, 0, tiled=True)
    early = jnp.sum(early.astype(F32), 0)
    late = jnp.sum(late.astype(F32), 0)
    n_second = shard * RING // 128
    ride = jnp.sum(early[n_second : n_second + 8, out_width:], 1)
    score_total = ride[0] + ride[1] + ride[2]
    valid_total = jnp.maximum(ride[3], 1.0)
    scale = 1.0 / valid_total
    n_first = late.shape[0] // 2
    return (
        jnp.concatenate([late[:n_first], late[n_first:]], 1) * scale,
        early[:n_second] * scale,
        early[n_second:, :out_width] * scale,
        score_total / valid_total,
    )


def solution(mesh):
    grid = Mesh(mesh.devices.reshape(4, 4, 2, 4), ("x", "z", "c", "y"))
    rows = P(("y", "x", "z", "c"))
    shares = P(("x", "z", "c", "y"), None)
    return jax.shard_map(
        per_device,
        mesh=grid,
        in_specs=(
            P(("x", "z", "c"), "y", None),
            P(None, "y"),
            P("y", None),
            P(None, "y"),
            rows,
            rows,
            rows,
        ),
        out_specs=(shares, shares, shares, P()),
        check_vma=False,
    )
```

```python
import functools

import jax
import jax.numpy as jnp
from jax import lax
from jax.experimental import pallas as pl
from jax.experimental.pallas import tpu as pltpu
from jax.sharding import Mesh
from jax.sharding import PartitionSpec as P

SMOOTHING = 1.0
LOSS_SCALE = 4096.0
RING = 4
PAIR_LOW = ((0, 1), (1, 0), (2, 3), (3, 2))
PAIR_HIGH = ((0, 3), (3, 0), (1, 2), (2, 1))
ROOT_2_PI = 0.7978845608028654
CUBIC = 0.044715
LANES = 256
MIB = 1 << 20
F32 = jnp.float32
BF16 = jnp.bfloat16


def shift(x, axis, by):
    size = lax.axis_size(axis)
    return lax.ppermute(x, axis, [(i, (i + by) % size) for i in range(size)])


def dot(a, b, contract=((1,), (0,))):
    return lax.dot_general(a, b, (contract, ((), ())), preferred_element_type=F32)


def in_hbm(x):
    return pltpu.with_memory_space_constraint(x, pltpu.HBM)


def params(mib):
    return pltpu.CompilerParams(dimension_semantics=("arbitrary",), vmem_limit_bytes=mib * MIB)


def forward_kernel(first_call, last_call, block_rows, sizes, *refs):
    width, half, head_rows = sizes
    place, tokens, mine, theirs = refs[:4]
    refs = refs[4:]
    if first_call:
        total_in = None
        slope, hidden, second, head, total = refs
    elif last_call:
        total_in, _, _, _, head_in, slope, hidden, second, head, residual, forecast = refs
    else:
        total_in, _, _, _, _, slope, hidden, second, head, total = refs
    block, core = place[0], place[1]
    chunks = width // LANES
    start = width
    head_start = start + chunks * half

    @pl.when(pl.program_id(0) == 0)
    def _():
        if last_call:
            head[...] = head_in[...]
        for pack, side in ((mine, core), (theirs, 1 - core)):
            below = pl.multiple_of(side * half, half)
            for q in range(chunks):
                second[pl.ds(below, half), q * LANES : (q + 1) * LANES] = pack[
                    start + q * half : start + (q + 1) * half, :
                ]
            for e in range(2):
                piece = pack[head_start + e * head_rows : head_start + (e + 1) * head_rows, :]
                lane = pl.multiple_of(side * (width // 2) + e * LANES, LANES)
                row = pl.multiple_of(block * head_rows, 64) if last_call else 0
                head[pl.ds(row, head_rows), pl.ds(lane, LANES)] = piece

    rows = tokens[...]
    base = rows.astype(F32) if first_call else total_in[...]
    sums = [base[:, q * LANES : (q + 1) * LANES] for q in range(chunks)]
    for pack, side in ((mine, core), (theirs, 1 - core)):
        x = dot(rows, pack[:width, :])
        sq = x * x
        t = jnp.tanh(ROOT_2_PI * (x + CUBIC * x * sq))
        up = 0.5 * (1.0 + t)
        active = (x * up).astype(BF16)
        lane = pl.multiple_of(side * half, half)
        slope[:, pl.ds(lane, half)] = up + (0.5 * ROOT_2_PI) * x * (1.0 - t * t) * (
            1.0 + (3.0 * CUBIC) * sq
        )
        hidden[:, pl.ds(lane, half)] = active
        for q in range(chunks):
            sums[q] = sums[q] + dot(active, pack[start + q * half : start + (q + 1) * half, :])
    full = jnp.concatenate(sums, 1)
    if last_call:
        rounded = full.astype(BF16)
        residual[...] = rounded
        forecast[...] = dot(rounded, head[...], ((1,), (1,))).astype(BF16)
    else:
        total[...] = full


def forward_part(place, tokens, mine, theirs, carried, out_width, last_call):
    rows, width = tokens.shape
    half = LANES
    hid = 2 * half * RING
    head_rows = out_width // RING
    first_call = carried is None
    block_rows = min(rows, 256)
    whole = lambda shape: pl.BlockSpec(
        shape, lambda i, s: (0,) * len(shape), pipeline_mode=pl.Buffered(1)
    )
    by_rows = lambda cols: pl.BlockSpec((block_rows, cols), lambda i, s: (i, 0))
    in_place = pl.BlockSpec(memory_space=pltpu.HBM)
    in_specs = [by_rows(width), whole(mine.shape), whole(theirs.shape)]
    args = [tokens, mine, theirs]
    aliases = {}
    if not first_call:
        slope, hidden, second, head, total = carried
        args += [total, in_hbm(slope), in_hbm(hidden), in_hbm(second)]
        args += [head if last_call else in_hbm(head)]
        in_specs += [by_rows(width), in_place, in_place, in_place]
        in_specs += [whole((out_width, width)) if last_call else in_place]
        aliases = {5: 0, 6: 1, 7: 2}
        if not last_call:
            aliases = {**aliases, 8: 3, 4: 4}
    column = pl.BlockSpec((block_rows, 2 * half), lambda i, s: (i, s[0]))
    out_specs = [
        column,
        column,
        pl.BlockSpec((2 * half, width), lambda i, s: (s[0], 0)),
        whole((out_width, width))
        if last_call
        else pl.BlockSpec((head_rows, width), lambda i, s: (s[0], 0)),
    ]
    out_shape = [
        jax.ShapeDtypeStruct((rows, hid), F32),
        jax.ShapeDtypeStruct((rows, hid), BF16),
        jax.ShapeDtypeStruct((hid, width), BF16),
        jax.ShapeDtypeStruct((out_width, width), BF16),
    ]
    if last_call:
        out_specs += [by_rows(width), by_rows(out_width)]
        out_shape += [
            jax.ShapeDtypeStruct((rows, width), BF16),
            jax.ShapeDtypeStruct((rows, out_width), BF16),
        ]
    else:
        out_specs += [by_rows(width)]
        out_shape += [jax.ShapeDtypeStruct((rows, width), F32)]
    return pl.pallas_call(
        functools.partial(
            forward_kernel, first_call, last_call, block_rows, (width, half, head_rows)
        ),
        grid_spec=pltpu.PrefetchScalarGridSpec(
            num_scalar_prefetch=1,
            grid=(rows // block_rows,),
            in_specs=in_specs,
            out_specs=out_specs,
        ),
        out_shape=out_shape,
        input_output_aliases=aliases,
        compiler_params=params(24),
        cost_estimate=pl.CostEstimate(
            flops=8 * rows * width * half, bytes_accessed=12 * MIB, transcendentals=rows * 2 * half
        ),
        name="forward_part",
    )(place, *args)


def once(shape):
    return pl.BlockSpec(shape, lambda i, s: (0, 0), pipeline_mode=pl.Buffered(1))


def store_halves(core, parts, keep, send):
    n, _, rows, cols = parts.shape
    zero = parts[:, 0].reshape(n * rows, cols).astype(BF16)
    one = parts[:, 1].reshape(n * rows, cols).astype(BF16)

    @pl.when(core == 0)
    def _():
        keep[0] = zero
        send[0] = one

    @pl.when(core == 1)
    def _():
        keep[0] = one
        send[0] = zero


def riders(place, scalars, shape):
    line = lax.broadcasted_iota(jnp.int32, shape, 0)
    lane = lax.broadcasted_iota(jnp.int32, shape, 1)
    score = jnp.full(shape, scalars[0], F32)
    out = jnp.where(line == 3, scalars[1], 0.0)
    for i in range(3):
        term = score.astype(BF16).astype(F32)
        out = jnp.where(line == i, term, out)
        score = score - term
    return jnp.where(lane == 2 * place[0] + place[1], out, 0.0)


def early_kernel(place, hidden, resid_grad, keep, send):
    second = dot(hidden[...], resid_grad[...], ((0,), (0,)))
    store_halves(place[1], second.reshape(RING, 2, -1, second.shape[1]), keep, send)


def early_grads(place, hidden, resid_grad):
    rows, hid = hidden.shape
    width = resid_grad.shape[1]
    lines = hid // RING // 2
    gray = lambda i: 2 * ((i // 2 + i) % 2) + i // 2
    out = pl.BlockSpec((1, lines, width), lambda i, s: (gray(i), 0, 0))
    return pl.pallas_call(
        early_kernel,
        grid_spec=pltpu.PrefetchScalarGridSpec(
            num_scalar_prefetch=1,
            grid=(RING,),
            in_specs=[
                pl.BlockSpec((rows, hid // RING), lambda i, s: (0, i)),
                once((rows, width)),
            ],
            out_specs=[out, out],
        ),
        out_shape=[jax.ShapeDtypeStruct((RING, lines, width), BF16)] * 2,
        compiler_params=params(28),
        cost_estimate=pl.CostEstimate(
            flops=2 * rows * width * hid, bytes_accessed=12 * MIB, transcendentals=0
        ),
        name="early_grads",
    )(place, in_hbm(hidden), resid_grad)


def late_kernel(steps, place, resid_grad, second, slope, tokens, *refs):
    keep, send = refs[-2:]
    hidden_grad = dot(resid_grad[...], second[...], ((1,), (1,)))
    preact_grad = (slope[...] * hidden_grad).astype(BF16)
    first = dot(tokens[...], preact_grad, ((0,), (0,)))
    cols = first.shape[1]

    def store(*grads):
        parts = jnp.concatenate([g.reshape(16, 2, RING, -1, cols) for g in grads], 3)
        parts = jnp.stack([parts[:, :, i] for i in (0, 3, 1, 2)], 2)
        store_halves(place[1], parts.reshape(16, 2, -1, cols), keep, send)

    if len(refs) == 2:
        store(first)
        return
    residual, grad_rows, scalars = refs[:3]
    width, out_width = residual.shape[1], grad_rows.shape[1]
    for j in range(steps):

        @pl.when(pl.program_id(0) == j)
        def _(j=j):
            head = dot(residual[...], grad_rows[:, j * cols : (j + 1) * cols], ((0,), (0,)))
            if j == steps - 1:
                blank = riders(place, scalars, (8, width - out_width))
                blank = jnp.broadcast_to(blank, (width // 8, *blank.shape))
                head = jnp.concatenate([head, blank.reshape(width, -1)], 1)
            store(first, head)


def late_grads(place, part, resid_grad, second, slope, tokens, *head):
    rows, width = resid_grad.shape
    tile = 2 * LANES
    steps = width // tile
    lines = width if head else width // 2
    out = pl.BlockSpec((1, lines, tile), lambda j, s: (0, 0, j))
    specs = []
    if head:
        specs = [once(head[0].shape), once(head[1].shape), pl.BlockSpec(memory_space=pltpu.SMEM)]
    return pl.pallas_call(
        functools.partial(late_kernel, steps),
        grid_spec=pltpu.PrefetchScalarGridSpec(
            num_scalar_prefetch=1,
            grid=(steps,),
            in_specs=[
                once((rows, width)),
                pl.BlockSpec((tile, width), lambda j, s: (part * steps + j, 0)),
                pl.BlockSpec((rows, tile), lambda j, s: (0, part * steps + j)),
                once((rows, width)),
                *specs,
            ],
            out_specs=[out, out],
        ),
        out_shape=[jax.ShapeDtypeStruct((1, lines, width), BF16)] * 2,
        compiler_params=params(36 if head else 28),
        cost_estimate=pl.CostEstimate(
            flops=4 * rows * width * width, bytes_accessed=12 * MIB, transcendentals=0
        ),
        name="late_grads",
    )(place, resid_grad, in_hbm(second), in_hbm(slope), tokens, *head)


def add(a, b):
    return (a.astype(F32) + b.astype(F32)).astype(BF16)


def take(x, index, axis):
    return lax.dynamic_index_in_dim(x, index, axis, keepdims=False)


def ring_bits(axis):
    here = lax.axis_index(axis)
    high = here // 2
    return (high + here) % 2, high


def ring_chain(axis, low_first):
    low, high = ring_bits(axis)
    if low_first:
        steps = ((PAIR_LOW, low, 0), (PAIR_HIGH, high, 0))
    else:
        steps = ((PAIR_HIGH, high, 1), (PAIR_LOW, low, 0))
    return [(pairs, axis, bit, dim) for pairs, bit, dim in steps]


def outgoing(x, step):
    _, _, bit, dim = step
    return take(x, 1 - bit, dim)


def sent_along(x, step):
    return lax.ppermute(x, step[1], step[0])


def kept_plus(x, arrived, step):
    _, _, bit, dim = step
    return add(take(x, bit, dim), arrived)


def by_ring(x):
    return x.reshape(16, 2, 2, -1, x.shape[-1]).transpose(1, 2, 0, 3, 4)


def tie(*arrays):
    return lax.optimization_barrier(arrays)


def after(x, *others):
    return lax.optimization_barrier((x, *others))[0]


def pack_kernel(side, first, second, head, out):
    width, half = first.shape
    out[:width, :] = first[...]
    at = width
    for q in range(second.shape[1] // LANES):
        out[at : at + half, :] = second[:, q * LANES : (q + 1) * LANES]
        at += half
    for e in range(head.shape[1] // LANES):
        out[at : at + head.shape[0], :] = head[:, e * LANES : (e + 1) * LANES]
        at += head.shape[0]


def packed(side, first, second, head):
    width, shard = first.shape
    half = shard // 2
    lines = width + half * width // LANES + head.shape[0] * width // 2 // LANES
    return pl.pallas_call(
        pack_kernel,
        grid_spec=pltpu.PrefetchScalarGridSpec(
            num_scalar_prefetch=1,
            grid=(1,),
            in_specs=[
                pl.BlockSpec((width, half), lambda i, s: (0, s[0])),
                pl.BlockSpec((half, width), lambda i, s: (s[0], 0)),
                pl.BlockSpec((head.shape[0], width // 2), lambda i, s: (0, s[0])),
            ],
            out_specs=pl.BlockSpec((lines, LANES), lambda i, s: (0, 0)),
        ),
        out_shape=jax.ShapeDtypeStruct((lines, LANES), BF16),
        compiler_params=params(8),
        name="packed",
    )(side, first, second, head)


def score(samples, target, valid_mask):
    count = samples.shape[0]
    wide = samples.astype(F32)
    gram = jnp.einsum("mpo,npo->pmn", samples, samples, preferred_element_type=F32)
    squares = jnp.sum(wide * wide, axis=2).T
    dist_sq = squares[:, :, None] + squares[:, None, :] - 2.0 * gram
    spread = jnp.sqrt(dist_sq + SMOOTHING)
    kernel = 1.0 / spread
    kernel_sum = jnp.sum(kernel, axis=2)
    pulled = jnp.einsum("pmn,npo->mpo", kernel, wide, precision=lax.Precision.HIGHEST)
    offset = wide - target[None]
    error_norm = jnp.sqrt(jnp.sum(offset * offset, axis=2) + SMOOTHING)
    repulse = wide * kernel_sum.T[:, :, None] - pulled
    validity = valid_mask.astype(F32)
    grad_raw = (
        LOSS_SCALE
        * validity[None, :, None]
        * (offset / (count * error_norm[:, :, None]) - repulse / (count * count))
    ).astype(BF16)
    scores = validity * (
        jnp.mean(error_norm, axis=0) - jnp.sum(spread, axis=(1, 2)) / (2.0 * count * count)
    )
    return grad_raw, jnp.sum(scores), jnp.sum(validity)


def per_device(latents, w_first, w_second, readout_matrix, observed, obs_index, valid_mask):
    members, patches, width = latents.shape
    out_width = observed.shape[1]
    core = lax.axis_index("c")
    here = lax.axis_index("y")
    own = obs_index.shape[0]
    rows = members * patches
    shard = w_first.shape[1]
    half = shard // 2

    side = jnp.reshape(core, (1,)).astype(jnp.int32)
    turned = readout_matrix.T
    mine = packed(side, w_first, w_second, turned)
    right = shift(mine, "y", 1)
    left = shift(mine, "y", -1)
    lines = mine.shape[0] // 2
    latents, other_side, mine = tie(latents, 1 - side, mine)
    tokens = (
        latents.reshape(members, 32, own, width).transpose(1, 0, 2, 3).reshape(rows, width)
    )
    theirs = packed(other_side, w_first, w_second, turned)
    place = lambda off: jnp.stack([(here + off) % RING, core, lax.axis_index("x")]).astype(jnp.int32)
    run = functools.partial(forward_part, out_width=out_width)
    carried = run(place(0), tokens, mine, theirs, carried=None, last_call=False)
    right, left, *carried = tie(right, left, *carried)
    far = [right[:lines], left[lines:]]
    right_other = shift(after(right, *far), "c", 1)
    left_other = shift(after(left, *far), "c", 1)
    far = [shift(far[0], "y", 1), shift(far[1], "y", -1)]
    carried = run(place(3), tokens, right, right_other, carried=carried, last_call=False)
    carried = run(place(1), tokens, left, left_other, carried=carried, last_call=False)
    near, past, *carried = tie(*far, *carried)
    far = jnp.concatenate([near, past], 0)
    far_other = shift(far, "c", 1)
    slope, hidden, second, head, residual, forecast = run(
        place(2), tokens, far, far_other, carried=carried, last_call=True
    )

    group = ("x", "z", "c")
    device = ((here * 4 + lax.axis_index("x")) * 4 + lax.axis_index("z")) * 2 + core
    target = jnp.take(observed, obs_index - device * own, axis=0)
    forecast, target = tie(forecast.reshape(32, members * own, out_width), target)
    gathered = lax.all_to_all(forecast, group, 0, 0, tiled=True)
    samples = gathered.reshape(32 * members, own, out_width)
    grad_raw, score_part, count_part = score(samples, target, valid_mask)
    grad_rows = lax.all_to_all(
        grad_raw.reshape(32, members * own, out_width), group, 0, 0, tiled=True
    ).reshape(rows, out_width)

    at = place(0)
    scalars = jnp.stack([score_part, count_part])
    resid_grad = dot(grad_rows, head).astype(BF16)
    early = early_grads(at, hidden, resid_grad)
    early_in = shift(early[1], "c", 1)
    late = late_grads(
        at,
        0,
        after(resid_grad, early[1]),
        second,
        slope,
        tokens,
        residual,
        grad_rows,
        scalars,
    )
    a_in = shift(late[1], "c", 1)
    x_steps = [ring_chain("x", True), ring_chain("x", False)]
    y_steps = [ring_chain("y", True), ring_chain("y", False)]
    early = add(after(early[0], late[1]), early_in).reshape(2, 2, 2, -1, width)
    early = [early[:, :, 0], early[:, :, 1]]
    early_sent = [outgoing(x, steps[0]) for x, steps in zip(early, x_steps)]
    early_in = [sent_along(x, steps[0]) for x, steps in zip(early_sent, x_steps)]
    a = by_ring(add(after(late[0], *early_sent), a_in))
    a_sent = outgoing(a, y_steps[0][0])
    a_in = sent_along(a_sent, y_steps[0][0])
    late = late_grads(at, 1, after(resid_grad, a_sent), second, slope, tokens)
    b_in = shift(after(late[1], *early_in), "c", 1)
    early = [kept_plus(x, v, steps[0]) for x, v, steps in zip(early, early_in, x_steps)]
    early_sent = [outgoing(x, steps[1]) for x, steps in zip(early, x_steps)]
    early_in = [sent_along(x, steps[1]) for x, steps in zip(early_sent, x_steps)]
    b = by_ring(add(after(late[0], *early_sent), b_in))
    b_sent = outgoing(b, y_steps[1][0])
    b_in = sent_along(b_sent, y_steps[1][0])
    early = [
        kept_plus(x, after(v, b_sent), steps[1]) for x, v, steps in zip(early, early_in, x_steps)
    ]
    early = jnp.concatenate(early).reshape(16, -1, width)
    a = kept_plus(a, after(a_in, b_sent), y_steps[0][0])
    a_sent = outgoing(a, y_steps[0][1])
    a_in = sent_along(a_sent, y_steps[0][1])
    b = kept_plus(b, after(b_in, a_sent), y_steps[1][0])
    b_sent = outgoing(b, y_steps[1][1])
    b_in = sent_along(b_sent, y_steps[1][1])
    a = kept_plus(a, after(a_in, b_sent), y_steps[0][1])
    b = kept_plus(b, b_in, y_steps[1][1])
    early = lax.all_to_all(early, ("z", "y"), 0, 0, tiled=True)
    late = lax.all_to_all(jnp.concatenate([a, b], 1), ("x", "z"), 0, 0, tiled=True)
    early = jnp.sum(early.astype(F32), 0)
    late = jnp.sum(late.astype(F32), 0)
    n = width // 128
    ride = jnp.sum(late[n : 2 * n, out_width:], 1)
    score_total = ride[0] + ride[1] + ride[2]
    valid_total = jnp.maximum(ride[3], 1.0)
    scale = 1.0 / valid_total
    return (
        jnp.concatenate([late[:n], late[2 * n :]], 1) * scale,
        early * scale,
        late[n : 2 * n, :out_width] * scale,
        score_total / valid_total,
    )


def solution(mesh):
    grid = Mesh(mesh.devices.reshape(4, 4, 2, 4), ("x", "z", "c", "y"))
    rows = P(("y", "x", "z", "c"))
    shares = P(("x", "z", "c", "y"), None)
    return jax.shard_map(
        per_device,
        mesh=grid,
        in_specs=(
            P(("x", "z", "c"), "y", None),
            P(None, "y"),
            P("y", None),
            P(None, "y"),
            rows,
            rows,
            rows,
        ),
        out_specs=(shares, shares, shares, P()),
        check_vma=False,
    )
```

```python
import functools

import jax
import jax.numpy as jnp
from jax import lax
from jax.experimental import pallas as pl
from jax.experimental.pallas import tpu as pltpu
from jax.sharding import Mesh
from jax.sharding import PartitionSpec as P

SMOOTHING = 1.0
LOSS_SCALE = 4096.0
RING = 4
PAIR_LOW = ((0, 1), (1, 0), (2, 3), (3, 2))
PAIR_HIGH = ((0, 3), (3, 0), (1, 2), (2, 1))
ROOT_2_PI = 0.7978845608028654
CUBIC = 0.044715
LANES = 256
MIB = 1 << 20
F32 = jnp.float32
BF16 = jnp.bfloat16


def shift(x, axis, by):
    size = lax.axis_size(axis)
    return lax.ppermute(x, axis, [(i, (i + by) % size) for i in range(size)])


def dot(a, b, contract=((1,), (0,))):
    return lax.dot_general(a, b, (contract, ((), ())), preferred_element_type=F32)


def in_hbm(x):
    return pltpu.with_memory_space_constraint(x, pltpu.HBM)


def params(mib):
    return pltpu.CompilerParams(dimension_semantics=("arbitrary",), vmem_limit_bytes=mib * MIB)


def forward_kernel(first_call, last_call, block_rows, sizes, *refs):
    width, half, head_rows = sizes
    place, tokens = refs[:2]
    packs = (refs[2:4], refs[4:6])
    refs = refs[6:]
    if first_call:
        total_in = None
        slope, hidden, second, head, total = refs
    elif last_call:
        total_in, _, _, _, head_in, slope, hidden, second, head, residual, forecast = refs
    else:
        total_in, _, _, _, _, slope, hidden, second, head, total = refs
    block, core = place[0], place[1]
    chunks = width // LANES
    sides = (core, 1 - core)

    @pl.when(pl.program_id(0) == 0)
    def _():
        if last_call:
            head[...] = head_in[...]
        for pair, side in zip(packs, sides):
            below = pl.multiple_of(side * half, half)
            for q in range(chunks):
                second[pl.ds(below, half), q * LANES : (q + 1) * LANES] = pair[1][
                    q * half : (q + 1) * half, :
                ]
            row = pl.multiple_of(block * head_rows, 64) if last_call else 0
            for e in range(2):
                lane = pl.multiple_of(side * (width // 2) + e * LANES, LANES)
                head[pl.ds(row, head_rows), pl.ds(lane, LANES)] = pair[e][width:, :]

    rows = tokens[...]
    base = rows.astype(F32) if first_call else total_in[...]
    sums = [base[:, q * LANES : (q + 1) * LANES] for q in range(chunks)]
    for pair, side in zip(packs, sides):
        x = dot(rows, pair[0][:width, :])
        sq = x * x
        t = jnp.tanh(ROOT_2_PI * (x + CUBIC * x * sq))
        up = 0.5 * (1.0 + t)
        active = (x * up).astype(BF16)
        lane = pl.multiple_of(side * half, half)
        turn = up + (0.5 * ROOT_2_PI) * x * (1.0 - t * t) * (1.0 + (3.0 * CUBIC) * sq)
        slope[:, pl.ds(lane, half)] = turn.astype(BF16)
        hidden[:, pl.ds(lane, half)] = active
        for q in range(chunks):
            sums[q] = sums[q] + dot(active, pair[1][q * half : (q + 1) * half, :])
    full = jnp.concatenate(sums, 1)
    if last_call:
        rounded = full.astype(BF16)
        residual[...] = rounded
        forecast[...] = dot(rounded, head[...], ((1,), (1,))).astype(BF16)
    else:
        total[...] = full


def forward_part(place, tokens, packs, carried, out_width, last_call):
    rows, width = tokens.shape
    half = LANES
    hid = 2 * half * RING
    head_rows = out_width // RING
    first_call = carried is None
    block_rows = min(rows, 256)
    whole = lambda shape: pl.BlockSpec(
        shape, lambda i, s: (0,) * len(shape), pipeline_mode=pl.Buffered(1)
    )
    by_rows = lambda cols: pl.BlockSpec((block_rows, cols), lambda i, s: (i, 0))
    in_place = pl.BlockSpec(memory_space=pltpu.HBM)
    in_specs = [by_rows(width), *[whole(p.shape) for p in packs]]
    args = [tokens, *packs]
    aliases = {}
    if not first_call:
        slope, hidden, second, head, total = carried
        args += [in_hbm(v) for v in (total, slope, hidden, second, head)]
        in_specs += [by_rows(width), in_place, in_place, in_place]
        in_specs += [whole((out_width, width)) if last_call else in_place]
        aliases = {7: 0, 8: 1, 9: 2}
        if not last_call:
            aliases = {**aliases, 10: 3, 6: 4}
    column = pl.BlockSpec((block_rows, 2 * half), lambda i, s: (i, s[0]))
    out_specs = [
        column,
        column,
        pl.BlockSpec((2 * half, width), lambda i, s: (s[0], 0)),
        whole((out_width, width))
        if last_call
        else pl.BlockSpec((head_rows, width), lambda i, s: (s[0], 0)),
    ]
    out_shape = [
        jax.ShapeDtypeStruct((rows, hid), BF16),
        jax.ShapeDtypeStruct((rows, hid), BF16),
        jax.ShapeDtypeStruct((hid, width), BF16),
        jax.ShapeDtypeStruct((out_width, width), BF16),
    ]
    if last_call:
        out_specs += [by_rows(width), by_rows(out_width)]
        out_shape += [
            jax.ShapeDtypeStruct((rows, width), BF16),
            jax.ShapeDtypeStruct((rows, out_width), BF16),
        ]
    else:
        out_specs += [by_rows(width)]
        out_shape += [jax.ShapeDtypeStruct((rows, width), F32)]
    return pl.pallas_call(
        functools.partial(
            forward_kernel, first_call, last_call, block_rows, (width, half, head_rows)
        ),
        grid_spec=pltpu.PrefetchScalarGridSpec(
            num_scalar_prefetch=1,
            grid=(rows // block_rows,),
            in_specs=in_specs,
            out_specs=out_specs,
        ),
        out_shape=out_shape,
        input_output_aliases=aliases,
        compiler_params=params(24),
        cost_estimate=pl.CostEstimate(
            flops=8 * rows * width * half, bytes_accessed=12 * MIB, transcendentals=rows * 2 * half
        ),
        name="forward_part",
    )(place, *args)


def once(shape):
    return pl.BlockSpec(shape, lambda i, s: (0, 0), pipeline_mode=pl.Buffered(1))


def store_halves(core, parts, keep, send):
    n, _, rows, cols = parts.shape
    zero = parts[:, 0].reshape(n * rows, cols).astype(BF16)
    one = parts[:, 1].reshape(n * rows, cols).astype(BF16)

    @pl.when(core == 0)
    def _():
        keep[0] = zero
        send[0] = one

    @pl.when(core == 1)
    def _():
        keep[0] = one
        send[0] = zero


def riders(place, scalars, shape):
    line = lax.broadcasted_iota(jnp.int32, shape, 0)
    lane = lax.broadcasted_iota(jnp.int32, shape, 1)
    score = jnp.full(shape, scalars[0], F32)
    out = jnp.where(line == 3, scalars[1], 0.0)
    for i in range(3):
        term = score.astype(BF16).astype(F32)
        out = jnp.where(line == i, term, out)
        score = score - term
    return jnp.where(lane == 2 * place[0] + place[1], out, 0.0)


def early_kernel(place, hidden, resid_grad, keep, send):
    second = dot(hidden[...], resid_grad[...], ((0,), (0,)))
    store_halves(place[1], second.reshape(RING, 2, -1, second.shape[1]), keep, send)


def early_grads(place, hidden, resid_grad):
    rows, hid = hidden.shape
    width = resid_grad.shape[1]
    lines = hid // RING // 2
    out = pl.BlockSpec((1, lines, width), lambda i, s: (i, 0, 0))
    return pl.pallas_call(
        early_kernel,
        grid_spec=pltpu.PrefetchScalarGridSpec(
            num_scalar_prefetch=1,
            grid=(RING,),
            in_specs=[
                pl.BlockSpec((rows, hid // RING), lambda i, s: (0, i)),
                once((rows, width)),
            ],
            out_specs=[out, out],
        ),
        out_shape=[jax.ShapeDtypeStruct((RING, lines, width), BF16)] * 2,
        compiler_params=params(28),
        cost_estimate=pl.CostEstimate(
            flops=2 * rows * width * hid, bytes_accessed=12 * MIB, transcendentals=0
        ),
        name="early_grads",
    )(place, in_hbm(hidden), resid_grad)


def late_kernel(steps, place, resid_grad, second, slope, tokens, *refs):
    keep, send = refs[-2:]
    hidden_grad = dot(resid_grad[...], second[...], ((1,), (1,)))
    preact_grad = (slope[...].astype(F32) * hidden_grad).astype(BF16)
    first = dot(tokens[...], preact_grad, ((0,), (0,)))
    cols = first.shape[1]

    def store(*grads):
        parts = jnp.concatenate([g.reshape(16, 2, RING, -1, cols) for g in grads], 3)
        parts = jnp.stack([parts[:, :, i] for i in (0, 3, 1, 2)], 2)
        store_halves(place[1], parts.reshape(16, 2, -1, cols), keep, send)

    if len(refs) == 2:
        store(first)
        return
    residual, grad_rows, scalars = refs[:3]
    width, out_width = residual.shape[1], grad_rows.shape[1]
    for j in range(steps):

        @pl.when(pl.program_id(0) == j)
        def _(j=j):
            head = dot(residual[...], grad_rows[:, j * cols : (j + 1) * cols], ((0,), (0,)))
            if j == steps - 1:
                blank = riders(place, scalars, (8, width - out_width))
                blank = jnp.broadcast_to(blank, (width // 8, *blank.shape))
                head = jnp.concatenate([head, blank.reshape(width, -1)], 1)
            store(first, head)


def late_grads(place, part, resid_grad, second, slope, tokens, *head):
    rows, width = resid_grad.shape
    tile = 2 * LANES
    steps = width // tile
    lines = width if head else width // 2
    out = pl.BlockSpec((1, lines, tile), lambda j, s: (0, 0, j))
    specs = []
    if head:
        specs = [once(head[0].shape), once(head[1].shape), pl.BlockSpec(memory_space=pltpu.SMEM)]
    return pl.pallas_call(
        functools.partial(late_kernel, steps),
        grid_spec=pltpu.PrefetchScalarGridSpec(
            num_scalar_prefetch=1,
            grid=(steps,),
            in_specs=[
                once((rows, width)),
                pl.BlockSpec((tile, width), lambda j, s: (part * steps + j, 0)),
                pl.BlockSpec((rows, tile), lambda j, s: (0, part * steps + j)),
                once((rows, width)),
                *specs,
            ],
            out_specs=[out, out],
        ),
        out_shape=[jax.ShapeDtypeStruct((1, lines, width), BF16)] * 2,
        compiler_params=params(36 if head else 28),
        cost_estimate=pl.CostEstimate(
            flops=4 * rows * width * width, bytes_accessed=12 * MIB, transcendentals=0
        ),
        name="late_grads",
    )(place, resid_grad, in_hbm(second), in_hbm(slope), tokens, *head)


def add(a, b):
    return (a.astype(F32) + b.astype(F32)).astype(BF16)


def take(x, index, axis):
    return lax.dynamic_index_in_dim(x, index, axis, keepdims=False)


def ring_bits(axis):
    here = lax.axis_index(axis)
    high = here // 2
    return (high + here) % 2, high


def ring_chain(axis, low_first):
    low, high = ring_bits(axis)
    if low_first:
        steps = ((PAIR_LOW, low, 0), (PAIR_HIGH, high, 0))
    else:
        steps = ((PAIR_HIGH, high, 1), (PAIR_LOW, low, 0))
    return [(pairs, axis, bit, dim) for pairs, bit, dim in steps]


def outgoing(x, step):
    _, _, bit, dim = step
    return take(x, 1 - bit, dim)


def sent_along(x, step):
    return lax.ppermute(x, step[1], step[0])


def kept_plus(x, arrived, step):
    _, _, bit, dim = step
    return add(take(x, bit, dim), arrived)


def by_ring(x):
    return x.reshape(16, 2, 2, -1, x.shape[-1]).transpose(1, 2, 0, 3, 4)


def tie(*arrays):
    return lax.optimization_barrier(arrays)


def after(x, *others):
    return lax.optimization_barrier((x, *others))[0]


def pack_kernel(side, first, second, head, a, b):
    width = first.shape[0]
    half = second.shape[0]
    a[:width, :] = first[...]
    for q in range(width // LANES):
        b[q * half : (q + 1) * half, :] = second[:, q * LANES : (q + 1) * LANES]
    a[width:, :] = head[:, :LANES]
    b[width:, :] = head[:, LANES:]


def packed(side, first, second, head):
    width, shard = first.shape
    half = shard // 2
    lines = width + head.shape[0]
    out = pl.BlockSpec((lines, LANES), lambda i, s: (0, 0))
    return pl.pallas_call(
        pack_kernel,
        grid_spec=pltpu.PrefetchScalarGridSpec(
            num_scalar_prefetch=1,
            grid=(1,),
            in_specs=[
                pl.BlockSpec((width, half), lambda i, s: (0, s[0])),
                pl.BlockSpec((half, width), lambda i, s: (s[0], 0)),
                pl.BlockSpec((head.shape[0], width // 2), lambda i, s: (0, s[0])),
            ],
            out_specs=[out, out],
        ),
        out_shape=[jax.ShapeDtypeStruct((lines, LANES), BF16)] * 2,
        compiler_params=params(8),
        name="packed",
    )(side, first, second, head)


def score(samples, target, valid_mask):
    count = samples.shape[0]
    wide = samples.astype(F32)
    gram = jnp.einsum("mpo,npo->pmn", samples, samples, preferred_element_type=F32)
    squares = jnp.sum(wide * wide, axis=2).T
    dist_sq = squares[:, :, None] + squares[:, None, :] - 2.0 * gram
    spread = jnp.sqrt(dist_sq + SMOOTHING)
    kernel = 1.0 / spread
    kernel_sum = jnp.sum(kernel, axis=2)
    pulled = jnp.einsum("pmn,npo->mpo", kernel, wide, precision=lax.Precision.HIGHEST)
    offset = wide - target[None]
    error_norm = jnp.sqrt(jnp.sum(offset * offset, axis=2) + SMOOTHING)
    repulse = wide * kernel_sum.T[:, :, None] - pulled
    validity = valid_mask.astype(F32)
    grad_raw = (
        LOSS_SCALE
        * validity[None, :, None]
        * (offset / (count * error_norm[:, :, None]) - repulse / (count * count))
    ).astype(BF16)
    scores = validity * (
        jnp.mean(error_norm, axis=0) - jnp.sum(spread, axis=(1, 2)) / (2.0 * count * count)
    )
    return grad_raw, jnp.sum(scores), jnp.sum(validity)


def per_device(latents, w_first, w_second, readout_matrix, observed, obs_index, valid_mask):
    members, patches, width = latents.shape
    out_width = observed.shape[1]
    core = lax.axis_index("c")
    here = lax.axis_index("y")
    own = obs_index.shape[0]
    rows = members * patches
    shard = w_first.shape[1]
    half = shard // 2

    side = jnp.reshape(core, (1,)).astype(jnp.int32)
    turned = readout_matrix.T
    own_a, own_b = packed(side, w_first, w_second, turned)
    right_a = shift(own_a, "y", 1)
    left_b = shift(own_b, "y", -1)
    latents, other_side, own_a, own_b = tie(latents, 1 - side, own_a, own_b)
    tokens = (
        latents.reshape(members, 32, own, width).transpose(1, 0, 2, 3).reshape(rows, width)
    )
    place = lambda off: jnp.stack([(here + off) % RING, core]).astype(jnp.int32)
    run = functools.partial(forward_part, out_width=out_width)
    swap = lambda x: shift(x, "c", 1)
    packs = (own_a, own_b, *packed(other_side, w_first, w_second, turned))
    carried = run(place(0), tokens, packs, carried=None, last_call=False)
    right_a, left_b, *carried = tie(right_a, left_b, *carried)
    left_a = shift(after(own_a, right_a, left_b), "y", -1)
    right_b = shift(after(own_b, right_a, left_b), "y", 1)
    right_a_other, left_b_other = swap(right_a), swap(left_b)
    left_a, right_b, right_a_other, left_b_other = tie(
        left_a, right_b, right_a_other, left_b_other
    )
    far_a = shift(after(right_a, left_a, right_b), "y", 1)
    far_b = shift(after(left_b, left_a, right_b), "y", -1)
    packs = (right_a, right_b, right_a_other, swap(right_b))
    carried = run(place(3), tokens, packs, carried=carried, last_call=False)
    packs = (left_a, left_b, swap(left_a), left_b_other)
    carried = run(place(1), tokens, packs, carried=carried, last_call=False)
    far_a, far_b, *carried = tie(far_a, far_b, *carried)
    slope, hidden, second, head, residual, forecast = run(
        place(2), tokens, (far_a, far_b, swap(far_a), swap(far_b)), carried=carried, last_call=True
    )

    group = ("x", "z", "c")
    device = ((here * 4 + lax.axis_index("x")) * 4 + lax.axis_index("z")) * 2 + core
    target = jnp.take(observed, obs_index - device * own, axis=0)
    forecast, target = tie(forecast.reshape(32, members * own, out_width), target)
    gathered = lax.all_to_all(forecast, group, 0, 0, tiled=True)
    samples = gathered.reshape(32 * members, own, out_width)
    grad_raw, score_part, count_part = score(samples, target, valid_mask)
    grad_rows = lax.all_to_all(
        grad_raw.reshape(32, members * own, out_width), group, 0, 0, tiled=True
    ).reshape(rows, out_width)

    at = place(0)
    scalars = jnp.stack([score_part, count_part])
    resid_grad = dot(grad_rows, head).astype(BF16)
    early = early_grads(at, hidden, resid_grad)
    early_in = shift(early[1], "c", 1)
    late = late_grads(
        at,
        0,
        after(resid_grad, early[1]),
        second,
        slope,
        tokens,
        residual,
        grad_rows,
        scalars,
    )
    a_in = shift(late[1], "c", 1)
    y_steps = [ring_chain("y", True), ring_chain("y", False)]
    early = add(after(early[0], late[1]), early_in).reshape(-1, width)
    early_sum = lax.psum_scatter(early, "x", scatter_dimension=0, tiled=True)
    a = by_ring(add(after(late[0], early), a_in))
    a_sent = outgoing(a, y_steps[0][0])
    a_in = sent_along(a_sent, y_steps[0][0])
    late = late_grads(at, 1, after(resid_grad, a_sent), second, slope, tokens)
    b_in = shift(late[1], "c", 1)
    b = by_ring(add(late[0], b_in))
    b_sent = outgoing(b, y_steps[1][0])
    b_in = sent_along(b_sent, y_steps[1][0])
    a = kept_plus(a, after(a_in, b_sent), y_steps[0][0])
    a_sent = outgoing(a, y_steps[0][1])
    a_in = sent_along(a_sent, y_steps[0][1])
    b = kept_plus(b, after(b_in, a_sent), y_steps[1][0])
    b_sent = outgoing(b, y_steps[1][1])
    b_in = sent_along(b_sent, y_steps[1][1])
    early = early_sum.reshape(16, -1, width)
    early = lax.all_to_all(early, ("z", "y"), 0, 0, tiled=True)
    a = kept_plus(a, after(a_in, b_sent, early_sum), y_steps[0][1])
    b = kept_plus(b, after(b_in, early_sum), y_steps[1][1])
    late = lax.all_to_all(jnp.concatenate([a, b], 1), ("x", "z"), 0, 0, tiled=True)
    early = jnp.sum(early.astype(F32), 0)
    late = jnp.sum(late.astype(F32), 0)
    n = width // 128
    ride = jnp.sum(late[n : 2 * n, out_width:], 1)
    score_total = ride[0] + ride[1] + ride[2]
    valid_total = jnp.maximum(ride[3], 1.0)
    scale = 1.0 / valid_total
    return (
        jnp.concatenate([late[:n], late[2 * n :]], 1) * scale,
        early * scale,
        late[n : 2 * n, :out_width] * scale,
        score_total / valid_total,
    )


def solution(mesh):
    grid = Mesh(mesh.devices.reshape(4, 4, 2, 4), ("x", "z", "c", "y"))
    rows = P(("y", "x", "z", "c"))
    shares = P(("x", "z", "c", "y"), None)
    return jax.shard_map(
        per_device,
        mesh=grid,
        in_specs=(
            P(("x", "z", "c"), "y", None),
            P(None, "y"),
            P("y", None),
            P(None, "y"),
            rows,
            rows,
            rows,
        ),
        out_specs=(shares, shares, shares, P()),
        check_vma=False,
    )
```

```python
import functools

import jax
import jax.numpy as jnp
from jax import lax
from jax.experimental import pallas as pl
from jax.experimental.pallas import tpu as pltpu
from jax.sharding import Mesh
from jax.sharding import PartitionSpec as P

SMOOTHING = 1.0
LOSS_SCALE = 4096.0
RING = 4
PAIR_LOW = ((0, 1), (1, 0), (2, 3), (3, 2))
PAIR_HIGH = ((0, 3), (3, 0), (1, 2), (2, 1))
ROOT_2_PI = 0.7978845608028654
CUBIC = 0.044715
LANES = 256
MIB = 1 << 20
F32 = jnp.float32
BF16 = jnp.bfloat16


def shift(x, axis, by):
    size = lax.axis_size(axis)
    return lax.ppermute(x, axis, [(i, (i + by) % size) for i in range(size)])


def dot(a, b, contract=((1,), (0,))):
    return lax.dot_general(a, b, (contract, ((), ())), preferred_element_type=F32)


def params(mib):
    return pltpu.CompilerParams(dimension_semantics=("arbitrary",), vmem_limit_bytes=mib * MIB)


def forward_kernel(first_call, last_call, block_rows, sizes, *refs):
    width, half, head_rows = sizes
    place, tokens = refs[:2]
    packs = (refs[2:4], refs[4:6])
    refs = refs[6:]
    if first_call:
        total_in = None
        slope, hidden, second, head, total = refs
    elif last_call:
        total_in, _, _, _, head_in, slope, hidden, second, head, residual, forecast = refs
    else:
        total_in, _, _, _, _, slope, hidden, second, head, total = refs
    block, core = place[0], place[1]
    chunks = width // LANES
    sides = (core, 1 - core)

    @pl.when(pl.program_id(0) == 0)
    def _():
        if last_call:
            head[...] = head_in[...]
        for pair, side in zip(packs, sides):
            below = pl.multiple_of(side * half, half)
            for q in range(chunks):
                second[pl.ds(below, half), q * LANES : (q + 1) * LANES] = pair[1][
                    q * half : (q + 1) * half, :
                ]
            row = pl.multiple_of(block * head_rows, 64) if last_call else 0
            for e in range(2):
                lane = pl.multiple_of(side * (width // 2) + e * LANES, LANES)
                head[pl.ds(row, head_rows), pl.ds(lane, LANES)] = pair[e][width:, :]

    rows = tokens[...]
    base = rows.astype(F32) if first_call else total_in[...]
    sums = [base[:, q * LANES : (q + 1) * LANES] for q in range(chunks)]
    for pair, side in zip(packs, sides):
        x = dot(rows, pair[0][:width, :])
        sq = x * x
        t = jnp.tanh(ROOT_2_PI * (x + CUBIC * x * sq))
        up = 0.5 * (1.0 + t)
        active = (x * up).astype(BF16)
        lane = pl.multiple_of(side * half, half)
        turn = up + (0.5 * ROOT_2_PI) * x * (1.0 - t * t) * (1.0 + (3.0 * CUBIC) * sq)
        slope[:, pl.ds(lane, half)] = turn.astype(BF16)
        hidden[:, pl.ds(lane, half)] = active
        for q in range(chunks):
            sums[q] = sums[q] + dot(active, pair[1][q * half : (q + 1) * half, :])
    full = jnp.concatenate(sums, 1)
    if last_call:
        rounded = full.astype(BF16)
        residual[...] = rounded
        forecast[...] = dot(rounded, head[...], ((1,), (1,))).astype(BF16)
    else:
        total[...] = full


def forward_part(place, tokens, packs, carried, out_width, last_call):
    rows, width = tokens.shape
    half = LANES
    hid = 2 * half * RING
    head_rows = out_width // RING
    first_call = carried is None
    block_rows = min(rows, 256)
    whole = lambda shape: pl.BlockSpec(
        shape, lambda i, s: (0,) * len(shape), pipeline_mode=pl.Buffered(1)
    )
    by_rows = lambda cols: pl.BlockSpec((block_rows, cols), lambda i, s: (i, 0))
    in_place = pl.BlockSpec(memory_space=pl.ANY)
    in_specs = [by_rows(width), *[whole(p.shape) for p in packs]]
    args = [tokens, *packs]
    aliases = {}
    if not first_call:
        slope, hidden, second, head, total = carried
        args += [total, slope, hidden, second, head]
        in_specs += [by_rows(width), in_place, in_place, in_place]
        in_specs += [whole((out_width, width)) if last_call else in_place]
        aliases = {7: 0, 8: 1, 9: 2}
        if not last_call:
            aliases = {**aliases, 10: 3, 6: 4}
    column = pl.BlockSpec((block_rows, 2 * half), lambda i, s: (i, s[0]))
    out_specs = [
        column,
        column,
        pl.BlockSpec((2 * half, width), lambda i, s: (s[0], 0)),
        whole((out_width, width))
        if last_call
        else pl.BlockSpec((head_rows, width), lambda i, s: (s[0], 0)),
    ]
    out_shape = [
        jax.ShapeDtypeStruct((rows, hid), BF16),
        jax.ShapeDtypeStruct((rows, hid), BF16),
        jax.ShapeDtypeStruct((hid, width), BF16),
        jax.ShapeDtypeStruct((out_width, width), BF16),
    ]
    if last_call:
        out_specs += [by_rows(width), by_rows(out_width)]
        out_shape += [
            jax.ShapeDtypeStruct((rows, width), BF16),
            jax.ShapeDtypeStruct((rows, out_width), BF16),
        ]
    else:
        out_specs += [by_rows(width)]
        out_shape += [jax.ShapeDtypeStruct((rows, width), F32)]
    return pl.pallas_call(
        functools.partial(
            forward_kernel, first_call, last_call, block_rows, (width, half, head_rows)
        ),
        grid_spec=pltpu.PrefetchScalarGridSpec(
            num_scalar_prefetch=1,
            grid=(rows // block_rows,),
            in_specs=in_specs,
            out_specs=out_specs,
        ),
        out_shape=out_shape,
        input_output_aliases=aliases,
        compiler_params=params(56),
        cost_estimate=pl.CostEstimate(
            flops=8 * rows * width * half, bytes_accessed=12 * MIB, transcendentals=rows * 2 * half
        ),
        name="forward_part",
    )(place, *args)


def once(shape):
    return pl.BlockSpec(shape, lambda i, s: (0, 0), pipeline_mode=pl.Buffered(1))


def store_halves(core, parts, keep, send):
    n, _, rows, cols = parts.shape
    zero = parts[:, 0].reshape(n * rows, cols).astype(BF16)
    one = parts[:, 1].reshape(n * rows, cols).astype(BF16)

    @pl.when(core == 0)
    def _():
        keep[0] = zero
        send[0] = one

    @pl.when(core == 1)
    def _():
        keep[0] = one
        send[0] = zero


def riders(place, scalars, shape):
    line = lax.broadcasted_iota(jnp.int32, shape, 0)
    lane = lax.broadcasted_iota(jnp.int32, shape, 1)
    score = jnp.full(shape, scalars[0], F32)
    out = jnp.where(line == 3, scalars[1], 0.0)
    for i in range(3):
        term = score.astype(BF16).astype(F32)
        out = jnp.where(line == i, term, out)
        score = score - term
    return jnp.where(lane == 2 * place[0] + place[1], out, 0.0)


def early_kernel(place, hidden, resid_grad, keep, send):
    second = dot(hidden[...], resid_grad[...], ((0,), (0,)))
    store_halves(place[1], second.reshape(RING, 2, -1, second.shape[1]), keep, send)


def early_grads(place, hidden, resid_grad):
    rows, hid = hidden.shape
    width = resid_grad.shape[1]
    lines = hid // RING // 2
    gray = lambda i: 2 * ((i // 2 + i) % 2) + i // 2
    out = pl.BlockSpec((1, lines, width), lambda i, s: (gray(i), 0, 0))
    return pl.pallas_call(
        early_kernel,
        grid_spec=pltpu.PrefetchScalarGridSpec(
            num_scalar_prefetch=1,
            grid=(RING,),
            in_specs=[
                pl.BlockSpec((rows, hid // RING), lambda i, s: (0, i)),
                once((rows, width)),
            ],
            out_specs=[out, out],
        ),
        out_shape=[jax.ShapeDtypeStruct((RING, lines, width), BF16)] * 2,
        compiler_params=params(56),
        cost_estimate=pl.CostEstimate(
            flops=2 * rows * width * hid, bytes_accessed=12 * MIB, transcendentals=0
        ),
        name="early_grads",
    )(place, hidden, resid_grad)


def late_kernel(steps, place, resid_grad, second, slope, tokens, *refs):
    keep, send = refs[-2:]
    hidden_grad = dot(resid_grad[...], second[...], ((1,), (1,)))
    preact_grad = (slope[...].astype(F32) * hidden_grad).astype(BF16)
    first = dot(tokens[...], preact_grad, ((0,), (0,)))
    cols = first.shape[1]

    def store(*grads):
        parts = jnp.concatenate([g.reshape(16, 2, RING, -1, cols) for g in grads], 3)
        parts = jnp.stack([parts[:, :, i] for i in (0, 3, 1, 2)], 2)
        store_halves(place[1], parts.reshape(16, 2, -1, cols), keep, send)

    if len(refs) == 2:
        store(first)
        return
    residual, grad_rows, scalars = refs[:3]
    width, out_width = residual.shape[1], grad_rows.shape[1]
    for j in range(steps):

        @pl.when(pl.program_id(0) == j)
        def _(j=j):
            head = dot(residual[...], grad_rows[:, j * cols : (j + 1) * cols], ((0,), (0,)))
            if j == steps - 1:
                blank = riders(place, scalars, (8, width - out_width))
                blank = jnp.broadcast_to(blank, (width // 8, *blank.shape))
                head = jnp.concatenate([head, blank.reshape(width, -1)], 1)
            store(first, head)


def late_grads(place, part, resid_grad, second, slope, tokens, *head):
    rows, width = resid_grad.shape
    tile = 2 * LANES
    steps = width // tile
    lines = width if head else width // 2
    out = pl.BlockSpec((1, lines, tile), lambda j, s: (0, 0, j))
    specs = []
    if head:
        specs = [once(head[0].shape), once(head[1].shape), pl.BlockSpec(memory_space=pltpu.SMEM)]
    return pl.pallas_call(
        functools.partial(late_kernel, steps),
        grid_spec=pltpu.PrefetchScalarGridSpec(
            num_scalar_prefetch=1,
            grid=(steps,),
            in_specs=[
                once((rows, width)),
                pl.BlockSpec((tile, width), lambda j, s: (part * steps + j, 0)),
                pl.BlockSpec((rows, tile), lambda j, s: (0, part * steps + j)),
                once((rows, width)),
                *specs,
            ],
            out_specs=[out, out],
        ),
        out_shape=[jax.ShapeDtypeStruct((1, lines, width), BF16)] * 2,
        compiler_params=params(56),
        cost_estimate=pl.CostEstimate(
            flops=4 * rows * width * width, bytes_accessed=12 * MIB, transcendentals=0
        ),
        name="late_grads",
    )(place, resid_grad, second, slope, tokens, *head)


def add(a, b):
    return (a.astype(F32) + b.astype(F32)).astype(BF16)


def take(x, index, axis):
    return lax.dynamic_index_in_dim(x, index, axis, keepdims=False)


def ring_bits(axis):
    here = lax.axis_index(axis)
    high = here // 2
    return (high + here) % 2, high


def ring_chain(axis, low_first):
    low, high = ring_bits(axis)
    if low_first:
        steps = ((PAIR_LOW, low, 0), (PAIR_HIGH, high, 0))
    else:
        steps = ((PAIR_HIGH, high, 1), (PAIR_LOW, low, 0))
    return [(pairs, axis, bit, dim) for pairs, bit, dim in steps]


def outgoing(x, step):
    _, _, bit, dim = step
    return take(x, 1 - bit, dim)


def sent_along(x, step):
    return lax.ppermute(x, step[1], step[0])


def kept_plus(x, arrived, step):
    _, _, bit, dim = step
    return add(take(x, bit, dim), arrived)


def by_ring(x):
    return x.reshape(16, 2, 2, -1, x.shape[-1]).transpose(1, 2, 0, 3, 4)


def tie(*arrays):
    return lax.optimization_barrier(arrays)


def after(x, *others):
    return lax.optimization_barrier((x, *others))[0]


def pack_kernel(side, first, second, head, a, b):
    width = first.shape[0]
    half = second.shape[0]
    a[:width, :] = first[...]
    for q in range(width // LANES):
        b[q * half : (q + 1) * half, :] = second[:, q * LANES : (q + 1) * LANES]
    a[width:, :] = head[:, :LANES]
    b[width:, :] = head[:, LANES:]


def packed(side, first, second, head):
    width, shard = first.shape
    half = shard // 2
    lines = width + head.shape[0]
    out = pl.BlockSpec((lines, LANES), lambda i, s: (0, 0))
    return pl.pallas_call(
        pack_kernel,
        grid_spec=pltpu.PrefetchScalarGridSpec(
            num_scalar_prefetch=1,
            grid=(1,),
            in_specs=[
                pl.BlockSpec((width, half), lambda i, s: (0, s[0])),
                pl.BlockSpec((half, width), lambda i, s: (s[0], 0)),
                pl.BlockSpec((head.shape[0], width // 2), lambda i, s: (0, s[0])),
            ],
            out_specs=[out, out],
        ),
        out_shape=[jax.ShapeDtypeStruct((lines, LANES), BF16)] * 2,
        compiler_params=params(8),
        name="packed",
    )(side, first, second, head)


def score(samples, target, valid_mask):
    count = samples.shape[0]
    wide = samples.astype(F32)
    gram = jnp.einsum("mpo,npo->pmn", samples, samples, preferred_element_type=F32)
    squares = jnp.sum(wide * wide, axis=2).T
    dist_sq = squares[:, :, None] + squares[:, None, :] - 2.0 * gram
    spread = jnp.sqrt(dist_sq + SMOOTHING)
    kernel = 1.0 / spread
    kernel_sum = jnp.sum(kernel, axis=2)
    pulled = jnp.einsum("pmn,npo->mpo", kernel, wide, precision=lax.Precision.HIGHEST)
    offset = wide - target[None]
    error_norm = jnp.sqrt(jnp.sum(offset * offset, axis=2) + SMOOTHING)
    repulse = wide * kernel_sum.T[:, :, None] - pulled
    validity = valid_mask.astype(F32)
    grad_raw = (
        LOSS_SCALE
        * validity[None, :, None]
        * (offset / (count * error_norm[:, :, None]) - repulse / (count * count))
    ).astype(BF16)
    scores = validity * (
        jnp.mean(error_norm, axis=0) - jnp.sum(spread, axis=(1, 2)) / (2.0 * count * count)
    )
    return grad_raw, jnp.sum(scores), jnp.sum(validity)


def per_device(latents, w_first, w_second, readout_matrix, observed, obs_index, valid_mask):
    members, patches, width = latents.shape
    out_width = observed.shape[1]
    core = lax.axis_index("c")
    here = lax.axis_index("y")
    own = obs_index.shape[0]
    rows = members * patches
    shard = w_first.shape[1]
    half = shard // 2

    side = jnp.reshape(core, (1,)).astype(jnp.int32)
    turned = readout_matrix.T
    own_a, own_b = packed(side, w_first, w_second, turned)
    right_a = shift(own_a, "y", 1)
    left_b = shift(own_b, "y", -1)
    latents, other_side, own_a, own_b = tie(latents, 1 - side, own_a, own_b)
    tokens = (
        latents.reshape(members, 32, own, width).transpose(1, 0, 2, 3).reshape(rows, width)
    )
    place = lambda off: jnp.stack([(here + off) % RING, core]).astype(jnp.int32)
    run = functools.partial(forward_part, out_width=out_width)
    swap = lambda x: shift(x, "c", 1)
    packs = (own_a, own_b, *packed(other_side, w_first, w_second, turned))
    carried = run(place(0), tokens, packs, carried=None, last_call=False)
    right_a, left_b, *_ = tie(right_a, left_b, carried[-1])
    left_a = shift(after(own_a, right_a, left_b), "y", -1)
    right_b = shift(after(own_b, right_a, left_b), "y", 1)
    right_a_other, left_b_other = swap(right_a), swap(left_b)
    left_a, right_b, right_a_other, left_b_other = tie(
        left_a, right_b, right_a_other, left_b_other
    )
    far_a = shift(after(right_a, left_a, right_b), "y", 1)
    far_b = shift(after(left_b, left_a, right_b), "y", -1)
    packs = (right_a, right_b, right_a_other, swap(right_b))
    carried = run(place(3), tokens, packs, carried=carried, last_call=False)
    packs = (left_a, left_b, swap(left_a), left_b_other)
    carried = run(place(1), tokens, packs, carried=carried, last_call=False)
    far_a, far_b, *carried = tie(far_a, far_b, *carried)
    slope, hidden, second, head, residual, forecast = run(
        place(2), tokens, (far_a, far_b, swap(far_a), swap(far_b)), carried=carried, last_call=True
    )

    group = ("x", "z", "c")
    device = ((here * 4 + lax.axis_index("x")) * 4 + lax.axis_index("z")) * 2 + core
    target = jnp.take(observed, obs_index - device * own, axis=0)
    forecast, target = tie(forecast.reshape(32, members * own, out_width), target)
    gathered = lax.all_to_all(forecast, group, 0, 0, tiled=True)
    samples = gathered.reshape(32 * members, own, out_width)
    grad_raw, score_part, count_part = score(samples, target, valid_mask)
    grad_rows = lax.all_to_all(
        grad_raw.reshape(32, members * own, out_width), group, 0, 0, tiled=True
    ).reshape(rows, out_width)

    at = place(0)
    scalars = jnp.stack([score_part, count_part])
    resid_grad = dot(grad_rows, head).astype(BF16)
    early = early_grads(at, hidden, resid_grad)
    early_in = shift(early[1], "c", 1)
    late = late_grads(
        at,
        0,
        after(resid_grad, early[1]),
        second,
        slope,
        tokens,
        residual,
        grad_rows,
        scalars,
    )
    a_in = shift(late[1], "c", 1)
    y_steps = [ring_chain("y", True), ring_chain("y", False)]
    x_steps = [ring_chain("x", True), ring_chain("x", False)]
    early = add(after(early[0], late[1]), early_in).reshape(2, 2, 2, -1, width)
    early = [early[:, :, 0], early[:, :, 1]]
    early_sent = [outgoing(x, steps[0]) for x, steps in zip(early, x_steps)]
    early_in = [sent_along(x, steps[0]) for x, steps in zip(early_sent, x_steps)]
    a = by_ring(add(after(late[0], *early_sent), a_in))
    a_sent = outgoing(a, y_steps[0][0])
    a_in = sent_along(a_sent, y_steps[0][0])
    late = late_grads(at, 1, after(resid_grad, a_sent), second, slope, tokens)
    b_in = shift(late[1], "c", 1)
    early = [
        kept_plus(x, after(v, late[1]), steps[0]) for x, v, steps in zip(early, early_in, x_steps)
    ]
    early_sent = [outgoing(x, steps[1]) for x, steps in zip(early, x_steps)]
    early_in = [sent_along(x, steps[1]) for x, steps in zip(early_sent, x_steps)]
    a = kept_plus(a, after(a_in, *early_sent), y_steps[0][0])
    a_sent = outgoing(a, y_steps[0][1])
    a_in = sent_along(a_sent, y_steps[0][1])
    b = by_ring(add(after(late[0], a_sent), b_in))
    b_sent = outgoing(b, y_steps[1][0])
    b_in = sent_along(b_sent, y_steps[1][0])
    early = [
        kept_plus(x, after(v, b_sent), steps[1]) for x, v, steps in zip(early, early_in, x_steps)
    ]
    early = jnp.concatenate(early).reshape(16, -1, width)
    early_all = lax.all_to_all(early, ("z", "y"), 0, 0, tiled=True)
    b = kept_plus(b, after(b_in, early), y_steps[1][0])
    b_sent = outgoing(b, y_steps[1][1])
    b_in = sent_along(b_sent, y_steps[1][1])
    a = kept_plus(a, after(a_in, b_sent), y_steps[0][1])
    b = kept_plus(b, b_in, y_steps[1][1])
    early = early_all
    late = lax.all_to_all(jnp.concatenate([a, b], 1), ("x", "z"), 0, 0, tiled=True)
    early = jnp.sum(early.astype(F32), 0)
    late = jnp.sum(late.astype(F32), 0)
    n = width // 128
    ride = jnp.sum(late[n : 2 * n, out_width:], 1)
    score_total = ride[0] + ride[1] + ride[2]
    valid_total = jnp.maximum(ride[3], 1.0)
    scale = 1.0 / valid_total
    return (
        jnp.concatenate([late[:n], late[2 * n :]], 1) * scale,
        early * scale,
        late[n : 2 * n, :out_width] * scale,
        score_total / valid_total,
    )


def solution(mesh):
    grid = Mesh(mesh.devices.reshape(4, 4, 2, 4), ("x", "z", "c", "y"))
    rows = P(("y", "x", "z", "c"))
    shares = P(("x", "z", "c", "y"), None)
    return jax.shard_map(
        per_device,
        mesh=grid,
        in_specs=(
            P(("x", "z", "c"), "y", None),
            P(None, "y"),
            P("y", None),
            P(None, "y"),
            rows,
            rows,
            rows,
        ),
        out_specs=(shares, shares, shares, P()),
        check_vma=False,
    )
```

```python
import functools

import jax
import jax.numpy as jnp
from jax import lax
from jax.experimental import pallas as pl
from jax.experimental.pallas import tpu as pltpu
from jax.sharding import Mesh
from jax.sharding import PartitionSpec as P

SMOOTHING = 1.0
LOSS_SCALE = 4096.0
RING = 4
PAIR_LOW = ((0, 1), (1, 0), (2, 3), (3, 2))
PAIR_HIGH = ((0, 3), (3, 0), (1, 2), (2, 1))
ROOT_2_PI = 0.7978845608028654
CUBIC = 0.044715
LANES = 256
MIB = 1 << 20
F32 = jnp.float32
BF16 = jnp.bfloat16


def shift(x, axis, by):
    size = lax.axis_size(axis)
    return lax.ppermute(x, axis, [(i, (i + by) % size) for i in range(size)])


def dot(a, b, contract=((1,), (0,))):
    return lax.dot_general(a, b, (contract, ((), ())), preferred_element_type=F32)


def params(mib):
    return pltpu.CompilerParams(dimension_semantics=("arbitrary",), vmem_limit_bytes=mib * MIB)


def forward_kernel(groups, first_call, last_call, sizes, *refs):
    width, half, head_rows = sizes
    place, tokens = refs[:2]
    packs = [(refs[2 + 4 * g : 4 + 4 * g], refs[4 + 4 * g : 6 + 4 * g]) for g in range(groups)]
    refs = refs[2 + 4 * groups :]
    if first_call:
        slope, hidden, second, head, total = refs
    elif last_call:
        total_in, _, _, _, head_in, slope, hidden, second, head, residual, forecast = refs
    elif groups > 1:
        total_in, _, _, _, _, slope, hidden, second, head, total, kept = refs
    else:
        total_in, _, _, _, _, slope, hidden, second, head, total = refs
    group, step = pl.program_id(0), pl.program_id(1)
    core = place[1]
    chunks = width // LANES
    sides = (core, 1 - core)

    def run(g):
        @pl.when(step == 0)
        def _():
            if last_call:
                head[...] = head_in[...]
            for pair, side in zip(packs[g], sides):
                below = pl.multiple_of(side * half, half)
                for q in range(chunks):
                    second[pl.ds(below, half), q * LANES : (q + 1) * LANES] = pair[1][
                        q * half : (q + 1) * half, :
                    ]
                row = pl.multiple_of(place[3] * head_rows, 64) if last_call else 0
                for e in range(2):
                    lane = pl.multiple_of(side * (width // 2) + e * LANES, LANES)
                    head[pl.ds(row, head_rows), pl.ds(lane, LANES)] = pair[e][width:, :]

        rows = tokens[...]
        count = rows.shape[0]
        line = pl.multiple_of(step * count, count)
        if first_call:
            base = rows.astype(F32)
        elif g == 0:
            base = total_in[...]
        else:
            base = kept[pl.ds(line, count), :]
        sums = [base[:, q * LANES : (q + 1) * LANES] for q in range(chunks)]
        for pair, side in zip(packs[g], sides):
            x = dot(rows, pair[0][:width, :])
            sq = x * x
            t = jnp.tanh(ROOT_2_PI * (x + CUBIC * x * sq))
            up = 0.5 * (1.0 + t)
            active = (x * up).astype(BF16)
            lane = pl.multiple_of(side * half, half)
            turn = up + (0.5 * ROOT_2_PI) * x * (1.0 - t * t) * (1.0 + (3.0 * CUBIC) * sq)
            slope[:, pl.ds(lane, half)] = turn.astype(BF16)
            hidden[:, pl.ds(lane, half)] = active
            for q in range(chunks):
                sums[q] = sums[q] + dot(active, pair[1][q * half : (q + 1) * half, :])
        full = jnp.concatenate(sums, 1)
        if last_call:
            rounded = full.astype(BF16)
            residual[...] = rounded
            forecast[...] = dot(rounded, head[...], ((1,), (1,))).astype(BF16)
        elif g + 1 < groups:
            kept[pl.ds(line, count), :] = full
        else:
            total[...] = full

    for g in range(groups):
        if groups == 1:
            run(g)
        else:
            pl.when(group == g)(functools.partial(run, g))


def forward_part(place, tokens, packs, carried, out_width, last_call):
    rows, width = tokens.shape
    groups = len(packs) // 4
    half = LANES
    hid = 2 * half * RING
    head_rows = out_width // RING
    first_call = carried is None
    block_rows = min(rows, 256)
    whole = lambda shape: pl.BlockSpec(
        shape, lambda g, i, s: (0,) * len(shape), pipeline_mode=pl.Buffered(1)
    )
    by_rows = lambda cols: pl.BlockSpec((block_rows, cols), lambda g, i, s: (i, 0))
    last_of = rows // block_rows - 1
    entering = pl.BlockSpec(
        (block_rows, width), lambda g, i, s: (jnp.where(g == 0, i, last_of), 0)
    )
    leaving = pl.BlockSpec(
        (block_rows, width), lambda g, i, s: (jnp.where(g == groups - 1, i, 0), 0)
    )
    in_place = pl.BlockSpec(memory_space=pl.ANY)
    in_specs = [by_rows(width), *[whole(p.shape) for p in packs]]
    args = [tokens, *packs]
    aliases = {}
    if not first_call:
        slope, hidden, second, head, total = carried
        at = 1 + len(args)
        args += [total, slope, hidden, second, head]
        in_specs += [entering, in_place, in_place, in_place]
        in_specs += [whole((out_width, width)) if last_call else in_place]
        aliases = {at + 1: 0, at + 2: 1, at + 3: 2}
        if not last_call:
            aliases = {**aliases, at + 4: 3}
    column = pl.BlockSpec((block_rows, 2 * half), lambda g, i, s: (i, s[3 + g]))
    out_specs = [
        column,
        column,
        pl.BlockSpec((2 * half, width), lambda g, i, s: (s[3 + g], 0)),
        whole((out_width, width))
        if last_call
        else pl.BlockSpec((head_rows, width), lambda g, i, s: (s[3 + g], 0)),
    ]
    out_shape = [
        jax.ShapeDtypeStruct((rows, hid), BF16),
        jax.ShapeDtypeStruct((rows, hid), BF16),
        jax.ShapeDtypeStruct((hid, width), BF16),
        jax.ShapeDtypeStruct((out_width, width), BF16),
    ]
    if last_call:
        out_specs += [by_rows(width), by_rows(out_width)]
        out_shape += [
            jax.ShapeDtypeStruct((rows, width), BF16),
            jax.ShapeDtypeStruct((rows, out_width), BF16),
        ]
    else:
        out_specs += [leaving]
        out_shape += [jax.ShapeDtypeStruct((rows, width), F32)]
    return pl.pallas_call(
        functools.partial(
            forward_kernel, groups, first_call, last_call, (width, half, head_rows)
        ),
        grid_spec=pltpu.PrefetchScalarGridSpec(
            num_scalar_prefetch=1,
            grid=(groups, rows // block_rows),
            in_specs=in_specs,
            out_specs=out_specs,
            scratch_shapes=[pltpu.VMEM((rows, width), F32)] if groups > 1 else [],
        ),
        out_shape=out_shape,
        input_output_aliases=aliases,
        compiler_params=pltpu.CompilerParams(
            dimension_semantics=("arbitrary",) * 2, vmem_limit_bytes=56 * MIB
        ),
        cost_estimate=pl.CostEstimate(
            flops=8 * groups * rows * width * half,
            bytes_accessed=12 * MIB,
            transcendentals=groups * rows * 2 * half,
        ),
        name="forward_part",
    )(place, *args)


def once(shape):
    return pl.BlockSpec(shape, lambda i, s: (0, 0), pipeline_mode=pl.Buffered(1))


def store_halves(core, parts, keep, send):
    n, _, rows, cols = parts.shape
    zero = parts[:, 0].reshape(n * rows, cols).astype(BF16)
    one = parts[:, 1].reshape(n * rows, cols).astype(BF16)

    @pl.when(core == 0)
    def _():
        keep[0] = zero
        send[0] = one

    @pl.when(core == 1)
    def _():
        keep[0] = one
        send[0] = zero


def riders(place, scalars, shape):
    line = lax.broadcasted_iota(jnp.int32, shape, 0)
    lane = lax.broadcasted_iota(jnp.int32, shape, 1)
    score = jnp.full(shape, scalars[0], F32)
    out = jnp.where(line == 3, scalars[1], 0.0)
    for i in range(3):
        term = score.astype(BF16).astype(F32)
        out = jnp.where(line == i, term, out)
        score = score - term
    return jnp.where(lane == 2 * place[2] + place[1], out, 0.0)


def early_kernel(place, hidden, resid_grad, residual, grad_rows, scalars, keep, send):
    second = dot(hidden[...], resid_grad[...], ((0,), (0,)))
    head = dot(residual[...], grad_rows[...], ((0,), (0,)))
    width, out_width = second.shape[1], head.shape[1]
    second = second.reshape(RING, 2, RING, -1, width)
    head = head.reshape(RING, 2, RING, -1, out_width)
    blank = riders(place, scalars, (head.shape[3], width - out_width))
    blank = jnp.broadcast_to(blank, (*head.shape[:3], *blank.shape))
    both = jnp.concatenate([second, jnp.concatenate([head, blank], 4)], 3)
    both = both.reshape(RING, 2, -1, width)
    store_halves(place[1], both, keep, send)


def early_grads(place, hidden, resid_grad, residual, grad_rows, scalars):
    rows, hid = hidden.shape
    width, out_width = residual.shape[1], grad_rows.shape[1]
    lines = (hid + width) // RING // 2
    gray = lambda i: 2 * ((i // 2 + i) % 2) + i // 2
    out = pl.BlockSpec((1, lines, width), lambda i, s: (gray(i), 0, 0))
    return pl.pallas_call(
        early_kernel,
        grid_spec=pltpu.PrefetchScalarGridSpec(
            num_scalar_prefetch=1,
            grid=(RING,),
            in_specs=[
                pl.BlockSpec((rows, hid // RING), lambda i, s: (0, i)),
                once((rows, width)),
                pl.BlockSpec((rows, width // RING), lambda i, s: (0, i)),
                once((rows, out_width)),
                pl.BlockSpec(memory_space=pltpu.SMEM),
            ],
            out_specs=[out, out],
        ),
        out_shape=[jax.ShapeDtypeStruct((RING, lines, width), BF16)] * 2,
        compiler_params=params(56),
        cost_estimate=pl.CostEstimate(
            flops=2 * rows * width * (hid + out_width), bytes_accessed=18 * MIB, transcendentals=0
        ),
        name="early_grads",
    )(place, hidden, resid_grad, residual, grad_rows, scalars)


def late_kernel(place, resid_grad, second, slope, tokens, keep, send):
    hidden_grad = dot(resid_grad[...], second[...], ((1,), (1,)))
    preact_grad = (slope[...].astype(F32) * hidden_grad).astype(BF16)
    first = dot(tokens[...], preact_grad, ((0,), (0,)))
    cols = first.shape[1]
    parts = first.reshape(16, 2, RING, -1, cols)
    parts = jnp.stack([parts[:, :, i] for i in (0, 3, 1, 2)], 2)
    store_halves(place[1], parts.reshape(16, 2, -1, cols), keep, send)


def late_grads(place, part, resid_grad, second, slope, tokens):
    rows, width = resid_grad.shape
    tile = 2 * LANES
    steps = width // tile
    out = pl.BlockSpec((1, width // 2, tile), lambda j, s: (0, 0, j))
    return pl.pallas_call(
        late_kernel,
        grid_spec=pltpu.PrefetchScalarGridSpec(
            num_scalar_prefetch=1,
            grid=(steps,),
            in_specs=[
                once((rows, width)),
                pl.BlockSpec((tile, width), lambda j, s: (part * steps + j, 0)),
                pl.BlockSpec((rows, tile), lambda j, s: (0, part * steps + j)),
                once((rows, width)),
            ],
            out_specs=[out, out],
        ),
        out_shape=[jax.ShapeDtypeStruct((1, width // 2, width), BF16)] * 2,
        compiler_params=params(56),
        cost_estimate=pl.CostEstimate(
            flops=4 * rows * width * width, bytes_accessed=12 * MIB, transcendentals=0
        ),
        name="late_grads",
    )(place, resid_grad, second, slope, tokens)


def add(a, b):
    return (a.astype(F32) + b.astype(F32)).astype(BF16)


def take(x, index, axis):
    return lax.dynamic_index_in_dim(x, index, axis, keepdims=False)


def ring_bits(axis):
    here = lax.axis_index(axis)
    high = here // 2
    return (high + here) % 2, high


def ring_chain(axis, low_first):
    low, high = ring_bits(axis)
    if low_first:
        steps = ((PAIR_LOW, low, 0), (PAIR_HIGH, high, 0))
    else:
        steps = ((PAIR_HIGH, high, 1), (PAIR_LOW, low, 0))
    return [(pairs, axis, bit, dim) for pairs, bit, dim in steps]


def outgoing(parts, step):
    return add(*[take(x, 1 - step[2], step[3]) for x in parts])


def staying(parts, step):
    return add(*[take(x, step[2], step[3]) for x in parts])


def sent_along(x, step):
    return lax.ppermute(x, step[1], step[0])


def by_ring(x):
    return x.reshape(16, 2, 2, -1, x.shape[-1]).transpose(1, 2, 0, 3, 4)


def tie(*arrays):
    return lax.optimization_barrier(arrays)


def after(x, *others):
    return lax.optimization_barrier((x, *others))[0]


def pack_kernel(side, first, second, head, a, b):
    width = first.shape[0]
    half = second.shape[0]
    a[:width, :] = first[...]
    for q in range(width // LANES):
        b[q * half : (q + 1) * half, :] = second[:, q * LANES : (q + 1) * LANES]
    a[width:, :] = head[:, :LANES]
    b[width:, :] = head[:, LANES:]


def packed(side, first, second, head):
    width, shard = first.shape
    half = shard // 2
    lines = width + head.shape[0]
    out = pl.BlockSpec((lines, LANES), lambda i, s: (0, 0))
    return pl.pallas_call(
        pack_kernel,
        grid_spec=pltpu.PrefetchScalarGridSpec(
            num_scalar_prefetch=1,
            grid=(1,),
            in_specs=[
                pl.BlockSpec((width, half), lambda i, s: (0, s[0])),
                pl.BlockSpec((half, width), lambda i, s: (s[0], 0)),
                pl.BlockSpec((head.shape[0], width // 2), lambda i, s: (0, s[0])),
            ],
            out_specs=[out, out],
        ),
        out_shape=[jax.ShapeDtypeStruct((lines, LANES), BF16)] * 2,
        compiler_params=params(8),
        name="packed",
    )(side, first, second, head)


def score(samples, target, valid_mask):
    count = samples.shape[0]
    wide = samples.astype(F32)
    gram = jnp.einsum("mpo,npo->pmn", samples, samples, preferred_element_type=F32)
    squares = jnp.sum(wide * wide, axis=2).T
    dist_sq = squares[:, :, None] + squares[:, None, :] - 2.0 * gram
    spread = jnp.sqrt(dist_sq + SMOOTHING)
    kernel = 1.0 / spread
    kernel_sum = jnp.sum(kernel, axis=2)
    pulled = jnp.einsum("pmn,npo->mpo", kernel, wide, precision=lax.Precision.HIGHEST)
    offset = wide - target[None]
    error_norm = jnp.sqrt(jnp.sum(offset * offset, axis=2) + SMOOTHING)
    repulse = wide * kernel_sum.T[:, :, None] - pulled
    validity = valid_mask.astype(F32)
    grad_raw = (
        LOSS_SCALE
        * validity[None, :, None]
        * (offset / (count * error_norm[:, :, None]) - repulse / (count * count))
    ).astype(BF16)
    scores = validity * (
        jnp.mean(error_norm, axis=0) - jnp.sum(spread, axis=(1, 2)) / (2.0 * count * count)
    )
    return grad_raw, jnp.sum(scores), jnp.sum(validity)


def per_device(latents, w_first, w_second, readout_matrix, observed, obs_index, valid_mask):
    members, patches, width = latents.shape
    out_width = observed.shape[1]
    core = lax.axis_index("c")
    here = lax.axis_index("y")
    own = obs_index.shape[0]
    rows = members * patches
    shard = w_first.shape[1]
    half = shard // 2

    side = jnp.reshape(core, (1,)).astype(jnp.int32)
    turned = readout_matrix.T
    own_a, own_b = packed(side, w_first, w_second, turned)
    right_a = shift(own_a, "y", 1)
    left_b = shift(own_b, "y", -1)
    latents, other_side, own_a, own_b = tie(latents, 1 - side, own_a, own_b)
    tokens = (
        latents.reshape(members, 32, own, width).transpose(1, 0, 2, 3).reshape(rows, width)
    )
    place = lambda *offs: jnp.stack(
        [here, core, lax.axis_index("x"), *[(here + off) % RING for off in offs]]
    ).astype(jnp.int32)
    run = functools.partial(forward_part, out_width=out_width)
    swap = lambda x: shift(x, "c", 1)
    packs = (own_a, own_b, *packed(other_side, w_first, w_second, turned))
    carried = run(place(0), tokens, packs, carried=None, last_call=False)
    right_a, left_b, *_ = tie(right_a, left_b, carried[-1])
    left_a = shift(after(own_a, right_a, left_b), "y", -1)
    right_b = shift(after(own_b, right_a, left_b), "y", 1)
    right_a_other, left_b_other = swap(right_a), swap(left_b)
    left_a, right_b, right_a_other, left_b_other = tie(
        left_a, right_b, right_a_other, left_b_other
    )
    far_a = shift(after(right_a, left_a, right_b), "y", 1)
    far_b = shift(after(left_b, left_a, right_b), "y", -1)
    packs = (right_a, right_b, right_a_other, swap(right_b))
    packs = (*packs, left_a, left_b, swap(left_a), left_b_other)
    carried = run(place(3, 1), tokens, packs, carried=carried, last_call=False)
    far_a, far_b, *carried = tie(far_a, far_b, *carried)
    slope, hidden, second, head, residual, forecast = run(
        place(2), tokens, (far_a, far_b, swap(far_a), swap(far_b)), carried=carried, last_call=True
    )

    group = ("x", "z", "c")
    device = ((here * 4 + lax.axis_index("x")) * 4 + lax.axis_index("z")) * 2 + core
    target = jnp.take(observed, obs_index - device * own, axis=0)
    forecast, target = tie(forecast.reshape(32, members * own, out_width), target)
    gathered = lax.all_to_all(forecast, group, 0, 0, tiled=True)
    samples = gathered.reshape(32 * members, own, out_width)
    grad_raw, score_part, count_part = score(samples, target, valid_mask)
    grad_rows = lax.all_to_all(
        grad_raw.reshape(32, members * own, out_width), group, 0, 0, tiled=True
    ).reshape(rows, out_width)

    at = place(0)
    scalars = jnp.stack([score_part, count_part])
    resid_grad = dot(grad_rows, head).astype(BF16)
    early = early_grads(at, hidden, resid_grad, residual, grad_rows, scalars)
    early_in = shift(early[1], "c", 1)
    late = late_grads(at, 0, after(resid_grad, early[1]), second, slope, tokens)
    a_in = shift(late[1], "c", 1)
    x_steps = [ring_chain("x", True), ring_chain("x", False)]
    y_steps = [ring_chain("y", True), ring_chain("y", False)]
    early = [v.reshape(2, 2, 2, -1, width) for v in (after(early[0], late[1]), early_in)]
    early = [[v[:, :, i] for v in early] for i in range(2)]
    early_sent = [outgoing(x, steps[0]) for x, steps in zip(early, x_steps)]
    early_in = [sent_along(x, steps[0]) for x, steps in zip(early_sent, x_steps)]
    a = [by_ring(after(late[0], *early_sent)), by_ring(a_in)]
    a_sent = outgoing(a, y_steps[0][0])
    a_in = sent_along(a_sent, y_steps[0][0])
    early = [staying(x, steps[0]) for x, steps in zip(early, x_steps)]
    a = staying(a, y_steps[0][0])
    late = late_grads(at, 1, after(resid_grad, a_sent), second, slope, tokens)
    b_in = shift(after(late[1], a_in, *early_in), "c", 1)
    a = [a, a_in]
    a_sent = outgoing(a, y_steps[0][1])
    a_in = sent_along(a_sent, y_steps[0][1])
    b = [by_ring(after(late[0], a_sent)), by_ring(b_in)]
    b_sent = outgoing(b, y_steps[1][0])
    b_in = sent_along(b_sent, y_steps[1][0])
    early = [[x, after(v, b_sent)] for x, v in zip(early, early_in)]
    early_sent = [outgoing(x, steps[1]) for x, steps in zip(early, x_steps)]
    early_in = [sent_along(x, steps[1]) for x, steps in zip(early_sent, x_steps)]
    early = [staying(x, steps[1]) for x, steps in zip(early, x_steps)]
    a = staying(a, y_steps[0][1])
    b = [staying(b, y_steps[1][0]), after(b_in, *early_sent)]
    b_sent = outgoing(b, y_steps[1][1])
    b_in = sent_along(b_sent, y_steps[1][1])
    b = staying(b, y_steps[1][1])
    early = [add(x, after(v, b_sent)) for x, v in zip(early, early_in)]
    early = jnp.concatenate(early).reshape(16, -1, width)
    early = lax.all_to_all(early, ("z", "y"), 0, 0, tiled=True)
    late = jnp.concatenate([add(a, a_in), add(b, b_in)], 1)
    late = lax.all_to_all(late, ("x", "z"), 0, 0, tiled=True)
    early = jnp.sum(early.astype(F32), 0)
    late = jnp.sum(late.astype(F32), 0)
    n_second = shard * RING // 128
    ride = jnp.sum(early[n_second : n_second + 8, out_width:], 1)
    score_total = ride[0] + ride[1] + ride[2]
    valid_total = jnp.maximum(ride[3], 1.0)
    scale = 1.0 / valid_total
    n_first = late.shape[0] // 2
    return (
        jnp.concatenate([late[:n_first], late[n_first:]], 1) * scale,
        early[:n_second] * scale,
        early[n_second:, :out_width] * scale,
        score_total / valid_total,
    )


def solution(mesh):
    grid = Mesh(mesh.devices.reshape(4, 4, 2, 4), ("x", "z", "c", "y"))
    rows = P(("y", "x", "z", "c"))
    shares = P(("x", "z", "c", "y"), None)
    return jax.shard_map(
        per_device,
        mesh=grid,
        in_specs=(
            P(("x", "z", "c"), "y", None),
            P(None, "y"),
            P("y", None),
            P(None, "y"),
            rows,
            rows,
            rows,
        ),
        out_specs=(shares, shares, shares, P()),
        check_vma=False,
    )
```

```python
import functools

import jax
import jax.numpy as jnp
from jax import lax
from jax.experimental import pallas as pl
from jax.experimental.pallas import tpu as pltpu
from jax.sharding import Mesh
from jax.sharding import PartitionSpec as P

SMOOTHING = 1.0
LOSS_SCALE = 4096.0
RING = 4
PAIR_LOW = ((0, 1), (1, 0), (2, 3), (3, 2))
PAIR_HIGH = ((0, 3), (3, 0), (1, 2), (2, 1))
ROOT_2_PI = 0.7978845608028654
CUBIC = 0.044715
LANES = 256
MIB = 1 << 20
F32 = jnp.float32
BF16 = jnp.bfloat16


def shift(x, axis, by):
    size = lax.axis_size(axis)
    return lax.ppermute(x, axis, [(i, (i + by) % size) for i in range(size)])


def dot(a, b, contract=((1,), (0,))):
    return lax.dot_general(a, b, (contract, ((), ())), preferred_element_type=F32)


def params(mib):
    return pltpu.CompilerParams(dimension_semantics=("arbitrary",), vmem_limit_bytes=mib * MIB)


def forward_kernel(groups, first_call, last_call, sizes, *refs):
    width, half, head_rows = sizes
    place, tokens = refs[:2]
    packs = [(refs[2 + 4 * g : 4 + 4 * g], refs[4 + 4 * g : 6 + 4 * g]) for g in range(groups)]
    refs = refs[2 + 4 * groups :]
    if first_call:
        slope, hidden, second, head, total = refs
    elif last_call:
        total_in, _, _, _, head_in, slope, hidden, second, head, residual, forecast = refs
    elif groups > 1:
        total_in, _, _, _, _, slope, hidden, second, head, total, kept = refs
    else:
        total_in, _, _, _, _, slope, hidden, second, head, total = refs
    group, step = pl.program_id(0), pl.program_id(1)
    core = place[1]
    chunks = width // LANES
    sides = (core, 1 - core)

    def run(g):
        @pl.when(step == 0)
        def _():
            if last_call:
                head[...] = head_in[...]
            for pair, side in zip(packs[g], sides):
                below = pl.multiple_of(side * half, half)
                for q in range(chunks):
                    second[pl.ds(below, half), q * LANES : (q + 1) * LANES] = pair[1][
                        q * half : (q + 1) * half, :
                    ]
                row = pl.multiple_of(place[3] * head_rows, 64) if last_call else 0
                for e in range(2):
                    lane = pl.multiple_of(side * (width // 2) + e * LANES, LANES)
                    head[pl.ds(row, head_rows), pl.ds(lane, LANES)] = pair[e][width:, :]

        rows = tokens[...]
        count = rows.shape[0]
        line = pl.multiple_of(step * count, count)
        if first_call:
            base = rows.astype(F32)
        elif g == 0:
            base = total_in[...]
        else:
            base = kept[pl.ds(line, count), :]
        sums = [base[:, q * LANES : (q + 1) * LANES] for q in range(chunks)]
        for pair, side in zip(packs[g], sides):
            x = dot(rows, pair[0][:width, :])
            sq = x * x
            t = jnp.tanh(ROOT_2_PI * (x + CUBIC * x * sq))
            up = 0.5 * (1.0 + t)
            active = (x * up).astype(BF16)
            lane = pl.multiple_of(side * half, half)
            turn = up + (0.5 * ROOT_2_PI) * x * (1.0 - t * t) * (1.0 + (3.0 * CUBIC) * sq)
            slope[:, pl.ds(lane, half)] = turn.astype(BF16)
            hidden[:, pl.ds(lane, half)] = active
            for q in range(chunks):
                sums[q] = sums[q] + dot(active, pair[1][q * half : (q + 1) * half, :])
        full = jnp.concatenate(sums, 1)
        if last_call:
            rounded = full.astype(BF16)
            residual[...] = rounded
            forecast[...] = dot(rounded, head[...], ((1,), (1,))).astype(BF16)
        elif g + 1 < groups:
            kept[pl.ds(line, count), :] = full
        else:
            total[...] = full

    for g in range(groups):
        if groups == 1:
            run(g)
        else:
            pl.when(group == g)(functools.partial(run, g))


def forward_part(place, tokens, packs, carried, out_width, last_call):
    rows, width = tokens.shape
    groups = len(packs) // 4
    half = LANES
    hid = 2 * half * RING
    head_rows = out_width // RING
    first_call = carried is None
    block_rows = min(rows, 256)
    whole = lambda shape: pl.BlockSpec(
        shape, lambda g, i, s: (0,) * len(shape), pipeline_mode=pl.Buffered(1)
    )
    by_rows = lambda cols: pl.BlockSpec((block_rows, cols), lambda g, i, s: (i, 0))
    last_of = rows // block_rows - 1
    entering = pl.BlockSpec(
        (block_rows, width), lambda g, i, s: (jnp.where(g == 0, i, last_of), 0)
    )
    leaving = pl.BlockSpec(
        (block_rows, width), lambda g, i, s: (jnp.where(g == groups - 1, i, 0), 0)
    )
    in_place = pl.BlockSpec(memory_space=pl.ANY)
    in_specs = [by_rows(width), *[whole(p.shape) for p in packs]]
    args = [tokens, *packs]
    aliases = {}
    if not first_call:
        slope, hidden, second, head, total = carried
        at = 1 + len(args)
        args += [total, slope, hidden, second, head]
        in_specs += [entering, in_place, in_place, in_place]
        in_specs += [whole((out_width, width)) if last_call else in_place]
        aliases = {at + 1: 0, at + 2: 1, at + 3: 2}
        if not last_call:
            aliases = {**aliases, at + 4: 3}
    column = pl.BlockSpec((block_rows, 2 * half), lambda g, i, s: (i, s[3 + g]))
    out_specs = [
        column,
        column,
        pl.BlockSpec((2 * half, width), lambda g, i, s: (s[3 + g], 0)),
        whole((out_width, width))
        if last_call
        else pl.BlockSpec((head_rows, width), lambda g, i, s: (s[3 + g], 0)),
    ]
    out_shape = [
        jax.ShapeDtypeStruct((rows, hid), BF16),
        jax.ShapeDtypeStruct((rows, hid), BF16),
        jax.ShapeDtypeStruct((hid, width), BF16),
        jax.ShapeDtypeStruct((out_width, width), BF16),
    ]
    if last_call:
        out_specs += [by_rows(width), by_rows(out_width)]
        out_shape += [
            jax.ShapeDtypeStruct((rows, width), BF16),
            jax.ShapeDtypeStruct((rows, out_width), BF16),
        ]
    else:
        out_specs += [leaving]
        out_shape += [jax.ShapeDtypeStruct((rows, width), F32)]
    return pl.pallas_call(
        functools.partial(
            forward_kernel, groups, first_call, last_call, (width, half, head_rows)
        ),
        grid_spec=pltpu.PrefetchScalarGridSpec(
            num_scalar_prefetch=1,
            grid=(groups, rows // block_rows),
            in_specs=in_specs,
            out_specs=out_specs,
            scratch_shapes=[pltpu.VMEM((rows, width), F32)] if groups > 1 else [],
        ),
        out_shape=out_shape,
        input_output_aliases=aliases,
        compiler_params=pltpu.CompilerParams(
            dimension_semantics=("arbitrary",) * 2, vmem_limit_bytes=56 * MIB
        ),
        cost_estimate=pl.CostEstimate(
            flops=8 * groups * rows * width * half,
            bytes_accessed=12 * MIB,
            transcendentals=groups * rows * 2 * half,
        ),
        name="forward_part",
    )(place, *args)


def once(shape):
    return pl.BlockSpec(shape, lambda i, s: (0, 0), pipeline_mode=pl.Buffered(1))


def store_halves(core, parts, keep, send):
    n, _, rows, cols = parts.shape
    zero = parts[:, 0].reshape(n * rows, cols).astype(BF16)
    one = parts[:, 1].reshape(n * rows, cols).astype(BF16)

    @pl.when(core == 0)
    def _():
        keep[0] = zero
        send[0] = one

    @pl.when(core == 1)
    def _():
        keep[0] = one
        send[0] = zero


def riders(place, scalars, shape):
    line = lax.broadcasted_iota(jnp.int32, shape, 0)
    lane = lax.broadcasted_iota(jnp.int32, shape, 1)
    score = jnp.full(shape, scalars[0], F32)
    out = jnp.where(line == 3, scalars[1], 0.0)
    for i in range(3):
        term = score.astype(BF16).astype(F32)
        out = jnp.where(line == i, term, out)
        score = score - term
    return jnp.where(lane == 2 * place[0] + place[1], out, 0.0)


def early_kernel(place, hidden, resid_grad, residual, grad_rows, scalars, keep, send):
    second = dot(hidden[...], resid_grad[...], ((0,), (0,)))
    head = dot(residual[...], grad_rows[...], ((0,), (0,)))
    width, out_width = second.shape[1], head.shape[1]
    second = second.reshape(RING, 2, RING, -1, width)
    head = head.reshape(RING, 2, RING, -1, out_width)
    blank = riders(place, scalars, (head.shape[3], width - out_width))
    blank = jnp.broadcast_to(blank, (*head.shape[:3], *blank.shape))
    both = jnp.concatenate([second, jnp.concatenate([head, blank], 4)], 3)
    both = jnp.stack([both[:, :, i] for i in (0, 3, 1, 2)], 2)
    store_halves(place[1], both.reshape(RING, 2, -1, width), keep, send)


def early_grads(place, hidden, resid_grad, residual, grad_rows, scalars):
    rows, hid = hidden.shape
    width, out_width = residual.shape[1], grad_rows.shape[1]
    lines = (hid + width) // RING // 2
    out = pl.BlockSpec((1, lines, width), lambda i, s: (i, 0, 0))
    return pl.pallas_call(
        early_kernel,
        grid_spec=pltpu.PrefetchScalarGridSpec(
            num_scalar_prefetch=1,
            grid=(RING,),
            in_specs=[
                pl.BlockSpec((rows, hid // RING), lambda i, s: (0, i)),
                once((rows, width)),
                pl.BlockSpec((rows, width // RING), lambda i, s: (0, i)),
                once((rows, out_width)),
                pl.BlockSpec(memory_space=pltpu.SMEM),
            ],
            out_specs=[out, out],
        ),
        out_shape=[jax.ShapeDtypeStruct((RING, lines, width), BF16)] * 2,
        compiler_params=params(56),
        cost_estimate=pl.CostEstimate(
            flops=2 * rows * width * (hid + out_width), bytes_accessed=18 * MIB, transcendentals=0
        ),
        name="early_grads",
    )(place, hidden, resid_grad, residual, grad_rows, scalars)


def late_kernel(place, resid_grad, second, slope, tokens, keep, send):
    hidden_grad = dot(resid_grad[...], second[...], ((1,), (1,)))
    preact_grad = (slope[...].astype(F32) * hidden_grad).astype(BF16)
    first = dot(tokens[...], preact_grad, ((0,), (0,)))
    cols = first.shape[1]
    store_halves(place[1], first.reshape(16, 2, -1, cols), keep, send)


def late_grads(place, part, resid_grad, second, slope, tokens):
    rows, width = resid_grad.shape
    tile = 2 * LANES
    steps = width // tile
    out = pl.BlockSpec((1, width // 2, tile), lambda j, s: (0, 0, j))
    return pl.pallas_call(
        late_kernel,
        grid_spec=pltpu.PrefetchScalarGridSpec(
            num_scalar_prefetch=1,
            grid=(steps,),
            in_specs=[
                once((rows, width)),
                pl.BlockSpec((tile, width), lambda j, s: (part * steps + j, 0)),
                pl.BlockSpec((rows, tile), lambda j, s: (0, part * steps + j)),
                once((rows, width)),
            ],
            out_specs=[out, out],
        ),
        out_shape=[jax.ShapeDtypeStruct((1, width // 2, width), BF16)] * 2,
        compiler_params=params(56),
        cost_estimate=pl.CostEstimate(
            flops=4 * rows * width * width, bytes_accessed=12 * MIB, transcendentals=0
        ),
        name="late_grads",
    )(place, resid_grad, second, slope, tokens)


def add(a, b):
    return (a.astype(F32) + b.astype(F32)).astype(BF16)


def take(x, index, axis):
    return lax.dynamic_index_in_dim(x, index, axis, keepdims=False)


def ring_bits(axis):
    here = lax.axis_index(axis)
    high = here // 2
    return (high + here) % 2, high


def ring_chain(axis, low_first):
    low, high = ring_bits(axis)
    if low_first:
        steps = ((PAIR_LOW, low, 0), (PAIR_HIGH, high, 0))
    else:
        steps = ((PAIR_HIGH, high, 1), (PAIR_LOW, low, 0))
    return [(pairs, axis, bit, dim) for pairs, bit, dim in steps]


def outgoing(x, step):
    return take(x, 1 - step[2], step[3])


def sent_along(x, step):
    return lax.ppermute(x, step[1], step[0])


def kept_plus(x, arrived, step):
    return add(take(x, step[2], step[3]), arrived)


def by_ring(x, lines):
    return x.reshape(-1, 2, 2, lines, x.shape[-1]).transpose(1, 2, 0, 3, 4)


def summed_over_y(x):
    here = lax.axis_index("y")
    total = take(x, here, 1)
    for by in range(1, RING):
        total = total + shift(take(x, (here + by) % RING, 1), "y", by)
    return total


def tie(*arrays):
    return lax.optimization_barrier(arrays)


def after(x, *others):
    return lax.optimization_barrier((x, *others))[0]


def pack_kernel(side, first, second, head, a, b):
    width = first.shape[0]
    half = second.shape[0]
    a[:width, :] = first[...]
    for q in range(width // LANES):
        b[q * half : (q + 1) * half, :] = second[:, q * LANES : (q + 1) * LANES]
    a[width:, :] = head[:, :LANES]
    b[width:, :] = head[:, LANES:]


def packed(side, first, second, head):
    width, shard = first.shape
    half = shard // 2
    lines = width + head.shape[0]
    out = pl.BlockSpec((lines, LANES), lambda i, s: (0, 0))
    return pl.pallas_call(
        pack_kernel,
        grid_spec=pltpu.PrefetchScalarGridSpec(
            num_scalar_prefetch=1,
            grid=(1,),
            in_specs=[
                pl.BlockSpec((width, half), lambda i, s: (0, s[0])),
                pl.BlockSpec((half, width), lambda i, s: (s[0], 0)),
                pl.BlockSpec((head.shape[0], width // 2), lambda i, s: (0, s[0])),
            ],
            out_specs=[out, out],
        ),
        out_shape=[jax.ShapeDtypeStruct((lines, LANES), BF16)] * 2,
        compiler_params=params(8),
        name="packed",
    )(side, first, second, head)


def score(samples, target, valid_mask):
    count = samples.shape[0]
    wide = samples.astype(F32)
    gram = jnp.einsum("mpo,npo->pmn", samples, samples, preferred_element_type=F32)
    squares = jnp.sum(wide * wide, axis=2).T
    dist_sq = squares[:, :, None] + squares[:, None, :] - 2.0 * gram
    spread = jnp.sqrt(dist_sq + SMOOTHING)
    kernel = 1.0 / spread
    kernel_sum = jnp.sum(kernel, axis=2)
    pulled = jnp.einsum("pmn,npo->mpo", kernel, wide, precision=lax.Precision.HIGHEST)
    offset = wide - target[None]
    error_norm = jnp.sqrt(jnp.sum(offset * offset, axis=2) + SMOOTHING)
    repulse = wide * kernel_sum.T[:, :, None] - pulled
    validity = valid_mask.astype(F32)
    grad_raw = (
        LOSS_SCALE
        * validity[None, :, None]
        * (offset / (count * error_norm[:, :, None]) - repulse / (count * count))
    ).astype(BF16)
    scores = validity * (
        jnp.mean(error_norm, axis=0) - jnp.sum(spread, axis=(1, 2)) / (2.0 * count * count)
    )
    return grad_raw, jnp.sum(scores), jnp.sum(validity)


def per_device(latents, w_first, w_second, readout_matrix, observed, obs_index, valid_mask):
    members, patches, width = latents.shape
    out_width = observed.shape[1]
    core = lax.axis_index("c")
    here = lax.axis_index("y")
    own = obs_index.shape[0]
    rows = members * patches
    shard = w_first.shape[1]
    half = shard // 2

    side = jnp.reshape(core, (1,)).astype(jnp.int32)
    turned = readout_matrix.T
    own_a, own_b = packed(side, w_first, w_second, turned)
    right_a = shift(own_a, "y", 1)
    left_b = shift(own_b, "y", -1)
    latents, other_side, own_a, own_b = tie(latents, 1 - side, own_a, own_b)
    tokens = (
        latents.reshape(members, 32, own, width).transpose(1, 0, 2, 3).reshape(rows, width)
    )
    place = lambda *offs: jnp.stack(
        [here, core, lax.axis_index("x"), *[(here + off) % RING for off in offs]]
    ).astype(jnp.int32)
    run = functools.partial(forward_part, out_width=out_width)
    swap = lambda x: shift(x, "c", 1)
    packs = (own_a, own_b, *packed(other_side, w_first, w_second, turned))
    carried = run(place(0), tokens, packs, carried=None, last_call=False)
    right_a, left_b, *_ = tie(right_a, left_b, carried[-1])
    left_a = shift(after(own_a, right_a, left_b), "y", -1)
    right_b = shift(after(own_b, right_a, left_b), "y", 1)
    right_a_other, left_b_other = swap(right_a), swap(left_b)
    left_a, right_b, right_a_other, left_b_other = tie(
        left_a, right_b, right_a_other, left_b_other
    )
    far_a = shift(after(right_a, left_a, right_b), "y", 1)
    far_b = shift(after(left_b, left_a, right_b), "y", -1)
    packs = (right_a, right_b, right_a_other, swap(right_b))
    packs = (*packs, left_a, left_b, swap(left_a), left_b_other)
    carried = run(place(3, 1), tokens, packs, carried=carried, last_call=False)
    far_a, far_b, *carried = tie(far_a, far_b, *carried)
    slope, hidden, second, head, residual, forecast = run(
        place(2), tokens, (far_a, far_b, swap(far_a), swap(far_b)), carried=carried, last_call=True
    )

    group = ("x", "z", "c")
    device = ((here * 4 + lax.axis_index("x")) * 4 + lax.axis_index("z")) * 2 + core
    target = jnp.take(observed, obs_index - device * own, axis=0)
    forecast, target = tie(forecast.reshape(32, members * own, out_width), target)
    gathered = lax.all_to_all(forecast, group, 0, 0, tiled=True)
    samples = gathered.reshape(32 * members, own, out_width)
    grad_raw, score_part, count_part = score(samples, target, valid_mask)
    grad_rows = lax.all_to_all(
        grad_raw.reshape(32, members * own, out_width), group, 0, 0, tiled=True
    ).reshape(rows, out_width)

    at = place(0)
    scalars = jnp.stack([score_part, count_part])
    resid_grad = dot(grad_rows, head).astype(BF16)
    early = early_grads(at, hidden, resid_grad, residual, grad_rows, scalars)
    early_in = shift(early[1], "c", 1)
    late = late_grads(at, 0, after(resid_grad, early[1]), second, slope, tokens)
    a_in = shift(late[1], "c", 1)
    steps = [ring_chain("y", True), ring_chain("y", False)]
    group = ("x", "z")
    n = width // 128
    early = add(after(early[0], late[1]), early_in)
    lines = early.shape[1] // 16
    early = [by_ring(v, lines) for v in (early[:2], early[2:])]
    early_sent = [outgoing(x, s[0]) for x, s in zip(early, steps)]
    early_in = [sent_along(x, s[0]) for x, s in zip(early_sent, steps)]
    a = add(after(late[0], *early_sent), a_in).reshape(16, RING * n, width)
    a_all = lax.all_to_all(a, group, 0, 0, tiled=True)
    late = late_grads(at, 1, after(resid_grad, a), second, slope, tokens)
    b_in = shift(after(late[1], a_all, *early_in), "c", 1)
    early = [kept_plus(x, v, s[0]) for x, v, s in zip(early, early_in, steps)]
    early_sent = [outgoing(x, s[1]) for x, s in zip(early, steps)]
    early_in = [sent_along(x, s[1]) for x, s in zip(early_sent, steps)]
    b = add(after(late[0], *early_sent), b_in).reshape(16, RING * n, width)
    b_all = lax.all_to_all(b, group, 0, 0, tiled=True)
    a = jnp.sum(after(a_all, b).astype(F32), 0)
    early = [kept_plus(x, after(v, b), s[1]) for x, v, s in zip(early, early_in, steps)]
    early = jnp.concatenate(early)
    b = jnp.sum(b_all.astype(F32), 0)
    early = lax.all_to_all(after(early, b_all), group, 0, 0, tiled=True)
    first = summed_over_y(jnp.stack([a, b]).reshape(2, RING, n, width))
    early = jnp.sum(early.astype(F32), 0)
    n_second = shard * RING // 128
    ride = jnp.sum(early[n_second:, out_width:], 1)
    score_total = ride[0] + ride[1] + ride[2]
    valid_total = jnp.maximum(ride[3], 1.0)
    scale = 1.0 / valid_total
    return (
        jnp.concatenate([first[0], first[1]], 1) * scale,
        early[:n_second] * scale,
        early[n_second:, :out_width] * scale,
        score_total / valid_total,
    )


def solution(mesh):
    grid = Mesh(mesh.devices.reshape(4, 4, 2, 4), ("x", "z", "c", "y"))
    rows = P(("y", "x", "z", "c"))
    shares = P(("x", "z", "c", "y"), None)
    return jax.shard_map(
        per_device,
        mesh=grid,
        in_specs=(
            P(("x", "z", "c"), "y", None),
            P(None, "y"),
            P("y", None),
            P(None, "y"),
            rows,
            rows,
            rows,
        ),
        out_specs=(shares, shares, shares, P()),
        check_vma=False,
    )
```

```python
import functools

import jax
import jax.numpy as jnp
from jax import lax
from jax.experimental import pallas as pl
from jax.experimental.pallas import tpu as pltpu
from jax.sharding import Mesh
from jax.sharding import PartitionSpec as P

SMOOTHING = 1.0
LOSS_SCALE = 4096.0
RING = 4
PAIR_LOW = ((0, 1), (1, 0), (2, 3), (3, 2))
PAIR_HIGH = ((0, 3), (3, 0), (1, 2), (2, 1))
ROOT_2_PI = 0.7978845608028654
CUBIC = 0.044715
LANES = 256
MIB = 1 << 20
F32 = jnp.float32
BF16 = jnp.bfloat16


def shift(x, axis, by):
    size = lax.axis_size(axis)
    return lax.ppermute(x, axis, [(i, (i + by) % size) for i in range(size)])


def dot(a, b, contract=((1,), (0,))):
    return lax.dot_general(a, b, (contract, ((), ())), preferred_element_type=F32)


def params(mib):
    return pltpu.CompilerParams(dimension_semantics=("arbitrary",), vmem_limit_bytes=mib * MIB)


def forward_kernel(groups, first_call, last_call, sizes, *refs):
    width, half, head_rows = sizes
    place, tokens = refs[:2]
    packs = [(refs[2 + 4 * g : 4 + 4 * g], refs[4 + 4 * g : 6 + 4 * g]) for g in range(groups)]
    refs = refs[2 + 4 * groups :]
    if first_call:
        slope, hidden, second, head, total = refs
    elif last_call:
        total_in, _, _, _, head_in, slope, hidden, second, head, residual, forecast = refs
    elif groups > 1:
        total_in, _, _, _, _, slope, hidden, second, head, total, kept = refs
    else:
        total_in, _, _, _, _, slope, hidden, second, head, total = refs
    group, step = pl.program_id(0), pl.program_id(1)
    core = place[1]
    chunks = width // LANES
    sides = (core, 1 - core)

    def run(g):
        @pl.when(step == 0)
        def _():
            if last_call:
                head[...] = head_in[...]
            for pair, side in zip(packs[g], sides):
                below = pl.multiple_of(side * half, half)
                for q in range(chunks):
                    second[pl.ds(below, half), q * LANES : (q + 1) * LANES] = pair[1][
                        q * half : (q + 1) * half, :
                    ]
                row = pl.multiple_of(place[3] * head_rows, 64) if last_call else 0
                for e in range(2):
                    lane = pl.multiple_of(side * (width // 2) + e * LANES, LANES)
                    head[pl.ds(row, head_rows), pl.ds(lane, LANES)] = pair[e][width:, :]

        rows = tokens[...]
        count = rows.shape[0]
        line = pl.multiple_of(step * count, count)
        if first_call:
            base = rows.astype(F32)
        elif g == 0:
            base = total_in[...]
        else:
            base = kept[pl.ds(line, count), :]
        sums = [base[:, q * LANES : (q + 1) * LANES] for q in range(chunks)]
        for pair, side in zip(packs[g], sides):
            x = dot(rows, pair[0][:width, :])
            sq = x * x
            t = jnp.tanh(ROOT_2_PI * (x + CUBIC * x * sq))
            up = 0.5 * (1.0 + t)
            active = (x * up).astype(BF16)
            lane = pl.multiple_of(side * half, half)
            turn = up + (0.5 * ROOT_2_PI) * x * (1.0 - t * t) * (1.0 + (3.0 * CUBIC) * sq)
            slope[:, pl.ds(lane, half)] = turn.astype(BF16)
            hidden[:, pl.ds(lane, half)] = active
            for q in range(chunks):
                sums[q] = sums[q] + dot(active, pair[1][q * half : (q + 1) * half, :])
        full = jnp.concatenate(sums, 1)
        if last_call:
            rounded = full.astype(BF16)
            residual[...] = rounded
            forecast[...] = dot(rounded, head[...], ((1,), (1,))).astype(BF16)
        elif g + 1 < groups:
            kept[pl.ds(line, count), :] = full
        else:
            total[...] = full

    for g in range(groups):
        if groups == 1:
            run(g)
        else:
            pl.when(group == g)(functools.partial(run, g))


def forward_part(place, tokens, packs, carried, out_width, last_call):
    rows, width = tokens.shape
    groups = len(packs) // 4
    half = LANES
    hid = 2 * half * RING
    head_rows = out_width // RING
    first_call = carried is None
    block_rows = min(rows, 256)
    whole = lambda shape: pl.BlockSpec(
        shape, lambda g, i, s: (0,) * len(shape), pipeline_mode=pl.Buffered(1)
    )
    by_rows = lambda cols: pl.BlockSpec((block_rows, cols), lambda g, i, s: (i, 0))
    last_of = rows // block_rows - 1
    entering = pl.BlockSpec(
        (block_rows, width), lambda g, i, s: (jnp.where(g == 0, i, last_of), 0)
    )
    leaving = pl.BlockSpec(
        (block_rows, width), lambda g, i, s: (jnp.where(g == groups - 1, i, 0), 0)
    )
    in_place = pl.BlockSpec(memory_space=pl.ANY)
    in_specs = [by_rows(width), *[whole(p.shape) for p in packs]]
    args = [tokens, *packs]
    aliases = {}
    if not first_call:
        slope, hidden, second, head, total = carried
        at = 1 + len(args)
        args += [total, slope, hidden, second, head]
        in_specs += [entering, in_place, in_place, in_place]
        in_specs += [whole((out_width, width)) if last_call else in_place]
        aliases = {at + 1: 0, at + 2: 1, at + 3: 2}
        if not last_call:
            aliases = {**aliases, at + 4: 3}
    column = pl.BlockSpec((block_rows, 2 * half), lambda g, i, s: (i, s[3 + g]))
    out_specs = [
        column,
        column,
        pl.BlockSpec((2 * half, width), lambda g, i, s: (s[3 + g], 0)),
        whole((out_width, width))
        if last_call
        else pl.BlockSpec((head_rows, width), lambda g, i, s: (s[3 + g], 0)),
    ]
    out_shape = [
        jax.ShapeDtypeStruct((rows, hid), BF16),
        jax.ShapeDtypeStruct((rows, hid), BF16),
        jax.ShapeDtypeStruct((hid, width), BF16),
        jax.ShapeDtypeStruct((out_width, width), BF16),
    ]
    if last_call:
        out_specs += [by_rows(width), by_rows(out_width)]
        out_shape += [
            jax.ShapeDtypeStruct((rows, width), BF16),
            jax.ShapeDtypeStruct((rows, out_width), BF16),
        ]
    else:
        out_specs += [leaving]
        out_shape += [jax.ShapeDtypeStruct((rows, width), F32)]
    return pl.pallas_call(
        functools.partial(
            forward_kernel, groups, first_call, last_call, (width, half, head_rows)
        ),
        grid_spec=pltpu.PrefetchScalarGridSpec(
            num_scalar_prefetch=1,
            grid=(groups, rows // block_rows),
            in_specs=in_specs,
            out_specs=out_specs,
            scratch_shapes=[pltpu.VMEM((rows, width), F32)] if groups > 1 else [],
        ),
        out_shape=out_shape,
        input_output_aliases=aliases,
        compiler_params=pltpu.CompilerParams(
            dimension_semantics=("arbitrary",) * 2, vmem_limit_bytes=56 * MIB
        ),
        cost_estimate=pl.CostEstimate(
            flops=8 * groups * rows * width * half,
            bytes_accessed=12 * MIB,
            transcendentals=groups * rows * 2 * half,
        ),
        name="forward_part",
    )(place, *args)


def once(shape):
    return pl.BlockSpec(shape, lambda i, s: (0, 0), pipeline_mode=pl.Buffered(1))


def store_halves(core, parts, keep, send):
    n, _, rows, cols = parts.shape
    zero = parts[:, 0].reshape(n * rows, cols).astype(BF16)
    one = parts[:, 1].reshape(n * rows, cols).astype(BF16)

    @pl.when(core == 0)
    def _():
        keep[0] = zero
        send[0] = one

    @pl.when(core == 1)
    def _():
        keep[0] = one
        send[0] = zero


def riders(place, scalars, shape):
    line = lax.broadcasted_iota(jnp.int32, shape, 0)
    lane = lax.broadcasted_iota(jnp.int32, shape, 1)
    score = jnp.full(shape, scalars[0], F32)
    out = jnp.where(line == 3, scalars[1], 0.0)
    for i in range(3):
        term = score.astype(BF16).astype(F32)
        out = jnp.where(line == i, term, out)
        score = score - term
    return jnp.where(lane == 2 * place[0] + place[1], out, 0.0)


def early_kernel(place, hidden, resid_grad, residual, grad_rows, scalars, keep, send):
    second = dot(hidden[...], resid_grad[...], ((0,), (0,)))
    head = dot(residual[...], grad_rows[...], ((0,), (0,)))
    width, out_width = second.shape[1], head.shape[1]
    second = second.reshape(RING, 2, RING, -1, width)
    head = head.reshape(RING, 2, RING, -1, out_width)
    blank = riders(place, scalars, (head.shape[3], width - out_width))
    blank = jnp.broadcast_to(blank, (*head.shape[:3], *blank.shape))
    both = jnp.concatenate([second, jnp.concatenate([head, blank], 4)], 3)
    both = jnp.stack([both[:, :, i] for i in (0, 3, 1, 2)], 2)
    store_halves(place[1], both.reshape(RING, 2, -1, width), keep, send)


def early_grads(place, hidden, resid_grad, residual, grad_rows, scalars):
    rows, hid = hidden.shape
    width, out_width = residual.shape[1], grad_rows.shape[1]
    lines = (hid + width) // RING // 2
    out = pl.BlockSpec((1, lines, width), lambda i, s: (i, 0, 0))
    return pl.pallas_call(
        early_kernel,
        grid_spec=pltpu.PrefetchScalarGridSpec(
            num_scalar_prefetch=1,
            grid=(RING,),
            in_specs=[
                pl.BlockSpec((rows, hid // RING), lambda i, s: (0, i)),
                once((rows, width)),
                pl.BlockSpec((rows, width // RING), lambda i, s: (0, i)),
                once((rows, out_width)),
                pl.BlockSpec(memory_space=pltpu.SMEM),
            ],
            out_specs=[out, out],
        ),
        out_shape=[jax.ShapeDtypeStruct((RING, lines, width), BF16)] * 2,
        compiler_params=params(56),
        cost_estimate=pl.CostEstimate(
            flops=2 * rows * width * (hid + out_width), bytes_accessed=18 * MIB, transcendentals=0
        ),
        name="early_grads",
    )(place, hidden, resid_grad, residual, grad_rows, scalars)


def late_kernel(place, resid_grad, second, slope, tokens, keep, send):
    hidden_grad = dot(resid_grad[...], second[...], ((1,), (1,)))
    preact_grad = (slope[...].astype(F32) * hidden_grad).astype(BF16)
    first = dot(tokens[...], preact_grad, ((0,), (0,)))
    cols = first.shape[1]
    store_halves(place[1], first.reshape(16, 2, -1, cols), keep, send)


def late_grads(place, part, resid_grad, second, slope, tokens):
    rows, width = resid_grad.shape
    tile = 2 * LANES
    steps = width // tile
    out = pl.BlockSpec((1, width // 2, tile), lambda j, s: (0, 0, j))
    return pl.pallas_call(
        late_kernel,
        grid_spec=pltpu.PrefetchScalarGridSpec(
            num_scalar_prefetch=1,
            grid=(steps,),
            in_specs=[
                once((rows, width)),
                pl.BlockSpec((tile, width), lambda j, s: (part * steps + j, 0)),
                pl.BlockSpec((rows, tile), lambda j, s: (0, part * steps + j)),
                once((rows, width)),
            ],
            out_specs=[out, out],
        ),
        out_shape=[jax.ShapeDtypeStruct((1, width // 2, width), BF16)] * 2,
        compiler_params=params(56),
        cost_estimate=pl.CostEstimate(
            flops=4 * rows * width * width, bytes_accessed=12 * MIB, transcendentals=0
        ),
        name="late_grads",
    )(place, resid_grad, second, slope, tokens)


def add(a, b):
    return (a.astype(F32) + b.astype(F32)).astype(BF16)


def take(x, index, axis):
    return lax.dynamic_index_in_dim(x, index, axis, keepdims=False)


def ring_bits(axis):
    here = lax.axis_index(axis)
    high = here // 2
    return (high + here) % 2, high


def ring_chain(axis, low_first):
    low, high = ring_bits(axis)
    if low_first:
        steps = ((PAIR_LOW, low, 0), (PAIR_HIGH, high, 0))
    else:
        steps = ((PAIR_HIGH, high, 1), (PAIR_LOW, low, 0))
    return [(pairs, axis, bit, dim) for pairs, bit, dim in steps]


def outgoing(x, step):
    return take(x, 1 - step[2], step[3])


def sent_along(x, step):
    return lax.ppermute(x, step[1], step[0])


def kept_plus(x, arrived, step):
    return add(take(x, step[2], step[3]), arrived)


def by_ring(x, lines):
    return x.reshape(-1, 2, 2, lines, x.shape[-1]).transpose(1, 2, 0, 3, 4)


def summed_over_y(x):
    here = lax.axis_index("y")
    total = take(x, here, 1)
    for by in range(1, RING):
        total = total + shift(take(x, (here + by) % RING, 1), "y", by)
    return total


def tie(*arrays):
    return lax.optimization_barrier(arrays)


def after(x, *others):
    return lax.optimization_barrier((x, *others))[0]


def pack_kernel(side, first, second, head, a, b):
    width = first.shape[0]
    half = second.shape[0]
    a[:width, :] = first[...]
    for q in range(width // LANES):
        b[q * half : (q + 1) * half, :] = second[:, q * LANES : (q + 1) * LANES]
    a[width:, :] = head[:, :LANES]
    b[width:, :] = head[:, LANES:]


def packed(side, first, second, head):
    width, shard = first.shape
    half = shard // 2
    lines = width + head.shape[0]
    out = pl.BlockSpec((lines, LANES), lambda i, s: (0, 0))
    return pl.pallas_call(
        pack_kernel,
        grid_spec=pltpu.PrefetchScalarGridSpec(
            num_scalar_prefetch=1,
            grid=(1,),
            in_specs=[
                pl.BlockSpec((width, half), lambda i, s: (0, s[0])),
                pl.BlockSpec((half, width), lambda i, s: (s[0], 0)),
                pl.BlockSpec((head.shape[0], width // 2), lambda i, s: (0, s[0])),
            ],
            out_specs=[out, out],
        ),
        out_shape=[jax.ShapeDtypeStruct((lines, LANES), BF16)] * 2,
        compiler_params=params(8),
        name="packed",
    )(side, first, second, head)


def score(samples, target, valid_mask):
    count = samples.shape[0]
    wide = samples.astype(F32)
    gram = jnp.einsum("mpo,npo->pmn", samples, samples, preferred_element_type=F32)
    squares = jnp.sum(wide * wide, axis=2).T
    dist_sq = squares[:, :, None] + squares[:, None, :] - 2.0 * gram
    spread = jnp.sqrt(dist_sq + SMOOTHING)
    kernel = 1.0 / spread
    kernel_sum = jnp.sum(kernel, axis=2)
    pulled = jnp.einsum("pmn,npo->mpo", kernel, wide, precision=lax.Precision.HIGHEST)
    offset = wide - target[None]
    error_norm = jnp.sqrt(jnp.sum(offset * offset, axis=2) + SMOOTHING)
    repulse = wide * kernel_sum.T[:, :, None] - pulled
    validity = valid_mask.astype(F32)
    grad_raw = (
        LOSS_SCALE
        * validity[None, :, None]
        * (offset / (count * error_norm[:, :, None]) - repulse / (count * count))
    ).astype(BF16)
    scores = validity * (
        jnp.mean(error_norm, axis=0) - jnp.sum(spread, axis=(1, 2)) / (2.0 * count * count)
    )
    return grad_raw, jnp.sum(scores), jnp.sum(validity)


def per_device(latents, w_first, w_second, readout_matrix, observed, obs_index, valid_mask):
    members, patches, width = latents.shape
    out_width = observed.shape[1]
    core = lax.axis_index("c")
    here = lax.axis_index("y")
    own = obs_index.shape[0]
    rows = members * patches
    shard = w_first.shape[1]
    half = shard // 2

    side = jnp.reshape(core, (1,)).astype(jnp.int32)
    turned = readout_matrix.T
    own_a, own_b = packed(side, w_first, w_second, turned)
    right_a = shift(own_a, "y", 1)
    left_b = shift(own_b, "y", -1)
    latents, other_side, own_a, own_b = tie(latents, 1 - side, own_a, own_b)
    tokens = (
        latents.reshape(members, 32, own, width).transpose(1, 0, 2, 3).reshape(rows, width)
    )
    place = lambda *offs: jnp.stack(
        [here, core, lax.axis_index("x"), *[(here + off) % RING for off in offs]]
    ).astype(jnp.int32)
    run = functools.partial(forward_part, out_width=out_width)
    swap = lambda x: shift(x, "c", 1)
    packs = (own_a, own_b, *packed(other_side, w_first, w_second, turned))
    carried = run(place(0), tokens, packs, carried=None, last_call=False)
    right_a, left_b, *_ = tie(right_a, left_b, carried[-1])
    left_a = shift(after(own_a, right_a, left_b), "y", -1)
    right_b = shift(after(own_b, right_a, left_b), "y", 1)
    right_a_other, left_b_other = swap(right_a), swap(left_b)
    left_a, right_b, right_a_other, left_b_other = tie(
        left_a, right_b, right_a_other, left_b_other
    )
    far_a = shift(after(right_a, left_a, right_b), "y", 1)
    far_b = shift(after(left_b, left_a, right_b), "y", -1)
    packs = (right_a, right_b, right_a_other, swap(right_b))
    packs = (*packs, left_a, left_b, swap(left_a), left_b_other)
    carried = run(place(3, 1), tokens, packs, carried=carried, last_call=False)
    far_a, far_b, *carried = tie(far_a, far_b, *carried)
    slope, hidden, second, head, residual, forecast = run(
        place(2), tokens, (far_a, far_b, swap(far_a), swap(far_b)), carried=carried, last_call=True
    )

    group = ("x", "z", "c")
    device = ((here * 4 + lax.axis_index("x")) * 4 + lax.axis_index("z")) * 2 + core
    target = jnp.take(observed, obs_index - device * own, axis=0)
    forecast, target = tie(forecast.reshape(32, members * own, out_width), target)
    gathered = lax.all_to_all(forecast, group, 0, 0, tiled=True)
    samples = gathered.reshape(32 * members, own, out_width)
    grad_raw, score_part, count_part = score(samples, target, valid_mask)
    grad_rows = lax.all_to_all(
        grad_raw.reshape(32, members * own, out_width), group, 0, 0, tiled=True
    ).reshape(rows, out_width)

    at = place(0)
    scalars = jnp.stack([score_part, count_part])
    resid_grad = dot(grad_rows, head).astype(BF16)
    early = early_grads(at, hidden, resid_grad, residual, grad_rows, scalars)
    early_in = shift(early[1], "c", 1)
    late = late_grads(at, 0, after(resid_grad, early[1]), second, slope, tokens)
    a_in = shift(late[1], "c", 1)
    steps = [ring_chain("y", True), ring_chain("y", False)]
    group = ("x", "z")
    n = width // 128
    early = add(after(early[0], late[1]), early_in)
    lines = early.shape[1] // 16
    early = [by_ring(v, lines) for v in (early[:2], early[2:])]
    early_sent = [outgoing(x, s[0]) for x, s in zip(early, steps)]
    early_in = [sent_along(x, s[0]) for x, s in zip(early_sent, steps)]
    a = add(after(late[0], *early_sent), a_in).reshape(16, RING * n, width)
    a_all = lax.all_to_all(a, group, 0, 0, tiled=True)
    late = late_grads(at, 1, after(resid_grad, a), second, slope, tokens)
    b_in = shift(after(late[1], a_all), "c", 1)
    b = add(late[0], b_in).reshape(16, RING * n, width)
    b_all = lax.all_to_all(b, group, 0, 0, tiled=True)
    early = [kept_plus(x, after(v, b), s[0]) for x, v, s in zip(early, early_in, steps)]
    early_sent = [outgoing(x, s[1]) for x, s in zip(early, steps)]
    early_in = [sent_along(x, s[1]) for x, s in zip(early_sent, steps)]
    a = jnp.sum(after(a_all, *early_sent).astype(F32), 0)
    early = [kept_plus(x, v, s[1]) for x, v, s in zip(early, early_in, steps)]
    early = jnp.concatenate(early)
    b = jnp.sum(b_all.astype(F32), 0)
    early = lax.all_to_all(after(early, b_all), group, 0, 0, tiled=True)
    first = summed_over_y(jnp.stack([a, b]).reshape(2, RING, n, width))
    early = jnp.sum(early.astype(F32), 0)
    n_second = shard * RING // 128
    ride = jnp.sum(early[n_second:, out_width:], 1)
    score_total = ride[0] + ride[1] + ride[2]
    valid_total = jnp.maximum(ride[3], 1.0)
    scale = 1.0 / valid_total
    return (
        jnp.concatenate([first[0], first[1]], 1) * scale,
        early[:n_second] * scale,
        early[n_second:, :out_width] * scale,
        score_total / valid_total,
    )


def solution(mesh):
    grid = Mesh(mesh.devices.reshape(4, 4, 2, 4), ("x", "z", "c", "y"))
    rows = P(("y", "x", "z", "c"))
    shares = P(("x", "z", "c", "y"), None)
    return jax.shard_map(
        per_device,
        mesh=grid,
        in_specs=(
            P(("x", "z", "c"), "y", None),
            P(None, "y"),
            P("y", None),
            P(None, "y"),
            rows,
            rows,
            rows,
        ),
        out_specs=(shares, shares, shares, P()),
        check_vma=False,
    )
```

```python
import functools

import jax
import jax.numpy as jnp
from jax import lax
from jax.experimental import pallas as pl
from jax.experimental.pallas import tpu as pltpu
from jax.sharding import Mesh
from jax.sharding import PartitionSpec as P

SMOOTHING = 1.0
LOSS_SCALE = 4096.0
RING = 4
PAIR_LOW = ((0, 1), (1, 0), (2, 3), (3, 2))
PAIR_HIGH = ((0, 3), (3, 0), (1, 2), (2, 1))
ROOT_2_PI = 0.7978845608028654
CUBIC = 0.044715
LANES = 256
MIB = 1 << 20
F32 = jnp.float32
BF16 = jnp.bfloat16


def shift(x, axis, by):
    size = lax.axis_size(axis)
    return lax.ppermute(x, axis, [(i, (i + by) % size) for i in range(size)])


def dot(a, b, contract=((1,), (0,))):
    return lax.dot_general(a, b, (contract, ((), ())), preferred_element_type=F32)


def params(mib):
    return pltpu.CompilerParams(dimension_semantics=("arbitrary",), vmem_limit_bytes=mib * MIB)


def forward_kernel(groups, first_call, last_call, sizes, *refs):
    width, half, head_rows = sizes
    place, tokens = refs[:2]
    packs = [(refs[2 + 4 * g : 4 + 4 * g], refs[4 + 4 * g : 6 + 4 * g]) for g in range(groups)]
    refs = refs[2 + 4 * groups :]
    if first_call:
        slope, hidden, second, head, total = refs
    elif last_call:
        total_in, _, _, _, head_in, slope, hidden, second, head, residual, forecast = refs
    elif groups > 1:
        total_in, _, _, _, _, slope, hidden, second, head, total, kept = refs
    else:
        total_in, _, _, _, _, slope, hidden, second, head, total = refs
    group, step = pl.program_id(0), pl.program_id(1)
    core = place[1]
    chunks = width // LANES
    sides = (core, 1 - core)

    def run(g):
        @pl.when(step == 0)
        def _():
            if last_call:
                head[...] = head_in[...]
            for pair, side in zip(packs[g], sides):
                below = pl.multiple_of(side * half, half)
                for q in range(chunks):
                    second[pl.ds(below, half), q * LANES : (q + 1) * LANES] = pair[1][
                        q * half : (q + 1) * half, :
                    ]
                row = pl.multiple_of(place[3] * head_rows, 64) if last_call else 0
                for e in range(2):
                    lane = pl.multiple_of(side * (width // 2) + e * LANES, LANES)
                    head[pl.ds(row, head_rows), pl.ds(lane, LANES)] = pair[e][width:, :]

        rows = tokens[...]
        count = rows.shape[0]
        line = pl.multiple_of(step * count, count)
        if first_call:
            base = rows.astype(F32)
        elif g == 0:
            base = total_in[...]
        else:
            base = kept[pl.ds(line, count), :]
        sums = [base[:, q * LANES : (q + 1) * LANES] for q in range(chunks)]
        for pair, side in zip(packs[g], sides):
            x = dot(rows, pair[0][:width, :])
            sq = x * x
            t = jnp.tanh(ROOT_2_PI * (x + CUBIC * x * sq))
            up = 0.5 * (1.0 + t)
            active = (x * up).astype(BF16)
            lane = pl.multiple_of(side * half, half)
            turn = up + (0.5 * ROOT_2_PI) * x * (1.0 - t * t) * (1.0 + (3.0 * CUBIC) * sq)
            slope[:, pl.ds(lane, half)] = turn.astype(BF16)
            hidden[:, pl.ds(lane, half)] = active
            for q in range(chunks):
                sums[q] = sums[q] + dot(active, pair[1][q * half : (q + 1) * half, :])
        full = jnp.concatenate(sums, 1)
        if last_call:
            rounded = full.astype(BF16)
            residual[...] = rounded
            forecast[...] = dot(rounded, head[...], ((1,), (1,))).astype(BF16)
        elif g + 1 < groups:
            kept[pl.ds(line, count), :] = full
        else:
            total[...] = full

    for g in range(groups):
        if groups == 1:
            run(g)
        else:
            pl.when(group == g)(functools.partial(run, g))


def forward_part(place, tokens, packs, carried, out_width, last_call):
    rows, width = tokens.shape
    groups = len(packs) // 4
    half = LANES
    hid = 2 * half * RING
    head_rows = out_width // RING
    first_call = carried is None
    block_rows = min(rows, 256)
    whole = lambda shape: pl.BlockSpec(
        shape, lambda g, i, s: (0,) * len(shape), pipeline_mode=pl.Buffered(1)
    )
    by_rows = lambda cols: pl.BlockSpec((block_rows, cols), lambda g, i, s: (i, 0))
    last_of = rows // block_rows - 1
    entering = pl.BlockSpec(
        (block_rows, width), lambda g, i, s: (jnp.where(g == 0, i, last_of), 0)
    )
    leaving = pl.BlockSpec(
        (block_rows, width), lambda g, i, s: (jnp.where(g == groups - 1, i, 0), 0)
    )
    in_place = pl.BlockSpec(memory_space=pl.ANY)
    in_specs = [by_rows(width), *[whole(p.shape) for p in packs]]
    args = [tokens, *packs]
    aliases = {}
    if not first_call:
        slope, hidden, second, head, total = carried
        at = 1 + len(args)
        args += [total, slope, hidden, second, head]
        in_specs += [entering, in_place, in_place, in_place]
        in_specs += [whole((out_width, width)) if last_call else in_place]
        aliases = {at + 1: 0, at + 2: 1, at + 3: 2}
        if not last_call:
            aliases = {**aliases, at + 4: 3}
    column = pl.BlockSpec((block_rows, 2 * half), lambda g, i, s: (i, s[3 + g]))
    out_specs = [
        column,
        column,
        pl.BlockSpec((2 * half, width), lambda g, i, s: (s[3 + g], 0)),
        whole((out_width, width))
        if last_call
        else pl.BlockSpec((head_rows, width), lambda g, i, s: (s[3 + g], 0)),
    ]
    out_shape = [
        jax.ShapeDtypeStruct((rows, hid), BF16),
        jax.ShapeDtypeStruct((rows, hid), BF16),
        jax.ShapeDtypeStruct((hid, width), BF16),
        jax.ShapeDtypeStruct((out_width, width), BF16),
    ]
    if last_call:
        out_specs += [by_rows(width), by_rows(out_width)]
        out_shape += [
            jax.ShapeDtypeStruct((rows, width), BF16),
            jax.ShapeDtypeStruct((rows, out_width), BF16),
        ]
    else:
        out_specs += [leaving]
        out_shape += [jax.ShapeDtypeStruct((rows, width), F32)]
    return pl.pallas_call(
        functools.partial(
            forward_kernel, groups, first_call, last_call, (width, half, head_rows)
        ),
        grid_spec=pltpu.PrefetchScalarGridSpec(
            num_scalar_prefetch=1,
            grid=(groups, rows // block_rows),
            in_specs=in_specs,
            out_specs=out_specs,
            scratch_shapes=[pltpu.VMEM((rows, width), F32)] if groups > 1 else [],
        ),
        out_shape=out_shape,
        input_output_aliases=aliases,
        compiler_params=pltpu.CompilerParams(
            dimension_semantics=("arbitrary",) * 2, vmem_limit_bytes=56 * MIB
        ),
        cost_estimate=pl.CostEstimate(
            flops=8 * groups * rows * width * half,
            bytes_accessed=12 * MIB,
            transcendentals=groups * rows * 2 * half,
        ),
        name="forward_part",
    )(place, *args)


def once(shape):
    return pl.BlockSpec(shape, lambda i, s: (0, 0), pipeline_mode=pl.Buffered(1))


def store_halves(core, parts, keep, send):
    n, _, rows, cols = parts.shape
    zero = parts[:, 0].reshape(n * rows, cols).astype(BF16)
    one = parts[:, 1].reshape(n * rows, cols).astype(BF16)

    @pl.when(core == 0)
    def _():
        keep[0] = zero
        send[0] = one

    @pl.when(core == 1)
    def _():
        keep[0] = one
        send[0] = zero


def riders(place, scalars, shape):
    line = lax.broadcasted_iota(jnp.int32, shape, 0)
    lane = lax.broadcasted_iota(jnp.int32, shape, 1)
    score = jnp.full(shape, scalars[0], F32)
    out = jnp.where(line == 3, scalars[1], 0.0)
    for i in range(3):
        term = score.astype(BF16).astype(F32)
        out = jnp.where(line == i, term, out)
        score = score - term
    return jnp.where(lane == 2 * place[0] + place[1], out, 0.0)


def early_kernel(place, hidden, resid_grad, residual, grad_rows, scalars, keep, send):
    second = dot(hidden[...], resid_grad[...], ((0,), (0,)))
    head = dot(residual[...], grad_rows[...], ((0,), (0,)))
    width, out_width = second.shape[1], head.shape[1]
    second = second.reshape(RING, 2, RING, -1, width)
    head = head.reshape(RING, 2, RING, -1, out_width)
    blank = riders(place, scalars, (head.shape[3], width - out_width))
    blank = jnp.broadcast_to(blank, (*head.shape[:3], *blank.shape))
    both = jnp.concatenate([second, jnp.concatenate([head, blank], 4)], 3)
    both = jnp.stack([both[:, :, i] for i in (0, 3, 1, 2)], 2)
    store_halves(place[1], both.reshape(RING, 2, -1, width), keep, send)


def early_grads(place, hidden, resid_grad, residual, grad_rows, scalars):
    rows, hid = hidden.shape
    width, out_width = residual.shape[1], grad_rows.shape[1]
    lines = (hid + width) // RING // 2
    out = pl.BlockSpec((1, lines, width), lambda i, s: (i, 0, 0))
    return pl.pallas_call(
        early_kernel,
        grid_spec=pltpu.PrefetchScalarGridSpec(
            num_scalar_prefetch=1,
            grid=(RING,),
            in_specs=[
                pl.BlockSpec((rows, hid // RING), lambda i, s: (0, i)),
                once((rows, width)),
                pl.BlockSpec((rows, width // RING), lambda i, s: (0, i)),
                once((rows, out_width)),
                pl.BlockSpec(memory_space=pltpu.SMEM),
            ],
            out_specs=[out, out],
        ),
        out_shape=[jax.ShapeDtypeStruct((RING, lines, width), BF16)] * 2,
        compiler_params=params(56),
        cost_estimate=pl.CostEstimate(
            flops=2 * rows * width * (hid + out_width), bytes_accessed=18 * MIB, transcendentals=0
        ),
        name="early_grads",
    )(place, hidden, resid_grad, residual, grad_rows, scalars)


def late_kernel(gray, place, resid_grad, second, slope, tokens, keep, send):
    hidden_grad = dot(resid_grad[...], second[...], ((1,), (1,)))
    preact_grad = (slope[...].astype(F32) * hidden_grad).astype(BF16)
    first = dot(tokens[...], preact_grad, ((0,), (0,)))
    cols = first.shape[1]
    parts = first.reshape(16, 2, RING, -1, cols)
    if gray:
        parts = jnp.stack([parts[:, :, i] for i in (0, 3, 1, 2)], 2)
    store_halves(place[1], parts.reshape(16, 2, -1, cols), keep, send)


def late_grads(place, part, resid_grad, second, slope, tokens):
    rows, width = resid_grad.shape
    tile = 2 * LANES
    steps = width // tile
    out = pl.BlockSpec((1, width // 2, tile), lambda j, s: (0, 0, j))
    return pl.pallas_call(
        functools.partial(late_kernel, part == 1),
        grid_spec=pltpu.PrefetchScalarGridSpec(
            num_scalar_prefetch=1,
            grid=(steps,),
            in_specs=[
                once((rows, width)),
                pl.BlockSpec((tile, width), lambda j, s: (part * steps + j, 0)),
                pl.BlockSpec((rows, tile), lambda j, s: (0, part * steps + j)),
                once((rows, width)),
            ],
            out_specs=[out, out],
        ),
        out_shape=[jax.ShapeDtypeStruct((1, width // 2, width), BF16)] * 2,
        compiler_params=params(56),
        cost_estimate=pl.CostEstimate(
            flops=4 * rows * width * width, bytes_accessed=12 * MIB, transcendentals=0
        ),
        name="late_grads",
    )(place, resid_grad, second, slope, tokens)


def add(a, b):
    return (a.astype(F32) + b.astype(F32)).astype(BF16)


def take(x, index, axis):
    return lax.dynamic_index_in_dim(x, index, axis, keepdims=False)


def ring_bits(axis):
    here = lax.axis_index(axis)
    high = here // 2
    return (high + here) % 2, high


def ring_chain(axis, low_first):
    low, high = ring_bits(axis)
    if low_first:
        steps = ((PAIR_LOW, low, 0), (PAIR_HIGH, high, 0))
    else:
        steps = ((PAIR_HIGH, high, 1), (PAIR_LOW, low, 0))
    return [(pairs, axis, bit, dim) for pairs, bit, dim in steps]


def outgoing(x, step):
    return take(x, 1 - step[2], step[3])


def sent_along(x, step):
    return lax.ppermute(x, step[1], step[0])


def kept_plus(x, arrived, step):
    return add(take(x, step[2], step[3]), arrived)


def by_ring(x, lines):
    return x.reshape(-1, 2, 2, lines, x.shape[-1]).transpose(1, 2, 0, 3, 4)


def summed_over_y(x):
    here = lax.axis_index("y")
    total = take(x, here, 1)
    for by in range(1, RING):
        total = total + shift(take(x, (here + by) % RING, 1), "y", by)
    return total


def tie(*arrays):
    return lax.optimization_barrier(arrays)


def after(x, *others):
    return lax.optimization_barrier((x, *others))[0]


def pack_kernel(side, first, second, head, a, b):
    width = first.shape[0]
    half = second.shape[0]
    a[:width, :] = first[...]
    for q in range(width // LANES):
        b[q * half : (q + 1) * half, :] = second[:, q * LANES : (q + 1) * LANES]
    a[width:, :] = head[:, :LANES]
    b[width:, :] = head[:, LANES:]


def packed(side, first, second, head):
    width, shard = first.shape
    half = shard // 2
    lines = width + head.shape[0]
    out = pl.BlockSpec((lines, LANES), lambda i, s: (0, 0))
    return pl.pallas_call(
        pack_kernel,
        grid_spec=pltpu.PrefetchScalarGridSpec(
            num_scalar_prefetch=1,
            grid=(1,),
            in_specs=[
                pl.BlockSpec((width, half), lambda i, s: (0, s[0])),
                pl.BlockSpec((half, width), lambda i, s: (s[0], 0)),
                pl.BlockSpec((head.shape[0], width // 2), lambda i, s: (0, s[0])),
            ],
            out_specs=[out, out],
        ),
        out_shape=[jax.ShapeDtypeStruct((lines, LANES), BF16)] * 2,
        compiler_params=params(8),
        name="packed",
    )(side, first, second, head)


def score(samples, target, valid_mask):
    count = samples.shape[0]
    wide = samples.astype(F32)
    gram = jnp.einsum("mpo,npo->pmn", samples, samples, preferred_element_type=F32)
    squares = jnp.sum(wide * wide, axis=2).T
    dist_sq = squares[:, :, None] + squares[:, None, :] - 2.0 * gram
    spread = jnp.sqrt(dist_sq + SMOOTHING)
    kernel = 1.0 / spread
    kernel_sum = jnp.sum(kernel, axis=2)
    pulled = jnp.einsum("pmn,npo->mpo", kernel, wide, precision=lax.Precision.HIGHEST)
    offset = wide - target[None]
    error_norm = jnp.sqrt(jnp.sum(offset * offset, axis=2) + SMOOTHING)
    repulse = wide * kernel_sum.T[:, :, None] - pulled
    validity = valid_mask.astype(F32)
    grad_raw = (
        LOSS_SCALE
        * validity[None, :, None]
        * (offset / (count * error_norm[:, :, None]) - repulse / (count * count))
    ).astype(BF16)
    scores = validity * (
        jnp.mean(error_norm, axis=0) - jnp.sum(spread, axis=(1, 2)) / (2.0 * count * count)
    )
    return grad_raw, jnp.sum(scores), jnp.sum(validity)


def per_device(latents, w_first, w_second, readout_matrix, observed, obs_index, valid_mask):
    members, patches, width = latents.shape
    out_width = observed.shape[1]
    core = lax.axis_index("c")
    here = lax.axis_index("y")
    own = obs_index.shape[0]
    rows = members * patches
    shard = w_first.shape[1]
    half = shard // 2

    side = jnp.reshape(core, (1,)).astype(jnp.int32)
    turned = readout_matrix.T
    own_a, own_b = packed(side, w_first, w_second, turned)
    right_a = shift(own_a, "y", 1)
    left_b = shift(own_b, "y", -1)
    latents, other_side, own_a, own_b = tie(latents, 1 - side, own_a, own_b)
    tokens = (
        latents.reshape(members, 32, own, width).transpose(1, 0, 2, 3).reshape(rows, width)
    )
    place = lambda *offs: jnp.stack(
        [here, core, lax.axis_index("x"), *[(here + off) % RING for off in offs]]
    ).astype(jnp.int32)
    run = functools.partial(forward_part, out_width=out_width)
    swap = lambda x: shift(x, "c", 1)
    packs = (own_a, own_b, *packed(other_side, w_first, w_second, turned))
    carried = run(place(0), tokens, packs, carried=None, last_call=False)
    right_a, left_b, *_ = tie(right_a, left_b, carried[-1])
    left_a = shift(after(own_a, right_a, left_b), "y", -1)
    right_b = shift(after(own_b, right_a, left_b), "y", 1)
    right_a_other, left_b_other = swap(right_a), swap(left_b)
    left_a, right_b, right_a_other, left_b_other = tie(
        left_a, right_b, right_a_other, left_b_other
    )
    far_a = shift(after(right_a, left_a, right_b), "y", 1)
    far_b = shift(after(left_b, left_a, right_b), "y", -1)
    packs = (right_a, right_b, right_a_other, swap(right_b))
    packs = (*packs, left_a, left_b, swap(left_a), left_b_other)
    carried = run(place(3, 1), tokens, packs, carried=carried, last_call=False)
    far_a, far_b, *carried = tie(far_a, far_b, *carried)
    slope, hidden, second, head, residual, forecast = run(
        place(2), tokens, (far_a, far_b, swap(far_a), swap(far_b)), carried=carried, last_call=True
    )

    group = ("x", "z", "c")
    device = ((here * 4 + lax.axis_index("x")) * 4 + lax.axis_index("z")) * 2 + core
    target = jnp.take(observed, obs_index - device * own, axis=0)
    forecast, target = tie(forecast.reshape(32, members * own, out_width), target)
    gathered = lax.all_to_all(forecast, group, 0, 0, tiled=True)
    samples = gathered.reshape(32 * members, own, out_width)
    grad_raw, score_part, count_part = score(samples, target, valid_mask)
    grad_rows = lax.all_to_all(
        grad_raw.reshape(32, members * own, out_width), group, 0, 0, tiled=True
    ).reshape(rows, out_width)

    at = place(0)
    scalars = jnp.stack([score_part, count_part])
    resid_grad = dot(grad_rows, head).astype(BF16)
    early = early_grads(at, hidden, resid_grad, residual, grad_rows, scalars)
    early_in = shift(early[1], "c", 1)
    late = late_grads(at, 0, after(resid_grad, early[1]), second, slope, tokens)
    a_in = shift(late[1], "c", 1)
    steps = [ring_chain("y", True), ring_chain("y", False)]
    group = ("x", "z")
    n = width // 128
    early = add(after(early[0], late[1]), early_in)
    lines = early.shape[1] // 16
    early = [by_ring(v, lines) for v in (early[:2], early[2:])]
    early_sent = [outgoing(x, s[0]) for x, s in zip(early, steps)]
    early_in = [sent_along(x, s[0]) for x, s in zip(early_sent, steps)]
    a = add(after(late[0], *early_sent), a_in).reshape(16, RING * n, width)
    a_all = lax.all_to_all(a, group, 0, 0, tiled=True)
    late = late_grads(at, 1, after(resid_grad, a), second, slope, tokens)
    b_in = shift(after(late[1], *early_in), "c", 1)
    early = [kept_plus(x, v, s[0]) for x, v, s in zip(early, early_in, steps)]
    early_sent = [outgoing(x, s[1]) for x, s in zip(early, steps)]
    early_in = [sent_along(x, s[1]) for x, s in zip(early_sent, steps)]
    b = add(after(late[0], *early_sent), b_in).reshape(2, -1, width)
    b = [by_ring(v, n) for v in (b[0], b[1])]
    b_sent = [outgoing(x, s[0]) for x, s in zip(b, steps)]
    b_in = [sent_along(x, s[0]) for x, s in zip(b_sent, steps)]
    a = jnp.sum(after(a_all, *b_sent).astype(F32), 0)
    first = summed_over_y(a.reshape(1, RING, n, width))
    early = [kept_plus(x, after(v, *b_sent), s[1]) for x, v, s in zip(early, early_in, steps)]
    b = [kept_plus(x, after(v, *early), s[0]) for x, v, s in zip(b, b_in, steps)]
    b_sent = [outgoing(x, s[1]) for x, s in zip(b, steps)]
    b_in = [sent_along(x, s[1]) for x, s in zip(b_sent, steps)]
    b = [kept_plus(x, v, s[1]) for x, v, s in zip(b, b_in, steps)]
    early = jnp.concatenate([jnp.concatenate(early), jnp.concatenate(b)], 1)
    early = lax.all_to_all(early, group, 0, 0, tiled=True)
    early = jnp.sum(early.astype(F32), 0)
    early, b = early[:-n], early[-n:]
    n_second = shard * RING // 128
    ride = jnp.sum(early[n_second:, out_width:], 1)
    score_total = ride[0] + ride[1] + ride[2]
    valid_total = jnp.maximum(ride[3], 1.0)
    scale = 1.0 / valid_total
    return (
        jnp.concatenate([first[0], b], 1) * scale,
        early[:n_second] * scale,
        early[n_second:, :out_width] * scale,
        score_total / valid_total,
    )


def solution(mesh):
    grid = Mesh(mesh.devices.reshape(4, 4, 2, 4), ("x", "z", "c", "y"))
    rows = P(("y", "x", "z", "c"))
    shares = P(("x", "z", "c", "y"), None)
    return jax.shard_map(
        per_device,
        mesh=grid,
        in_specs=(
            P(("x", "z", "c"), "y", None),
            P(None, "y"),
            P("y", None),
            P(None, "y"),
            rows,
            rows,
            rows,
        ),
        out_specs=(shares, shares, shares, P()),
        check_vma=False,
    )
```

```python
import functools

import jax
import jax.numpy as jnp
from jax import lax
from jax.experimental import pallas as pl
from jax.experimental.pallas import tpu as pltpu
from jax.sharding import Mesh
from jax.sharding import PartitionSpec as P

SMOOTHING = 1.0
LOSS_SCALE = 4096.0
RING = 4
PAIR_LOW = ((0, 1), (1, 0), (2, 3), (3, 2))
PAIR_HIGH = ((0, 3), (3, 0), (1, 2), (2, 1))
ROOT_2_PI = 0.7978845608028654
CUBIC = 0.044715
LANES = 256
MIB = 1 << 20
F32 = jnp.float32
BF16 = jnp.bfloat16


def shift(x, axis, by):
    size = lax.axis_size(axis)
    return lax.ppermute(x, axis, [(i, (i + by) % size) for i in range(size)])


def dot(a, b, contract=((1,), (0,))):
    return lax.dot_general(a, b, (contract, ((), ())), preferred_element_type=F32)


def params(mib):
    return pltpu.CompilerParams(dimension_semantics=("arbitrary",), vmem_limit_bytes=mib * MIB)


def forward_kernel(groups, first_call, last_call, sizes, *refs):
    width, half, head_rows = sizes
    place, tokens = refs[:2]
    packs = [(refs[2 + 4 * g : 4 + 4 * g], refs[4 + 4 * g : 6 + 4 * g]) for g in range(groups)]
    refs = refs[2 + 4 * groups :]
    if first_call:
        slope, hidden, second, head, total = refs
    elif last_call:
        total_in, _, _, _, head_in, slope, hidden, second, head, residual, forecast = refs
    elif groups > 1:
        total_in, _, _, _, _, slope, hidden, second, head, total, kept = refs
    else:
        total_in, _, _, _, _, slope, hidden, second, head, total = refs
    group, step = pl.program_id(0), pl.program_id(1)
    core = place[1]
    chunks = width // LANES
    sides = (core, 1 - core)

    def run(g):
        @pl.when(step == 0)
        def _():
            if last_call:
                head[...] = head_in[...]
            for pair, side in zip(packs[g], sides):
                below = pl.multiple_of(side * half, half)
                for q in range(chunks):
                    second[pl.ds(below, half), q * LANES : (q + 1) * LANES] = pair[1][
                        q * half : (q + 1) * half, :
                    ]
                row = pl.multiple_of(place[3] * head_rows, 64) if last_call else 0
                for e in range(2):
                    lane = pl.multiple_of(side * (width // 2) + e * LANES, LANES)
                    head[pl.ds(row, head_rows), pl.ds(lane, LANES)] = pair[e][width:, :]

        rows = tokens[...]
        count = rows.shape[0]
        line = pl.multiple_of(step * count, count)
        if first_call:
            base = rows.astype(F32)
        elif g == 0:
            base = total_in[...]
        else:
            base = kept[pl.ds(line, count), :]
        sums = [base[:, q * LANES : (q + 1) * LANES] for q in range(chunks)]
        for pair, side in zip(packs[g], sides):
            x = dot(rows, pair[0][:width, :])
            sq = x * x
            t = jnp.tanh(ROOT_2_PI * (x + CUBIC * x * sq))
            up = 0.5 * (1.0 + t)
            active = (x * up).astype(BF16)
            lane = pl.multiple_of(side * half, half)
            turn = up + (0.5 * ROOT_2_PI) * x * (1.0 - t * t) * (1.0 + (3.0 * CUBIC) * sq)
            slope[:, pl.ds(lane, half)] = turn.astype(BF16)
            hidden[:, pl.ds(lane, half)] = active
            for q in range(chunks):
                sums[q] = sums[q] + dot(active, pair[1][q * half : (q + 1) * half, :])
        full = jnp.concatenate(sums, 1)
        if last_call:
            rounded = full.astype(BF16)
            residual[...] = rounded
            forecast[...] = dot(rounded, head[...], ((1,), (1,))).astype(BF16)
        elif g + 1 < groups:
            kept[pl.ds(line, count), :] = full
        else:
            total[...] = full

    for g in range(groups):
        if groups == 1:
            run(g)
        else:
            pl.when(group == g)(functools.partial(run, g))


def forward_part(place, tokens, packs, carried, out_width, last_call):
    rows, width = tokens.shape
    groups = len(packs) // 4
    half = LANES
    hid = 2 * half * RING
    head_rows = out_width // RING
    first_call = carried is None
    block_rows = min(rows, 256)
    whole = lambda shape: pl.BlockSpec(
        shape, lambda g, i, s: (0,) * len(shape), pipeline_mode=pl.Buffered(1)
    )
    by_rows = lambda cols: pl.BlockSpec((block_rows, cols), lambda g, i, s: (i, 0))
    last_of = rows // block_rows - 1
    entering = pl.BlockSpec(
        (block_rows, width), lambda g, i, s: (jnp.where(g == 0, i, last_of), 0)
    )
    leaving = pl.BlockSpec(
        (block_rows, width), lambda g, i, s: (jnp.where(g == groups - 1, i, 0), 0)
    )
    in_place = pl.BlockSpec(memory_space=pl.ANY)
    in_specs = [by_rows(width), *[whole(p.shape) for p in packs]]
    args = [tokens, *packs]
    aliases = {}
    if not first_call:
        slope, hidden, second, head, total = carried
        at = 1 + len(args)
        args += [total, slope, hidden, second, head]
        in_specs += [entering, in_place, in_place, in_place]
        in_specs += [whole((out_width, width)) if last_call else in_place]
        aliases = {at + 1: 0, at + 2: 1, at + 3: 2}
        if not last_call:
            aliases = {**aliases, at + 4: 3}
    column = pl.BlockSpec((block_rows, 2 * half), lambda g, i, s: (i, s[3 + g]))
    out_specs = [
        column,
        column,
        pl.BlockSpec((2 * half, width), lambda g, i, s: (s[3 + g], 0)),
        whole((out_width, width))
        if last_call
        else pl.BlockSpec((head_rows, width), lambda g, i, s: (s[3 + g], 0)),
    ]
    out_shape = [
        jax.ShapeDtypeStruct((rows, hid), BF16),
        jax.ShapeDtypeStruct((rows, hid), BF16),
        jax.ShapeDtypeStruct((hid, width), BF16),
        jax.ShapeDtypeStruct((out_width, width), BF16),
    ]
    if last_call:
        out_specs += [by_rows(width), by_rows(out_width)]
        out_shape += [
            jax.ShapeDtypeStruct((rows, width), BF16),
            jax.ShapeDtypeStruct((rows, out_width), BF16),
        ]
    else:
        out_specs += [leaving]
        out_shape += [jax.ShapeDtypeStruct((rows, width), F32)]
    return pl.pallas_call(
        functools.partial(
            forward_kernel, groups, first_call, last_call, (width, half, head_rows)
        ),
        grid_spec=pltpu.PrefetchScalarGridSpec(
            num_scalar_prefetch=1,
            grid=(groups, rows // block_rows),
            in_specs=in_specs,
            out_specs=out_specs,
            scratch_shapes=[pltpu.VMEM((rows, width), F32)] if groups > 1 else [],
        ),
        out_shape=out_shape,
        input_output_aliases=aliases,
        compiler_params=pltpu.CompilerParams(
            dimension_semantics=("arbitrary",) * 2, vmem_limit_bytes=56 * MIB
        ),
        cost_estimate=pl.CostEstimate(
            flops=8 * groups * rows * width * half,
            bytes_accessed=12 * MIB,
            transcendentals=groups * rows * 2 * half,
        ),
        name="forward_part",
    )(place, *args)


def once(shape):
    return pl.BlockSpec(shape, lambda i, s: (0, 0), pipeline_mode=pl.Buffered(1))


def store_halves(core, parts, keep, send):
    n, _, rows, cols = parts.shape
    zero = parts[:, 0].reshape(n * rows, cols).astype(BF16)
    one = parts[:, 1].reshape(n * rows, cols).astype(BF16)

    @pl.when(core == 0)
    def _():
        keep[0] = zero
        send[0] = one

    @pl.when(core == 1)
    def _():
        keep[0] = one
        send[0] = zero


def riders(place, scalars, shape):
    line = lax.broadcasted_iota(jnp.int32, shape, 0)
    lane = lax.broadcasted_iota(jnp.int32, shape, 1)
    score = jnp.full(shape, scalars[0], F32)
    out = jnp.where(line == 3, scalars[1], 0.0)
    for i in range(3):
        term = score.astype(BF16).astype(F32)
        out = jnp.where(line == i, term, out)
        score = score - term
    return jnp.where(lane == 2 * place[0] + place[1], out, 0.0)


def early_kernel(place, hidden, resid_grad, keep, send):
    second = dot(hidden[...], resid_grad[...], ((0,), (0,)))
    parts = second.reshape(RING, 2, RING, -1, second.shape[1])
    parts = jnp.stack([parts[:, :, i] for i in (0, 3, 1, 2)], 2)
    store_halves(place[1], parts.reshape(RING, 2, -1, second.shape[1]), keep, send)


def early_grads(place, hidden, resid_grad):
    rows, hid = hidden.shape
    width = resid_grad.shape[1]
    lines = hid // RING // 2
    out = pl.BlockSpec((1, lines, width), lambda i, s: (i, 0, 0))
    return pl.pallas_call(
        early_kernel,
        grid_spec=pltpu.PrefetchScalarGridSpec(
            num_scalar_prefetch=1,
            grid=(RING,),
            in_specs=[
                pl.BlockSpec((rows, hid // RING), lambda i, s: (0, i)),
                once((rows, width)),
            ],
            out_specs=[out, out],
        ),
        out_shape=[jax.ShapeDtypeStruct((RING, lines, width), BF16)] * 2,
        compiler_params=params(56),
        cost_estimate=pl.CostEstimate(
            flops=2 * rows * width * hid, bytes_accessed=12 * MIB, transcendentals=0
        ),
        name="early_grads",
    )(place, hidden, resid_grad)


def late_kernel(steps, place, resid_grad, second, slope, tokens, *refs):
    keep, send = refs[-2:]
    hidden_grad = dot(resid_grad[...], second[...], ((1,), (1,)))
    preact_grad = (slope[...].astype(F32) * hidden_grad).astype(BF16)
    first = dot(tokens[...], preact_grad, ((0,), (0,)))
    cols = first.shape[1]

    def store(*grads):
        parts = jnp.concatenate([g.reshape(16, 2, RING, -1, cols) for g in grads], 3)
        if len(refs) == 2:
            parts = jnp.stack([parts[:, :, i] for i in (0, 3, 1, 2)], 2)
        store_halves(place[1], parts.reshape(16, 2, -1, cols), keep, send)

    if len(refs) == 2:
        store(first)
        return
    residual, grad_rows, scalars = refs[:3]
    width, out_width = residual.shape[1], grad_rows.shape[1]
    for j in range(steps):

        @pl.when(pl.program_id(0) == j)
        def _(j=j):
            head = dot(residual[...], grad_rows[:, j * cols : (j + 1) * cols], ((0,), (0,)))
            if j == steps - 1:
                blank = riders(place, scalars, (8, width - out_width))
                blank = jnp.broadcast_to(blank, (width // 8, *blank.shape))
                head = jnp.concatenate([head, blank.reshape(width, -1)], 1)
            store(first, head)


def late_grads(place, part, resid_grad, second, slope, tokens, *head):
    rows, width = resid_grad.shape
    tile = 2 * LANES
    steps = width // tile
    lines = width if head else width // 2
    out = pl.BlockSpec((1, lines, tile), lambda j, s: (0, 0, j))
    specs = []
    if head:
        specs = [once(head[0].shape), once(head[1].shape), pl.BlockSpec(memory_space=pltpu.SMEM)]
    return pl.pallas_call(
        functools.partial(late_kernel, steps),
        grid_spec=pltpu.PrefetchScalarGridSpec(
            num_scalar_prefetch=1,
            grid=(steps,),
            in_specs=[
                once((rows, width)),
                pl.BlockSpec((tile, width), lambda j, s: (part * steps + j, 0)),
                pl.BlockSpec((rows, tile), lambda j, s: (0, part * steps + j)),
                once((rows, width)),
                *specs,
            ],
            out_specs=[out, out],
        ),
        out_shape=[jax.ShapeDtypeStruct((1, lines, width), BF16)] * 2,
        compiler_params=params(56),
        cost_estimate=pl.CostEstimate(
            flops=4 * rows * width * width, bytes_accessed=12 * MIB, transcendentals=0
        ),
        name="late_grads",
    )(place, resid_grad, second, slope, tokens, *head)


def add(a, b):
    return (a.astype(F32) + b.astype(F32)).astype(BF16)


def take(x, index, axis):
    return lax.dynamic_index_in_dim(x, index, axis, keepdims=False)


def ring_bits(axis):
    here = lax.axis_index(axis)
    high = here // 2
    return (high + here) % 2, high


def ring_chain(axis, low_first):
    low, high = ring_bits(axis)
    if low_first:
        steps = ((PAIR_LOW, low, 0), (PAIR_HIGH, high, 0))
    else:
        steps = ((PAIR_HIGH, high, 1), (PAIR_LOW, low, 0))
    return [(pairs, axis, bit, dim) for pairs, bit, dim in steps]


def outgoing(x, step):
    return take(x, 1 - step[2], step[3])


def sent_along(x, step):
    return lax.ppermute(x, step[1], step[0])


def kept_plus(x, arrived, step):
    return add(take(x, step[2], step[3]), arrived)


def by_ring(x, lines):
    return x.reshape(-1, 2, 2, lines, x.shape[-1]).transpose(1, 2, 0, 3, 4)


def summed_over_y(x):
    here = lax.axis_index("y")
    total = take(x, here, 1)
    for by in range(1, RING):
        total = total + shift(take(x, (here + by) % RING, 1), "y", by)
    return total


def tie(*arrays):
    return lax.optimization_barrier(arrays)


def after(x, *others):
    return lax.optimization_barrier((x, *others))[0]


def pack_kernel(side, first, second, head, a, b):
    width = first.shape[0]
    half = second.shape[0]
    a[:width, :] = first[...]
    for q in range(width // LANES):
        b[q * half : (q + 1) * half, :] = second[:, q * LANES : (q + 1) * LANES]
    a[width:, :] = head[:, :LANES]
    b[width:, :] = head[:, LANES:]


def packed(side, first, second, head):
    width, shard = first.shape
    half = shard // 2
    lines = width + head.shape[0]
    out = pl.BlockSpec((lines, LANES), lambda i, s: (0, 0))
    return pl.pallas_call(
        pack_kernel,
        grid_spec=pltpu.PrefetchScalarGridSpec(
            num_scalar_prefetch=1,
            grid=(1,),
            in_specs=[
                pl.BlockSpec((width, half), lambda i, s: (0, s[0])),
                pl.BlockSpec((half, width), lambda i, s: (s[0], 0)),
                pl.BlockSpec((head.shape[0], width // 2), lambda i, s: (0, s[0])),
            ],
            out_specs=[out, out],
        ),
        out_shape=[jax.ShapeDtypeStruct((lines, LANES), BF16)] * 2,
        compiler_params=params(8),
        name="packed",
    )(side, first, second, head)


def score(samples, target, valid_mask):
    count = samples.shape[0]
    wide = samples.astype(F32)
    gram = jnp.einsum("mpo,npo->pmn", samples, samples, preferred_element_type=F32)
    squares = jnp.sum(wide * wide, axis=2).T
    dist_sq = squares[:, :, None] + squares[:, None, :] - 2.0 * gram
    spread = jnp.sqrt(dist_sq + SMOOTHING)
    kernel = 1.0 / spread
    kernel_sum = jnp.sum(kernel, axis=2)
    pulled = jnp.einsum("pmn,npo->mpo", kernel, wide, precision=lax.Precision.HIGHEST)
    offset = wide - target[None]
    error_norm = jnp.sqrt(jnp.sum(offset * offset, axis=2) + SMOOTHING)
    repulse = wide * kernel_sum.T[:, :, None] - pulled
    validity = valid_mask.astype(F32)
    grad_raw = (
        LOSS_SCALE
        * validity[None, :, None]
        * (offset / (count * error_norm[:, :, None]) - repulse / (count * count))
    ).astype(BF16)
    scores = validity * (
        jnp.mean(error_norm, axis=0) - jnp.sum(spread, axis=(1, 2)) / (2.0 * count * count)
    )
    return grad_raw, jnp.sum(scores), jnp.sum(validity)


def per_device(latents, w_first, w_second, readout_matrix, observed, obs_index, valid_mask):
    members, patches, width = latents.shape
    out_width = observed.shape[1]
    core = lax.axis_index("c")
    here = lax.axis_index("y")
    own = obs_index.shape[0]
    rows = members * patches
    shard = w_first.shape[1]
    half = shard // 2

    side = jnp.reshape(core, (1,)).astype(jnp.int32)
    turned = readout_matrix.T
    own_a, own_b = packed(side, w_first, w_second, turned)
    right_a = shift(own_a, "y", 1)
    left_b = shift(own_b, "y", -1)
    latents, other_side, own_a, own_b = tie(latents, 1 - side, own_a, own_b)
    tokens = (
        latents.reshape(members, 32, own, width).transpose(1, 0, 2, 3).reshape(rows, width)
    )
    place = lambda *offs: jnp.stack(
        [here, core, lax.axis_index("x"), *[(here + off) % RING for off in offs]]
    ).astype(jnp.int32)
    run = functools.partial(forward_part, out_width=out_width)
    swap = lambda x: shift(x, "c", 1)
    packs = (own_a, own_b, *packed(other_side, w_first, w_second, turned))
    carried = run(place(0), tokens, packs, carried=None, last_call=False)
    right_a, left_b, *_ = tie(right_a, left_b, carried[-1])
    left_a = shift(after(own_a, right_a, left_b), "y", -1)
    right_b = shift(after(own_b, right_a, left_b), "y", 1)
    right_a_other, left_b_other = swap(right_a), swap(left_b)
    left_a, right_b, right_a_other, left_b_other = tie(
        left_a, right_b, right_a_other, left_b_other
    )
    far_a = shift(after(right_a, left_a, right_b), "y", 1)
    far_b = shift(after(left_b, left_a, right_b), "y", -1)
    packs = (right_a, right_b, right_a_other, swap(right_b))
    packs = (*packs, left_a, left_b, swap(left_a), left_b_other)
    carried = run(place(3, 1), tokens, packs, carried=carried, last_call=False)
    far_a, far_b, *carried = tie(far_a, far_b, *carried)
    slope, hidden, second, head, residual, forecast = run(
        place(2), tokens, (far_a, far_b, swap(far_a), swap(far_b)), carried=carried, last_call=True
    )

    group = ("x", "z", "c")
    device = ((here * 4 + lax.axis_index("x")) * 4 + lax.axis_index("z")) * 2 + core
    target = jnp.take(observed, obs_index - device * own, axis=0)
    forecast, target = tie(forecast.reshape(32, members * own, out_width), target)
    gathered = lax.all_to_all(forecast, group, 0, 0, tiled=True)
    samples = gathered.reshape(32 * members, own, out_width)
    grad_raw, score_part, count_part = score(samples, target, valid_mask)
    grad_rows = lax.all_to_all(
        grad_raw.reshape(32, members * own, out_width), group, 0, 0, tiled=True
    ).reshape(rows, out_width)

    at = place(0)
    scalars = jnp.stack([score_part, count_part])
    resid_grad = dot(grad_rows, head).astype(BF16)
    early = early_grads(at, hidden, resid_grad)
    early_in = shift(early[1], "c", 1)
    late = late_grads(
        at,
        0,
        after(resid_grad, early[1]),
        second,
        slope,
        tokens,
        residual,
        grad_rows,
        scalars,
    )
    a_in = shift(late[1], "c", 1)
    steps = [ring_chain("y", True), ring_chain("y", False)]
    group = ("x", "z")
    n = width // 128
    early = add(after(early[0], late[1]), early_in)
    lines = early.shape[1] // 16
    early = [by_ring(v, lines) for v in (early[:2], early[2:])]
    early_sent = [outgoing(x, s[0]) for x, s in zip(early, steps)]
    early_in = [sent_along(x, s[0]) for x, s in zip(early_sent, steps)]
    a = add(after(late[0], *early_sent), a_in).reshape(16, 2 * RING * n, width)
    a_all = lax.all_to_all(a, group, 0, 0, tiled=True)
    late = late_grads(at, 1, after(resid_grad, a), second, slope, tokens)
    b_in = shift(after(late[1], *early_in), "c", 1)
    early = [kept_plus(x, v, s[0]) for x, v, s in zip(early, early_in, steps)]
    early_sent = [outgoing(x, s[1]) for x, s in zip(early, steps)]
    early_in = [sent_along(x, s[1]) for x, s in zip(early_sent, steps)]
    b = add(after(late[0], *early_sent), b_in).reshape(2, -1, width)
    b = [by_ring(v, n) for v in (b[0], b[1])]
    b_sent = [outgoing(x, s[0]) for x, s in zip(b, steps)]
    b_in = [sent_along(x, s[0]) for x, s in zip(b_sent, steps)]
    a = jnp.sum(after(a_all, *b_sent).astype(F32), 0)
    first = summed_over_y(a.reshape(1, RING, 2 * n, width))[0]
    early = [kept_plus(x, after(v, *b_sent), s[1]) for x, v, s in zip(early, early_in, steps)]
    b = [kept_plus(x, after(v, *early), s[0]) for x, v, s in zip(b, b_in, steps)]
    b_sent = [outgoing(x, s[1]) for x, s in zip(b, steps)]
    b_in = [sent_along(x, s[1]) for x, s in zip(b_sent, steps)]
    b = [kept_plus(x, v, s[1]) for x, v, s in zip(b, b_in, steps)]
    early = jnp.concatenate([jnp.concatenate(early), jnp.concatenate(b)], 1)
    early = lax.all_to_all(early, group, 0, 0, tiled=True)
    early = jnp.sum(early.astype(F32), 0)
    early, b = early[:-n], early[-n:]
    first, head = first[:n], first[n:]
    ride = jnp.sum(head[:, out_width:], 1)
    score_total = ride[0] + ride[1] + ride[2]
    valid_total = jnp.maximum(ride[3], 1.0)
    scale = 1.0 / valid_total
    return (
        jnp.concatenate([first, b], 1) * scale,
        early * scale,
        head[:, :out_width] * scale,
        score_total / valid_total,
    )


def solution(mesh):
    grid = Mesh(mesh.devices.reshape(4, 4, 2, 4), ("x", "z", "c", "y"))
    rows = P(("y", "x", "z", "c"))
    shares = P(("x", "z", "c", "y"), None)
    return jax.shard_map(
        per_device,
        mesh=grid,
        in_specs=(
            P(("x", "z", "c"), "y", None),
            P(None, "y"),
            P("y", None),
            P(None, "y"),
            rows,
            rows,
            rows,
        ),
        out_specs=(shares, shares, shares, P()),
        check_vma=False,
    )
```

```python
import functools

import jax
import jax.numpy as jnp
from jax import lax
from jax.experimental import pallas as pl
from jax.experimental.pallas import tpu as pltpu
from jax.sharding import Mesh
from jax.sharding import PartitionSpec as P

SMOOTHING = 1.0
LOSS_SCALE = 4096.0
RING = 4
PAIR_LOW = ((0, 1), (1, 0), (2, 3), (3, 2))
PAIR_HIGH = ((0, 3), (3, 0), (1, 2), (2, 1))
ROOT_2_PI = 0.7978845608028654
CUBIC = 0.044715
LANES = 256
MIB = 1 << 20
F32 = jnp.float32
BF16 = jnp.bfloat16


def shift(x, axis, by):
    size = lax.axis_size(axis)
    return lax.ppermute(x, axis, [(i, (i + by) % size) for i in range(size)])


def dot(a, b, contract=((1,), (0,))):
    return lax.dot_general(a, b, (contract, ((), ())), preferred_element_type=F32)


def params(mib):
    return pltpu.CompilerParams(dimension_semantics=("arbitrary",), vmem_limit_bytes=mib * MIB)


def forward_kernel(groups, first_call, last_call, sizes, *refs):
    width, half, head_rows = sizes
    place, tokens = refs[:2]
    packs = [(refs[2 + 4 * g : 4 + 4 * g], refs[4 + 4 * g : 6 + 4 * g]) for g in range(groups)]
    refs = refs[2 + 4 * groups :]
    if first_call:
        slope, hidden, second, head, total = refs
    elif last_call:
        total_in, _, _, _, head_in, slope, hidden, second, head, residual, forecast = refs
    elif groups > 1:
        total_in, _, _, _, _, slope, hidden, second, head, total, kept = refs
    else:
        total_in, _, _, _, _, slope, hidden, second, head, total = refs
    group, step = pl.program_id(0), pl.program_id(1)
    core = place[1]
    chunks = width // LANES
    sides = (core, 1 - core)

    def run(g):
        @pl.when(step == 0)
        def _():
            if last_call:
                head[...] = head_in[...]
            for pair, side in zip(packs[g], sides):
                below = pl.multiple_of(side * half, half)
                for q in range(chunks):
                    second[pl.ds(below, half), q * LANES : (q + 1) * LANES] = pair[1][
                        q * half : (q + 1) * half, :
                    ]
                row = pl.multiple_of(place[3] * head_rows, 64) if last_call else 0
                for e in range(2):
                    lane = pl.multiple_of(side * (width // 2) + e * LANES, LANES)
                    head[pl.ds(row, head_rows), pl.ds(lane, LANES)] = pair[e][width:, :]

        rows = tokens[...]
        count = rows.shape[0]
        line = pl.multiple_of(step * count, count)
        if first_call:
            base = rows.astype(F32)
        elif g == 0:
            base = total_in[...]
        else:
            base = kept[pl.ds(line, count), :]
        sums = [base[:, q * LANES : (q + 1) * LANES] for q in range(chunks)]
        for pair, side in zip(packs[g], sides):
            x = dot(rows, pair[0][:width, :])
            sq = x * x
            t = jnp.tanh(ROOT_2_PI * (x + CUBIC * x * sq))
            up = 0.5 * (1.0 + t)
            active = (x * up).astype(BF16)
            lane = pl.multiple_of(side * half, half)
            turn = up + (0.5 * ROOT_2_PI) * x * (1.0 - t * t) * (1.0 + (3.0 * CUBIC) * sq)
            slope[:, pl.ds(lane, half)] = turn.astype(BF16)
            hidden[:, pl.ds(lane, half)] = active
            for q in range(chunks):
                sums[q] = sums[q] + dot(active, pair[1][q * half : (q + 1) * half, :])
        full = jnp.concatenate(sums, 1)
        if last_call:
            rounded = full.astype(BF16)
            residual[...] = rounded
            forecast[...] = dot(rounded, head[...], ((1,), (1,))).astype(BF16)
        elif g + 1 < groups:
            kept[pl.ds(line, count), :] = full
        else:
            total[...] = full

    for g in range(groups):
        if groups == 1:
            run(g)
        else:
            pl.when(group == g)(functools.partial(run, g))


def forward_part(place, tokens, packs, carried, out_width, last_call):
    rows, width = tokens.shape
    groups = len(packs) // 4
    half = LANES
    hid = 2 * half * RING
    head_rows = out_width // RING
    first_call = carried is None
    block_rows = min(rows, 256)
    whole = lambda shape: pl.BlockSpec(
        shape, lambda g, i, s: (0,) * len(shape), pipeline_mode=pl.Buffered(1)
    )
    by_rows = lambda cols: pl.BlockSpec((block_rows, cols), lambda g, i, s: (i, 0))
    last_of = rows // block_rows - 1
    entering = pl.BlockSpec(
        (block_rows, width), lambda g, i, s: (jnp.where(g == 0, i, last_of), 0)
    )
    leaving = pl.BlockSpec(
        (block_rows, width), lambda g, i, s: (jnp.where(g == groups - 1, i, 0), 0)
    )
    in_place = pl.BlockSpec(memory_space=pl.ANY)
    in_specs = [by_rows(width), *[whole(p.shape) for p in packs]]
    args = [tokens, *packs]
    aliases = {}
    if not first_call:
        slope, hidden, second, head, total = carried
        at = 1 + len(args)
        args += [total, slope, hidden, second, head]
        in_specs += [entering, in_place, in_place, in_place]
        in_specs += [whole((out_width, width)) if last_call else in_place]
        aliases = {at + 1: 0, at + 2: 1, at + 3: 2}
        if not last_call:
            aliases = {**aliases, at + 4: 3}
    column = pl.BlockSpec((block_rows, 2 * half), lambda g, i, s: (i, s[3 + g]))
    out_specs = [
        column,
        column,
        pl.BlockSpec((2 * half, width), lambda g, i, s: (s[3 + g], 0)),
        whole((out_width, width))
        if last_call
        else pl.BlockSpec((head_rows, width), lambda g, i, s: (s[3 + g], 0)),
    ]
    out_shape = [
        jax.ShapeDtypeStruct((rows, hid), BF16),
        jax.ShapeDtypeStruct((rows, hid), BF16),
        jax.ShapeDtypeStruct((hid, width), BF16),
        jax.ShapeDtypeStruct((out_width, width), BF16),
    ]
    if last_call:
        out_specs += [by_rows(width), by_rows(out_width)]
        out_shape += [
            jax.ShapeDtypeStruct((rows, width), BF16),
            jax.ShapeDtypeStruct((rows, out_width), BF16),
        ]
    else:
        out_specs += [leaving]
        out_shape += [jax.ShapeDtypeStruct((rows, width), F32)]
    return pl.pallas_call(
        functools.partial(
            forward_kernel, groups, first_call, last_call, (width, half, head_rows)
        ),
        grid_spec=pltpu.PrefetchScalarGridSpec(
            num_scalar_prefetch=1,
            grid=(groups, rows // block_rows),
            in_specs=in_specs,
            out_specs=out_specs,
            scratch_shapes=[pltpu.VMEM((rows, width), F32)] if groups > 1 else [],
        ),
        out_shape=out_shape,
        input_output_aliases=aliases,
        compiler_params=pltpu.CompilerParams(
            dimension_semantics=("arbitrary",) * 2, vmem_limit_bytes=56 * MIB
        ),
        cost_estimate=pl.CostEstimate(
            flops=8 * groups * rows * width * half,
            bytes_accessed=12 * MIB,
            transcendentals=groups * rows * 2 * half,
        ),
        name="forward_part",
    )(place, *args)


def once(shape):
    return pl.BlockSpec(shape, lambda i, s: (0, 0), pipeline_mode=pl.Buffered(1))


def store_halves(core, parts, keep, send):
    n, _, rows, cols = parts.shape
    zero = parts[:, 0].reshape(n * rows, cols).astype(BF16)
    one = parts[:, 1].reshape(n * rows, cols).astype(BF16)

    @pl.when(core == 0)
    def _():
        keep[0] = zero
        send[0] = one

    @pl.when(core == 1)
    def _():
        keep[0] = one
        send[0] = zero


def riders(place, scalars, shape):
    line = lax.broadcasted_iota(jnp.int32, shape, 0)
    lane = lax.broadcasted_iota(jnp.int32, shape, 1)
    score = jnp.full(shape, scalars[0], F32)
    out = jnp.where(line == 3, scalars[1], 0.0)
    for i in range(3):
        term = score.astype(BF16).astype(F32)
        out = jnp.where(line == i, term, out)
        score = score - term
    return jnp.where(lane == 2 * place[0] + place[1], out, 0.0)


def early_kernel(place, hidden, resid_grad, residual, grad_rows, scalars, keep, send):
    second = dot(hidden[...], resid_grad[...], ((0,), (0,)))
    head = dot(residual[...], grad_rows[...], ((0,), (0,)))
    width, out_width = second.shape[1], head.shape[1]
    second = second.reshape(RING, 2, RING, -1, width)
    head = head.reshape(RING, 2, RING, -1, out_width)
    blank = riders(place, scalars, (head.shape[3], width - out_width))
    blank = jnp.broadcast_to(blank, (*head.shape[:3], *blank.shape))
    both = jnp.concatenate([second, jnp.concatenate([head, blank], 4)], 3)
    both = jnp.stack([both[:, :, i] for i in (0, 3, 1, 2)], 2)
    store_halves(place[1], both.reshape(RING, 2, -1, width), keep, send)


def early_grads(place, hidden, resid_grad, residual, grad_rows, scalars):
    rows, hid = hidden.shape
    width, out_width = residual.shape[1], grad_rows.shape[1]
    lines = (hid + width) // RING // 2
    out = pl.BlockSpec((1, lines, width), lambda i, s: (i, 0, 0))
    return pl.pallas_call(
        early_kernel,
        grid_spec=pltpu.PrefetchScalarGridSpec(
            num_scalar_prefetch=1,
            grid=(RING,),
            in_specs=[
                pl.BlockSpec((rows, hid // RING), lambda i, s: (0, i)),
                once((rows, width)),
                pl.BlockSpec((rows, width // RING), lambda i, s: (0, i)),
                once((rows, out_width)),
                pl.BlockSpec(memory_space=pltpu.SMEM),
            ],
            out_specs=[out, out],
        ),
        out_shape=[jax.ShapeDtypeStruct((RING, lines, width), BF16)] * 2,
        compiler_params=params(56),
        cost_estimate=pl.CostEstimate(
            flops=2 * rows * width * (hid + out_width), bytes_accessed=18 * MIB, transcendentals=0
        ),
        name="early_grads",
    )(place, hidden, resid_grad, residual, grad_rows, scalars)


def late_kernel(gray, place, resid_grad, second, slope, tokens, keep, send):
    hidden_grad = dot(resid_grad[...], second[...], ((1,), (1,)))
    preact_grad = (slope[...].astype(F32) * hidden_grad).astype(BF16)
    first = dot(tokens[...], preact_grad, ((0,), (0,)))
    cols = first.shape[1]
    parts = first.reshape(16, 2, RING, -1, cols)
    if gray:
        parts = jnp.stack([parts[:, :, i] for i in (0, 3, 1, 2)], 2)
    store_halves(place[1], parts.reshape(16, 2, -1, cols), keep, send)


def late_grads(place, part, resid_grad, second, slope, tokens):
    rows, width = resid_grad.shape
    tile = 2 * LANES
    steps = width // tile
    out = pl.BlockSpec((1, width // 2, tile), lambda j, s: (0, 0, j))
    return pl.pallas_call(
        functools.partial(late_kernel, part == 1),
        grid_spec=pltpu.PrefetchScalarGridSpec(
            num_scalar_prefetch=1,
            grid=(steps,),
            in_specs=[
                once((rows, width)),
                pl.BlockSpec((tile, width), lambda j, s: (part * steps + j, 0)),
                pl.BlockSpec((rows, tile), lambda j, s: (0, part * steps + j)),
                once((rows, width)),
            ],
            out_specs=[out, out],
        ),
        out_shape=[jax.ShapeDtypeStruct((1, width // 2, width), BF16)] * 2,
        compiler_params=params(56),
        cost_estimate=pl.CostEstimate(
            flops=4 * rows * width * width, bytes_accessed=12 * MIB, transcendentals=0
        ),
        name="late_grads",
    )(place, resid_grad, second, slope, tokens)


def finish_kernel(arrived, half, first, second, head, loss):
    total = jnp.sum(arrived[...].astype(F32), 0)
    n, width = half.shape
    out_width = head.shape[1]
    lines = second.shape[0]
    ride = total[lines : lines + n, out_width:]
    line = lax.broadcasted_iota(jnp.int32, ride.shape, 0)
    score = jnp.sum(jnp.where(line < 3, ride, 0.0), axis=(0, 1), keepdims=True)
    count = jnp.sum(jnp.where(line == 3, ride, 0.0), axis=(0, 1), keepdims=True)
    valid = jnp.maximum(count, 1.0)
    scale = 1.0 / valid
    first[:, :width] = half[...] * scale
    first[:, width:] = total[lines + n :] * scale
    second[...] = total[:lines] * scale
    head[...] = total[lines : lines + n, :out_width] * scale
    loss[...] = score / valid


def finish(arrived, half, out_width):
    n, width = half.shape
    shapes = [(n, 2 * width), (arrived.shape[1] - 2 * n, width), (n, out_width), (1, 1)]
    first, second, head, loss = pl.pallas_call(
        finish_kernel,
        out_shape=[jax.ShapeDtypeStruct(v, F32) for v in shapes],
        compiler_params=pltpu.CompilerParams(vmem_limit_bytes=8 * MIB),
        name="finish",
    )(arrived, half)
    return first, second, head, loss[0, 0]


def add(a, b):
    return (a.astype(F32) + b.astype(F32)).astype(BF16)


def take(x, index, axis):
    return lax.dynamic_index_in_dim(x, index, axis, keepdims=False)


def ring_bits(axis):
    here = lax.axis_index(axis)
    high = here // 2
    return (high + here) % 2, high


def ring_chain(axis, low_first):
    low, high = ring_bits(axis)
    if low_first:
        steps = ((PAIR_LOW, low, 0), (PAIR_HIGH, high, 0))
    else:
        steps = ((PAIR_HIGH, high, 1), (PAIR_LOW, low, 0))
    return [(pairs, axis, bit, dim) for pairs, bit, dim in steps]


def outgoing(x, step):
    return take(x, 1 - step[2], step[3])


def sent_along(x, step):
    return lax.ppermute(x, step[1], step[0])


def kept_plus(x, arrived, step):
    return add(take(x, step[2], step[3]), arrived)


def by_ring(x, lines):
    return x.reshape(-1, 2, 2, lines, x.shape[-1]).transpose(1, 2, 0, 3, 4)


def summed_over_y(x):
    here = lax.axis_index("y")
    total = take(x, here, 1)
    for by in range(1, RING):
        total = total + shift(take(x, (here + by) % RING, 1), "y", by)
    return total


def tie(*arrays):
    return lax.optimization_barrier(arrays)


def after(x, *others):
    return lax.optimization_barrier((x, *others))[0]


def pack_kernel(side, first, second, head, a, b):
    width = first.shape[0]
    half = second.shape[0]
    a[:width, :] = first[...]
    for q in range(width // LANES):
        b[q * half : (q + 1) * half, :] = second[:, q * LANES : (q + 1) * LANES]
    a[width:, :] = head[:, :LANES]
    b[width:, :] = head[:, LANES:]


def packed(side, first, second, head):
    width, shard = first.shape
    half = shard // 2
    lines = width + head.shape[0]
    out = pl.BlockSpec((lines, LANES), lambda i, s: (0, 0))
    return pl.pallas_call(
        pack_kernel,
        grid_spec=pltpu.PrefetchScalarGridSpec(
            num_scalar_prefetch=1,
            grid=(1,),
            in_specs=[
                pl.BlockSpec((width, half), lambda i, s: (0, s[0])),
                pl.BlockSpec((half, width), lambda i, s: (s[0], 0)),
                pl.BlockSpec((head.shape[0], width // 2), lambda i, s: (0, s[0])),
            ],
            out_specs=[out, out],
        ),
        out_shape=[jax.ShapeDtypeStruct((lines, LANES), BF16)] * 2,
        compiler_params=params(8),
        name="packed",
    )(side, first, second, head)


def score(samples, target, valid_mask):
    count = samples.shape[0]
    wide = samples.astype(F32)
    gram = jnp.einsum("mpo,npo->pmn", samples, samples, preferred_element_type=F32)
    squares = jnp.sum(wide * wide, axis=2).T
    dist_sq = squares[:, :, None] + squares[:, None, :] - 2.0 * gram
    spread = jnp.sqrt(dist_sq + SMOOTHING)
    kernel = 1.0 / spread
    kernel_sum = jnp.sum(kernel, axis=2)
    pulled = jnp.einsum("pmn,npo->mpo", kernel, wide, precision=lax.Precision.HIGHEST)
    offset = wide - target[None]
    error_norm = jnp.sqrt(jnp.sum(offset * offset, axis=2) + SMOOTHING)
    repulse = wide * kernel_sum.T[:, :, None] - pulled
    validity = valid_mask.astype(F32)
    grad_raw = (
        LOSS_SCALE
        * validity[None, :, None]
        * (offset / (count * error_norm[:, :, None]) - repulse / (count * count))
    ).astype(BF16)
    scores = validity * (
        jnp.mean(error_norm, axis=0) - jnp.sum(spread, axis=(1, 2)) / (2.0 * count * count)
    )
    return grad_raw, jnp.sum(scores), jnp.sum(validity)


def per_device(latents, w_first, w_second, readout_matrix, observed, obs_index, valid_mask):
    members, patches, width = latents.shape
    out_width = observed.shape[1]
    core = lax.axis_index("c")
    here = lax.axis_index("y")
    own = obs_index.shape[0]
    rows = members * patches
    shard = w_first.shape[1]
    half = shard // 2

    side = jnp.reshape(core, (1,)).astype(jnp.int32)
    turned = readout_matrix.T
    own_a, own_b = packed(side, w_first, w_second, turned)
    right_a = shift(own_a, "y", 1)
    left_b = shift(own_b, "y", -1)
    latents, other_side, own_a, own_b = tie(latents, 1 - side, own_a, own_b)
    tokens = (
        latents.reshape(members, 32, own, width).transpose(1, 0, 2, 3).reshape(rows, width)
    )
    place = lambda *offs: jnp.stack(
        [here, core, lax.axis_index("x"), *[(here + off) % RING for off in offs]]
    ).astype(jnp.int32)
    run = functools.partial(forward_part, out_width=out_width)
    swap = lambda x: shift(x, "c", 1)
    packs = (own_a, own_b, *packed(other_side, w_first, w_second, turned))
    carried = run(place(0), tokens, packs, carried=None, last_call=False)
    right_a, left_b, *_ = tie(right_a, left_b, carried[-1])
    left_a = shift(after(own_a, right_a, left_b), "y", -1)
    right_b = shift(after(own_b, right_a, left_b), "y", 1)
    right_a_other, left_b_other = swap(right_a), swap(left_b)
    left_a, right_b, right_a_other, left_b_other = tie(
        left_a, right_b, right_a_other, left_b_other
    )
    far_a = shift(after(right_a, left_a, right_b), "y", 1)
    far_b = shift(after(left_b, left_a, right_b), "y", -1)
    packs = (right_a, right_b, right_a_other, swap(right_b))
    packs = (*packs, left_a, left_b, swap(left_a), left_b_other)
    carried = run(place(3, 1), tokens, packs, carried=carried, last_call=False)
    far_a, far_b, *carried = tie(far_a, far_b, *carried)
    slope, hidden, second, head, residual, forecast = run(
        place(2), tokens, (far_a, far_b, swap(far_a), swap(far_b)), carried=carried, last_call=True
    )

    group = ("x", "z", "c")
    device = ((here * 4 + lax.axis_index("x")) * 4 + lax.axis_index("z")) * 2 + core
    target = jnp.take(observed, obs_index - device * own, axis=0)
    forecast, target = tie(forecast.reshape(32, members * own, out_width), target)
    gathered = lax.all_to_all(forecast, group, 0, 0, tiled=True)
    samples = gathered.reshape(32 * members, own, out_width)
    grad_raw, score_part, count_part = score(samples, target, valid_mask)
    grad_rows = lax.all_to_all(
        grad_raw.reshape(32, members * own, out_width), group, 0, 0, tiled=True
    ).reshape(rows, out_width)

    at = place(0)
    scalars = jnp.stack([score_part, count_part])
    resid_grad = dot(grad_rows, head).astype(BF16)
    early = early_grads(at, hidden, resid_grad, residual, grad_rows, scalars)
    early_in = shift(early[1], "c", 1)
    late = late_grads(at, 0, after(resid_grad, early[1]), second, slope, tokens)
    a_in = shift(late[1], "c", 1)
    steps = [ring_chain("y", True), ring_chain("y", False)]
    group = ("x", "z")
    n = width // 128
    early = add(after(early[0], late[1]), early_in)
    lines = early.shape[1] // 16
    early = [by_ring(v, lines) for v in (early[:2], early[2:])]
    early_sent = [outgoing(x, s[0]) for x, s in zip(early, steps)]
    early_in = [sent_along(x, s[0]) for x, s in zip(early_sent, steps)]
    a = add(after(late[0], *early_sent), a_in).reshape(16, RING * n, width)
    a_all = lax.all_to_all(a, group, 0, 0, tiled=True)
    late = late_grads(at, 1, after(resid_grad, a), second, slope, tokens)
    b_in = shift(after(late[1], *early_in), "c", 1)
    early = [kept_plus(x, v, s[0]) for x, v, s in zip(early, early_in, steps)]
    early_sent = [outgoing(x, s[1]) for x, s in zip(early, steps)]
    early_in = [sent_along(x, s[1]) for x, s in zip(early_sent, steps)]
    b = add(after(late[0], *early_sent), b_in).reshape(2, -1, width)
    b = [by_ring(v, n) for v in (b[0], b[1])]
    b_sent = [outgoing(x, s[0]) for x, s in zip(b, steps)]
    b_in = [sent_along(x, s[0]) for x, s in zip(b_sent, steps)]
    a = jnp.sum(after(a_all, *b_sent).astype(F32), 0)
    first = summed_over_y(a.reshape(1, RING, n, width))
    early = [kept_plus(x, after(v, *b_sent), s[1]) for x, v, s in zip(early, early_in, steps)]
    b = [kept_plus(x, after(v, *early), s[0]) for x, v, s in zip(b, b_in, steps)]
    b_sent = [outgoing(x, s[1]) for x, s in zip(b, steps)]
    b_in = [sent_along(x, s[1]) for x, s in zip(b_sent, steps)]
    b = [kept_plus(x, v, s[1]) for x, v, s in zip(b, b_in, steps)]
    early = jnp.concatenate([jnp.concatenate(early), jnp.concatenate(b)], 1)
    early = lax.all_to_all(early, group, 0, 0, tiled=True)
    return finish(early, first[0], out_width)


def solution(mesh):
    grid = Mesh(mesh.devices.reshape(4, 4, 2, 4), ("x", "z", "c", "y"))
    rows = P(("y", "x", "z", "c"))
    shares = P(("x", "z", "c", "y"), None)
    return jax.shard_map(
        per_device,
        mesh=grid,
        in_specs=(
            P(("x", "z", "c"), "y", None),
            P(None, "y"),
            P("y", None),
            P(None, "y"),
            rows,
            rows,
            rows,
        ),
        out_specs=(shares, shares, shares, P()),
        check_vma=False,
    )
```

```python
import functools

import jax
import jax.numpy as jnp
from jax import lax
from jax.experimental import pallas as pl
from jax.experimental.pallas import tpu as pltpu
from jax.sharding import Mesh
from jax.sharding import PartitionSpec as P

SMOOTHING = 1.0
LOSS_SCALE = 4096.0
RING = 4
PAIR_LOW = ((0, 1), (1, 0), (2, 3), (3, 2))
PAIR_HIGH = ((0, 3), (3, 0), (1, 2), (2, 1))
ROOT_2_PI = 0.7978845608028654
CUBIC = 0.044715
LANES = 256
MIB = 1 << 20
F32 = jnp.float32
BF16 = jnp.bfloat16


def shift(x, axis, by):
    size = lax.axis_size(axis)
    return lax.ppermute(x, axis, [(i, (i + by) % size) for i in range(size)])


def dot(a, b, contract=((1,), (0,))):
    return lax.dot_general(a, b, (contract, ((), ())), preferred_element_type=F32)


def params(mib):
    return pltpu.CompilerParams(dimension_semantics=("arbitrary",), vmem_limit_bytes=mib * MIB)


def forward_kernel(groups, first_call, last_call, sizes, *refs):
    width, half, head_rows = sizes
    place, tokens = refs[:2]
    packs = [(refs[2 + 4 * g : 4 + 4 * g], refs[4 + 4 * g : 6 + 4 * g]) for g in range(groups)]
    refs = refs[2 + 4 * groups :]
    if first_call:
        slope, hidden, second, head, total = refs
    elif last_call:
        total_in, _, _, _, head_in, slope, hidden, second, head, residual, forecast = refs
    elif groups > 1:
        total_in, _, _, _, _, slope, hidden, second, head, total, kept = refs
    else:
        total_in, _, _, _, _, slope, hidden, second, head, total = refs
    group, step = pl.program_id(0), pl.program_id(1)
    core = place[1]
    chunks = width // LANES
    sides = (core, 1 - core)

    def run(g):
        @pl.when(step == 0)
        def _():
            if last_call:
                head[...] = head_in[...]
            for pair, side in zip(packs[g], sides):
                below = pl.multiple_of(side * half, half)
                for q in range(chunks):
                    second[pl.ds(below, half), q * LANES : (q + 1) * LANES] = pair[1][
                        q * half : (q + 1) * half, :
                    ]
                row = pl.multiple_of(place[3] * head_rows, 64) if last_call else 0
                for e in range(2):
                    lane = pl.multiple_of(side * (width // 2) + e * LANES, LANES)
                    head[pl.ds(row, head_rows), pl.ds(lane, LANES)] = pair[e][width:, :]

        rows = tokens[...]
        count = rows.shape[0]
        line = pl.multiple_of(step * count, count)
        if first_call:
            base = rows.astype(F32)
        elif g == 0:
            base = total_in[...]
        else:
            base = kept[pl.ds(line, count), :]
        sums = [base[:, q * LANES : (q + 1) * LANES] for q in range(chunks)]
        for pair, side in zip(packs[g], sides):
            x = dot(rows, pair[0][:width, :])
            sq = x * x
            t = jnp.tanh(ROOT_2_PI * (x + CUBIC * x * sq))
            up = 0.5 * (1.0 + t)
            active = (x * up).astype(BF16)
            lane = pl.multiple_of(side * half, half)
            turn = up + (0.5 * ROOT_2_PI) * x * (1.0 - t * t) * (1.0 + (3.0 * CUBIC) * sq)
            slope[:, pl.ds(lane, half)] = turn.astype(BF16)
            hidden[:, pl.ds(lane, half)] = active
            for q in range(chunks):
                sums[q] = sums[q] + dot(active, pair[1][q * half : (q + 1) * half, :])
        full = jnp.concatenate(sums, 1)
        if last_call:
            rounded = full.astype(BF16)
            residual[...] = rounded
            forecast[...] = dot(rounded, head[...], ((1,), (1,))).astype(BF16)
        elif g + 1 < groups:
            kept[pl.ds(line, count), :] = full
        else:
            total[...] = full

    for g in range(groups):
        if groups == 1:
            run(g)
        else:
            pl.when(group == g)(functools.partial(run, g))


def forward_part(place, tokens, packs, carried, out_width, last_call):
    rows, width = tokens.shape
    groups = len(packs) // 4
    half = LANES
    hid = 2 * half * RING
    head_rows = out_width // RING
    first_call = carried is None
    block_rows = min(rows, 512)
    whole = lambda shape: pl.BlockSpec(
        shape, lambda g, i, s: (0,) * len(shape), pipeline_mode=pl.Buffered(1)
    )
    by_rows = lambda cols: pl.BlockSpec((block_rows, cols), lambda g, i, s: (i, 0))
    last_of = rows // block_rows - 1
    entering = pl.BlockSpec(
        (block_rows, width), lambda g, i, s: (jnp.where(g == 0, i, last_of), 0)
    )
    leaving = pl.BlockSpec(
        (block_rows, width), lambda g, i, s: (jnp.where(g == groups - 1, i, 0), 0)
    )
    in_place = pl.BlockSpec(memory_space=pl.ANY)
    in_specs = [by_rows(width), *[whole(p.shape) for p in packs]]
    args = [tokens, *packs]
    aliases = {}
    if not first_call:
        slope, hidden, second, head, total = carried
        at = 1 + len(args)
        args += [total, slope, hidden, second, head]
        in_specs += [entering, in_place, in_place, in_place]
        in_specs += [whole((out_width, width)) if last_call else in_place]
        aliases = {at + 1: 0, at + 2: 1, at + 3: 2}
        if not last_call:
            aliases = {**aliases, at + 4: 3}
    column = pl.BlockSpec((block_rows, 2 * half), lambda g, i, s: (i, s[3 + g]))
    out_specs = [
        column,
        column,
        pl.BlockSpec((2 * half, width), lambda g, i, s: (s[3 + g], 0)),
        whole((out_width, width))
        if last_call
        else pl.BlockSpec((head_rows, width), lambda g, i, s: (s[3 + g], 0)),
    ]
    out_shape = [
        jax.ShapeDtypeStruct((rows, hid), BF16),
        jax.ShapeDtypeStruct((rows, hid), BF16),
        jax.ShapeDtypeStruct((hid, width), BF16),
        jax.ShapeDtypeStruct((out_width, width), BF16),
    ]
    if last_call:
        out_specs += [by_rows(width), by_rows(out_width)]
        out_shape += [
            jax.ShapeDtypeStruct((rows, width), BF16),
            jax.ShapeDtypeStruct((rows, out_width), BF16),
        ]
    else:
        out_specs += [leaving]
        out_shape += [jax.ShapeDtypeStruct((rows, width), F32)]
    return pl.pallas_call(
        functools.partial(
            forward_kernel, groups, first_call, last_call, (width, half, head_rows)
        ),
        grid_spec=pltpu.PrefetchScalarGridSpec(
            num_scalar_prefetch=1,
            grid=(groups, rows // block_rows),
            in_specs=in_specs,
            out_specs=out_specs,
            scratch_shapes=[pltpu.VMEM((rows, width), F32)] if groups > 1 else [],
        ),
        out_shape=out_shape,
        input_output_aliases=aliases,
        compiler_params=pltpu.CompilerParams(
            dimension_semantics=("arbitrary",) * 2, vmem_limit_bytes=56 * MIB
        ),
        cost_estimate=pl.CostEstimate(
            flops=8 * groups * rows * width * half,
            bytes_accessed=12 * MIB,
            transcendentals=groups * rows * 2 * half,
        ),
        name="forward_part",
    )(place, *args)


def once(shape):
    return pl.BlockSpec(shape, lambda i, s: (0, 0), pipeline_mode=pl.Buffered(1))


def store_halves(core, parts, keep, send):
    n, _, rows, cols = parts.shape
    zero = parts[:, 0].reshape(n * rows, cols).astype(BF16)
    one = parts[:, 1].reshape(n * rows, cols).astype(BF16)

    @pl.when(core == 0)
    def _():
        keep[0] = zero
        send[0] = one

    @pl.when(core == 1)
    def _():
        keep[0] = one
        send[0] = zero


def riders(place, scalars, shape):
    line = lax.broadcasted_iota(jnp.int32, shape, 0)
    lane = lax.broadcasted_iota(jnp.int32, shape, 1)
    score = jnp.full(shape, scalars[0], F32)
    out = jnp.where(line == 3, scalars[1], 0.0)
    for i in range(3):
        term = score.astype(BF16).astype(F32)
        out = jnp.where(line == i, term, out)
        score = score - term
    return jnp.where(lane == 2 * place[0] + place[1], out, 0.0)


def early_kernel(place, hidden, resid_grad, residual, grad_rows, scalars, keep, send):
    second = dot(hidden[...], resid_grad[...], ((0,), (0,)))
    head = dot(residual[...], grad_rows[...], ((0,), (0,)))
    width, out_width = second.shape[1], head.shape[1]
    second = second.reshape(RING, 2, RING, -1, width)
    head = head.reshape(RING, 2, RING, -1, out_width)
    blank = riders(place, scalars, (head.shape[3], width - out_width))
    blank = jnp.broadcast_to(blank, (*head.shape[:3], *blank.shape))
    both = jnp.concatenate([second, jnp.concatenate([head, blank], 4)], 3)
    both = jnp.stack([both[:, :, i] for i in (0, 3, 1, 2)], 2)
    store_halves(place[1], both.reshape(RING, 2, -1, width), keep, send)


def early_grads(place, hidden, resid_grad, residual, grad_rows, scalars):
    rows, hid = hidden.shape
    width, out_width = residual.shape[1], grad_rows.shape[1]
    lines = (hid + width) // RING // 2
    out = pl.BlockSpec((1, lines, width), lambda i, s: (i, 0, 0))
    return pl.pallas_call(
        early_kernel,
        grid_spec=pltpu.PrefetchScalarGridSpec(
            num_scalar_prefetch=1,
            grid=(RING,),
            in_specs=[
                pl.BlockSpec((rows, hid // RING), lambda i, s: (0, i)),
                once((rows, width)),
                pl.BlockSpec((rows, width // RING), lambda i, s: (0, i)),
                once((rows, out_width)),
                pl.BlockSpec(memory_space=pltpu.SMEM),
            ],
            out_specs=[out, out],
        ),
        out_shape=[jax.ShapeDtypeStruct((RING, lines, width), BF16)] * 2,
        compiler_params=params(56),
        cost_estimate=pl.CostEstimate(
            flops=2 * rows * width * (hid + out_width), bytes_accessed=18 * MIB, transcendentals=0
        ),
        name="early_grads",
    )(place, hidden, resid_grad, residual, grad_rows, scalars)


def late_kernel(gray, place, resid_grad, second, slope, tokens, keep, send):
    hidden_grad = dot(resid_grad[...], second[...], ((1,), (1,)))
    preact_grad = (slope[...].astype(F32) * hidden_grad).astype(BF16)
    first = dot(tokens[...], preact_grad, ((0,), (0,)))
    cols = first.shape[1]
    parts = first.reshape(16, 2, RING, -1, cols)
    if gray:
        parts = jnp.stack([parts[:, :, i] for i in (0, 3, 1, 2)], 2)
    store_halves(place[1], parts.reshape(16, 2, -1, cols), keep, send)


def late_grads(place, part, resid_grad, second, slope, tokens):
    rows, width = resid_grad.shape
    tile = 2 * LANES
    steps = width // tile
    out = pl.BlockSpec((1, width // 2, tile), lambda j, s: (0, 0, j))
    return pl.pallas_call(
        functools.partial(late_kernel, part == 1),
        grid_spec=pltpu.PrefetchScalarGridSpec(
            num_scalar_prefetch=1,
            grid=(steps,),
            in_specs=[
                once((rows, width)),
                pl.BlockSpec((tile, width), lambda j, s: (part * steps + j, 0)),
                pl.BlockSpec((rows, tile), lambda j, s: (0, part * steps + j)),
                once((rows, width)),
            ],
            out_specs=[out, out],
        ),
        out_shape=[jax.ShapeDtypeStruct((1, width // 2, width), BF16)] * 2,
        compiler_params=params(56),
        cost_estimate=pl.CostEstimate(
            flops=4 * rows * width * width, bytes_accessed=12 * MIB, transcendentals=0
        ),
        name="late_grads",
    )(place, resid_grad, second, slope, tokens)


def finish_kernel(arrived, half, first, second, head, loss):
    total = jnp.sum(arrived[...].astype(F32), 0)
    n, width = half.shape
    out_width = head.shape[1]
    lines = second.shape[0]
    ride = total[lines : lines + n, out_width:]
    line = lax.broadcasted_iota(jnp.int32, ride.shape, 0)
    score = jnp.sum(jnp.where(line < 3, ride, 0.0), axis=(0, 1), keepdims=True)
    count = jnp.sum(jnp.where(line == 3, ride, 0.0), axis=(0, 1), keepdims=True)
    valid = jnp.maximum(count, 1.0)
    scale = 1.0 / valid
    first[:, :width] = half[...] * scale
    first[:, width:] = total[lines + n :] * scale
    second[...] = total[:lines] * scale
    head[...] = total[lines : lines + n, :out_width] * scale
    loss[...] = score / valid


def finish(arrived, half, out_width):
    n, width = half.shape
    shapes = [(n, 2 * width), (arrived.shape[1] - 2 * n, width), (n, out_width), (1, 1)]
    first, second, head, loss = pl.pallas_call(
        finish_kernel,
        out_shape=[jax.ShapeDtypeStruct(v, F32) for v in shapes],
        compiler_params=pltpu.CompilerParams(vmem_limit_bytes=8 * MIB),
        name="finish",
    )(arrived, half)
    return first, second, head, loss[0, 0]


def add(a, b):
    return (a.astype(F32) + b.astype(F32)).astype(BF16)


def take(x, index, axis):
    return lax.dynamic_index_in_dim(x, index, axis, keepdims=False)


def ring_bits(axis):
    here = lax.axis_index(axis)
    high = here // 2
    return (high + here) % 2, high


def ring_chain(axis, low_first):
    low, high = ring_bits(axis)
    if low_first:
        steps = ((PAIR_LOW, low, 0), (PAIR_HIGH, high, 0))
    else:
        steps = ((PAIR_HIGH, high, 1), (PAIR_LOW, low, 0))
    return [(pairs, axis, bit, dim) for pairs, bit, dim in steps]


def outgoing(x, step):
    return take(x, 1 - step[2], step[3])


def sent_along(x, step):
    return lax.ppermute(x, step[1], step[0])


def kept_plus(x, arrived, step):
    return add(take(x, step[2], step[3]), arrived)


def by_ring(x, lines):
    return x.reshape(-1, 2, 2, lines, x.shape[-1]).transpose(1, 2, 0, 3, 4)


def summed_over_y(x):
    here = lax.axis_index("y")
    total = take(x, here, 1)
    for by in range(1, RING):
        total = total + shift(take(x, (here + by) % RING, 1), "y", by)
    return total


def tie(*arrays):
    return lax.optimization_barrier(arrays)


def after(x, *others):
    return lax.optimization_barrier((x, *others))[0]


def pack_kernel(side, first, second, head, a, b):
    width = first.shape[0]
    half = second.shape[0]
    a[:width, :] = first[...]
    for q in range(width // LANES):
        b[q * half : (q + 1) * half, :] = second[:, q * LANES : (q + 1) * LANES]
    a[width:, :] = head[:, :LANES]
    b[width:, :] = head[:, LANES:]


def packed(side, first, second, head):
    width, shard = first.shape
    half = shard // 2
    lines = width + head.shape[0]
    out = pl.BlockSpec((lines, LANES), lambda i, s: (0, 0))
    return pl.pallas_call(
        pack_kernel,
        grid_spec=pltpu.PrefetchScalarGridSpec(
            num_scalar_prefetch=1,
            grid=(1,),
            in_specs=[
                pl.BlockSpec((width, half), lambda i, s: (0, s[0])),
                pl.BlockSpec((half, width), lambda i, s: (s[0], 0)),
                pl.BlockSpec((head.shape[0], width // 2), lambda i, s: (0, s[0])),
            ],
            out_specs=[out, out],
        ),
        out_shape=[jax.ShapeDtypeStruct((lines, LANES), BF16)] * 2,
        compiler_params=params(56),
        name="packed",
    )(side, first, second, head)


def score(samples, target, valid_mask):
    count = samples.shape[0]
    wide = samples.astype(F32)
    gram = jnp.einsum("mpo,npo->pmn", samples, samples, preferred_element_type=F32)
    squares = jnp.sum(wide * wide, axis=2).T
    dist_sq = squares[:, :, None] + squares[:, None, :] - 2.0 * gram
    spread = jnp.sqrt(dist_sq + SMOOTHING)
    kernel = 1.0 / spread
    kernel_sum = jnp.sum(kernel, axis=2)
    pulled = jnp.einsum("pmn,npo->mpo", kernel, wide, precision=lax.Precision.HIGHEST)
    offset = wide - target[None]
    error_norm = jnp.sqrt(jnp.sum(offset * offset, axis=2) + SMOOTHING)
    repulse = wide * kernel_sum.T[:, :, None] - pulled
    validity = valid_mask.astype(F32)
    grad_raw = (
        LOSS_SCALE
        * validity[None, :, None]
        * (offset / (count * error_norm[:, :, None]) - repulse / (count * count))
    ).astype(BF16)
    scores = validity * (
        jnp.mean(error_norm, axis=0) - jnp.sum(spread, axis=(1, 2)) / (2.0 * count * count)
    )
    return grad_raw, jnp.sum(scores), jnp.sum(validity)


def per_device(latents, w_first, w_second, readout_matrix, observed, obs_index, valid_mask):
    members, patches, width = latents.shape
    out_width = observed.shape[1]
    core = lax.axis_index("c")
    here = lax.axis_index("y")
    own = obs_index.shape[0]
    rows = members * patches
    shard = w_first.shape[1]
    half = shard // 2

    side = jnp.reshape(core, (1,)).astype(jnp.int32)
    turned = readout_matrix.T
    own_a, own_b = packed(side, w_first, w_second, turned)
    right_a = shift(own_a, "y", 1)
    left_b = shift(own_b, "y", -1)
    latents, other_side, own_a, own_b = tie(latents, 1 - side, own_a, own_b)
    tokens = (
        latents.reshape(members, 32, own, width).transpose(1, 0, 2, 3).reshape(rows, width)
    )
    place = lambda *offs: jnp.stack(
        [here, core, lax.axis_index("x"), *[(here + off) % RING for off in offs]]
    ).astype(jnp.int32)
    run = functools.partial(forward_part, out_width=out_width)
    swap = lambda x: shift(x, "c", 1)
    packs = (own_a, own_b, *packed(other_side, w_first, w_second, turned))
    carried = run(place(0), tokens, packs, carried=None, last_call=False)
    right_a, left_b, *_ = tie(right_a, left_b, carried[-1])
    left_a = shift(after(own_a, right_a, left_b), "y", -1)
    right_b = shift(after(own_b, right_a, left_b), "y", 1)
    right_a_other, left_b_other = swap(right_a), swap(left_b)
    left_a, right_b, right_a_other, left_b_other = tie(
        left_a, right_b, right_a_other, left_b_other
    )
    far_a = shift(after(right_a, left_a, right_b), "y", 1)
    far_b = shift(after(left_b, left_a, right_b), "y", -1)
    packs = (right_a, right_b, right_a_other, swap(right_b))
    packs = (*packs, left_a, left_b, swap(left_a), left_b_other)
    carried = run(place(3, 1), tokens, packs, carried=carried, last_call=False)
    far_a, far_b, *carried = tie(far_a, far_b, *carried)
    slope, hidden, second, head, residual, forecast = run(
        place(2), tokens, (far_a, far_b, swap(far_a), swap(far_b)), carried=carried, last_call=True
    )

    group = ("x", "z", "c")
    device = ((here * 4 + lax.axis_index("x")) * 4 + lax.axis_index("z")) * 2 + core
    target = jnp.take(observed, obs_index - device * own, axis=0)
    forecast, target = tie(forecast.reshape(32, members * own, out_width), target)
    gathered = lax.all_to_all(forecast, group, 0, 0, tiled=True)
    samples = gathered.reshape(32 * members, own, out_width)
    grad_raw, score_part, count_part = score(samples, target, valid_mask)
    grad_rows = lax.all_to_all(
        grad_raw.reshape(32, members * own, out_width), group, 0, 0, tiled=True
    ).reshape(rows, out_width)

    at = place(0)
    scalars = jnp.stack([score_part, count_part])
    resid_grad = dot(grad_rows, head).astype(BF16)
    early = early_grads(at, hidden, resid_grad, residual, grad_rows, scalars)
    early_in = shift(early[1], "c", 1)
    late = late_grads(at, 0, after(resid_grad, early[1]), second, slope, tokens)
    a_in = shift(late[1], "c", 1)
    steps = [ring_chain("y", True), ring_chain("y", False)]
    group = ("x", "z")
    n = width // 128
    early = add(after(early[0], late[1]), early_in)
    lines = early.shape[1] // 16
    early = [by_ring(v, lines) for v in (early[:2], early[2:])]
    early_sent = [outgoing(x, s[0]) for x, s in zip(early, steps)]
    early_in = [sent_along(x, s[0]) for x, s in zip(early_sent, steps)]
    a = add(after(late[0], *early_sent), a_in).reshape(16, RING * n, width)
    a_all = lax.all_to_all(a, group, 0, 0, tiled=True)
    late = late_grads(at, 1, after(resid_grad, a), second, slope, tokens)
    b_in = shift(after(late[1], *early_in), "c", 1)
    early = [kept_plus(x, v, s[0]) for x, v, s in zip(early, early_in, steps)]
    early_sent = [outgoing(x, s[1]) for x, s in zip(early, steps)]
    early_in = [sent_along(x, s[1]) for x, s in zip(early_sent, steps)]
    b = add(after(late[0], *early_sent), b_in).reshape(2, -1, width)
    b = [by_ring(v, n) for v in (b[0], b[1])]
    b_sent = [outgoing(x, s[0]) for x, s in zip(b, steps)]
    b_in = [sent_along(x, s[0]) for x, s in zip(b_sent, steps)]
    a = jnp.sum(after(a_all, *b_sent).astype(F32), 0)
    first = summed_over_y(a.reshape(1, RING, n, width))
    early = [kept_plus(x, after(v, *b_sent), s[1]) for x, v, s in zip(early, early_in, steps)]
    b = [kept_plus(x, after(v, *early), s[0]) for x, v, s in zip(b, b_in, steps)]
    b_sent = [outgoing(x, s[1]) for x, s in zip(b, steps)]
    b_in = [sent_along(x, s[1]) for x, s in zip(b_sent, steps)]
    b = [kept_plus(x, v, s[1]) for x, v, s in zip(b, b_in, steps)]
    early = jnp.concatenate([jnp.concatenate(early), jnp.concatenate(b)], 1)
    early = lax.all_to_all(early, group, 0, 0, tiled=True)
    return finish(early, first[0], out_width)


def solution(mesh):
    grid = Mesh(mesh.devices.reshape(4, 4, 2, 4), ("x", "z", "c", "y"))
    rows = P(("y", "x", "z", "c"))
    shares = P(("x", "z", "c", "y"), None)
    return jax.shard_map(
        per_device,
        mesh=grid,
        in_specs=(
            P(("x", "z", "c"), "y", None),
            P(None, "y"),
            P("y", None),
            P(None, "y"),
            rows,
            rows,
            rows,
        ),
        out_specs=(shares, shares, shares, P()),
        check_vma=False,
    )
```
